32 devices in a mesh: req: 16 (over z, x, core), tp: 2 (over y).
Axes of the slice: x: 2, y: 2, z: 4, core: 2. Of those that a mesh axis runs over, the one named last changes fastest.
Arguments:
- x_in: bfloat16 [2048, 8192], P('req', 'tp'), may hold values from -6 to 6
- z_gate: bfloat16 [2048, 8192], P('req', 'tp'), may hold values from -6 to 6
- conv_edge: bfloat16 [128, 3, 8192], P('req', None, 'tp'), may hold values from -6 to 6
- conv_weight: float32 [4, 8192], P(None, 'tp'), may hold values from -3 to 3
- conv_bias: float32 [8192], P('tp'), may hold values from -3 to 3
- x_proj_weight: bfloat16 [8192, 288], P('tp'), may hold values from -0.0625 to 0.0625
- dt_gain: float32 [256], replicated, may hold values from 0.5 to 1.5
- b_gain: float32 [16], replicated, may hold values from 0.5 to 1.5
- c_gain: float32 [16], replicated, may hold values from 0.5 to 1.5
- dt_proj_weight: bfloat16 [256, 8192], P(None, 'tp'), may hold values from -0.375 to 0.375
- dt_bias: float32 [8192], P('tp'), may hold values from -6 to -2
- a_log: float32 [16, 8192], P(None, 'tp'), may hold values from 0 to 3
- skip: float32 [8192], P('tp'), may hold values from 0.5 to 1.5
- ssm_state: bfloat16 [128, 16, 8192], P('req', None, 'tp'), may hold values from -6 to 6
- accepted: int32 [128], P('req'), may hold values from 0 to 16, as said below
- prompt_len: int32 [128], P('req'), may hold values from 1 to 8192, 131072 in all
- tenant_range: int32 [4, 2], replicated, may hold values from 0 to 128, as said below
- owner: int32 [128], replicated, may hold values from 0 to 15, as said below
Outputs:
- mixed_out: bfloat16 [2048, 8192], P('req', 'tp')
- owned_state: bfloat16 [192, 16, 8192], P('req', None, 'tp')
- owned_edge: bfloat16 [192, 3, 8192], P('req', None, 'tp')
- tenant_stats: float32 [4, 2], replicated
The draws below stay inside these ranges and needn't reach their ends.
Inputs may be any that keep to these rules, and one draw needn't show every extreme that they name: `accepted`: accepted draft tokens; the largest value 16 occurs in every draw. `tenant_range`: the rows cover all requests in order, row k starting where row k - 1 ends; every tenant has at least one request. The 8 requests of one device go to 8 different owners; at most 12 requests go to one owner, and some owner receives exactly 12 in every draw.
All inputs are finite; a program needn't handle non-finite values. No bound on the sum of `prompt_len` on one device may be relied on, other than what follows from the above.
Results may differ from the reference program's by a relative error of at most 0.0085.
Values may be sent and summed in bfloat16 or wider, within the bound.
No kernel may reach another device: no remote copies, remote signals or barrier semaphores. Data moves between devices by JAX's collectives and lax.ppermute only.
A program may use at most 64 MiB of HBM per device.

```python
import math
import jax
import jax.numpy as jnp
import numpy as np
from jax import lax

INNER = 8192
STATE = 16
RANK = 256
CONV = 4
STEPS = 16
TENANTS = 4
REQ_DEV = 8
OWN_MOST = 12
REQUESTS = 128
TOKENS = 2048
OWNED = 192


def draw_accepted(key, part):
    first_key, second_key = jax.random.split(key)
    request_ids = jnp.arange(REQUESTS, dtype=jnp.int32)
    ceiling = 5 + 11 * request_ids // max(REQUESTS - 1, 1)
    random_bits = jax.random.randint(first_key, (REQUESTS,), 0, 1 << 20)
    counts = random_bits % (ceiling + 1)
    full_spot = jax.random.randint(second_key, (), REQUESTS - REQ_DEV, REQUESTS)
    counts = jnp.where(request_ids == full_spot, STEPS, counts)
    counts = jnp.where(request_ids == 0, 0, counts)
    return counts.astype(jnp.int32)


def draw_tenant_range(key, part):
    shuffled = jax.random.permutation(key, REQUESTS - 1) + 1
    cut_points = jnp.sort(shuffled[:TENANTS - 1]).astype(jnp.int32)
    range_starts = jnp.concatenate([jnp.zeros((1,), jnp.int32), cut_points])
    range_ends = jnp.concatenate([cut_points, jnp.full((1,), REQUESTS, jnp.int32)])
    return jnp.stack([range_starts, range_ends], axis=1)


def shuffle_one(sub_key):
    return jax.random.permutation(sub_key, REQ_DEV)


def draw_owner(key, part):
    owners = REQUESTS // REQ_DEV
    first_key, second_key, third_key = jax.random.split(key, 3)
    shuffle = jax.random.permutation(first_key, owners)
    orders = jax.vmap(shuffle_one)(jax.random.split(second_key, owners))
    busiest = jax.random.randint(third_key, (), 0, owners)
    source = jnp.arange(owners, dtype=jnp.int32)[:, None]
    drawn_pos = (source + orders) % owners
    offset = (busiest - source) % owners
    redirect = (offset >= REQ_DEV) & (offset < OWN_MOST) & (orders == 0)
    position = jnp.where(redirect, busiest, drawn_pos)
    return shuffle[position].reshape(-1).astype(jnp.int32)


def level_of(stream_key, shape, cuts, least, largest):
    factor_of, own = 1.0, jax.random.fold_in(stream_key, 6)
    for dim, parts in cuts:
        draws = jnp.exp(jax.random.uniform(jax.random.fold_in(own, dim), (parts,), jnp.float32, least / len(cuts), largest / len(cuts)))
        factor_of = factor_of * jnp.repeat(draws, shape[dim] // parts).reshape([-1 if axis == dim else 1 for axis in range(len(shape))])
    return factor_of


def length_profile(count, total, bound, slope):
    loads = [(1 << 20) // math.isqrt(standing ** slope) + 1 for standing in range(2, count + 1)]
    spare, holding = total - bound - (count - 1), [1] * (count - 1)
    while spare > 0:
        free = [i for i in range(count - 1) if holding[i] < bound]
        mass, remaining = sum([loads[i] for i in free]), spare
        for i in free:
            more = min(bound - holding[i], max(1, remaining * loads[i] // mass), spare)
            holding[i] = holding[i] + more
            spare = spare - more
    return np.array([bound] + holding)


def uneven(key, number_of, total, bound, skew):
    if number_of == 2:
        one = jax.random.randint(key, (), max(1, total - bound), min(bound, total - 1) + 1)
        return jnp.stack([one, total - one])
    lengths = jnp.asarray(length_profile(number_of, total, bound, skew), jnp.int32)
    twos = (number_of - 1) // 2
    donor, sink = lengths[1:1 + 2 * twos:2], lengths[2:2 + 2 * twos:2]
    room = jnp.minimum(donor - 1, bound - sink)
    passed = jax.random.randint(jax.random.fold_in(key, 1), (twos,), 0, 1 << 20) % (room + 1)
    lengths = lengths.at[1:1 + 2 * twos:2].set(donor - passed).at[2:2 + 2 * twos:2].set(sink + passed)
    return lengths[jax.random.permutation(jax.random.fold_in(key, 2), number_of)]


def scatter_about(key, extent, scale, most, cuts=(), kind=jnp.bfloat16):
    entries = jax.random.normal(key, extent, jnp.float32) * scale
    if len(cuts) > 0:
        entries = level_of(key, extent, cuts, -0.22, 0.18) * entries
    return jnp.clip(entries, min=-most, max=most).astype(kind)


def setup_inputs(seed: int = 0) -> dict:
    key_of = jax.random.split(jax.random.key(seed), 19)
    return {
        "x_in": scatter_about(key_of[0], (TOKENS, INNER), 1.0, 6.0, ((0, 16), (1, 2))),
        "z_gate": scatter_about(key_of[1], (TOKENS, INNER), 1.0, 6.0, ((0, 16), (1, 2))),
        "conv_edge": scatter_about(key_of[2], (REQUESTS, CONV - 1, INNER), 1.0, 6.0, ((0, 16), (2, 2))),
        "conv_weight": scatter_about(key_of[3], (CONV, INNER), CONV ** -0.5, 3.0, ((1, 2),), jnp.float32),
        "conv_bias": scatter_about(key_of[4], (INNER,), 0.3, 3.0, ((0, 2),), jnp.float32),
        "x_proj_weight": scatter_about(key_of[5], (INNER, RANK + 2 * STATE), INNER ** -0.5, 0.0625, ((0, 2),)),
        "dt_gain": jnp.clip(1.0 + 0.1 * jax.random.normal(key_of[6], (RANK,), jnp.float32), 0.5, 1.5),
        "b_gain": jnp.clip(1.0 + 0.1 * jax.random.normal(key_of[7], (STATE,), jnp.float32), 0.5, 1.5),
        "c_gain": jnp.clip(1.0 + 0.1 * jax.random.normal(key_of[8], (STATE,), jnp.float32), 0.5, 1.5),
        "dt_proj_weight": scatter_about(key_of[9], (RANK, INNER), RANK ** -0.5, 0.375, ((1, 2),)),
        "dt_bias": jnp.clip(-6.0 + 4.0 * jax.random.uniform(key_of[10], (INNER,), jnp.float32) ** level_of(key_of[10], (INNER,), ((0, 2),), -0.2, 0.2), -6.0, -2.0),
        "a_log": jnp.clip(3.0 * jax.random.uniform(key_of[11], (STATE, INNER), jnp.float32) ** level_of(key_of[11], (STATE, INNER), ((1, 2),), -0.2, 0.2), 0.0, 3.0),
        "skip": jnp.clip(1.0 + 0.1 * jax.random.normal(key_of[12], (INNER,), jnp.float32), 0.5, 1.5),
        "ssm_state": scatter_about(key_of[13], (REQUESTS, STATE, INNER), 1.0, 6.0, ((0, 16), (2, 2))),
        "accepted": draw_accepted(jax.random.fold_in(key_of[18], 71), 0),
        "prompt_len": uneven(key_of[15], REQUESTS, REQUESTS * 1024, 8192, 2).astype(jnp.int32),
        "tenant_range": draw_tenant_range(jax.random.fold_in(key_of[18], 71), 0),
        "owner": draw_owner(jax.random.fold_in(key_of[18], 71), 0),
    }


EPSILON = 1e-06
SQUARE_FLOOR = 0.25

def rms_scaled(values, scale_gain, floor_value, eps_value):
    square = lax.optimization_barrier(jnp.mean(values * values, axis=-1, keepdims=True))
    return values * lax.rsqrt(jnp.maximum(square, floor_value) + eps_value) * scale_gain

def reference(x_in, z_gate, conv_edge, conv_weight, conv_bias, x_proj_weight, dt_gain, b_gain, c_gain, dt_proj_weight, dt_bias, a_log, skip, ssm_state, accepted, prompt_len, tenant_range, owner):
    blocks = REQUESTS // REQ_DEV
    decay_rate = -jnp.exp(a_log)

    def one_block(inputs):
        x_block, z_block, edge_block, state_block, accept_block = inputs
        window = jnp.concatenate([edge_block, x_block], axis=1)
        summed = jnp.zeros((REQ_DEV, STEPS, INNER), jnp.float32) + conv_bias
        for offset in range(CONV):
            summed = summed + conv_weight[offset] * window[:, offset:offset + STEPS, :].astype(jnp.float32)
        conv_out = jax.nn.silu(summed).astype(jnp.bfloat16)
        flattened = conv_out.reshape(REQ_DEV * STEPS, INNER)
        projected = jnp.dot(flattened, x_proj_weight, preferred_element_type=jnp.float32)
        dt_low = rms_scaled(projected[:, :RANK], dt_gain, 0.0, EPSILON).astype(jnp.bfloat16)
        input_map = rms_scaled(projected[:, RANK:RANK + STATE], b_gain, SQUARE_FLOOR, 0.0).astype(jnp.bfloat16)
        output_map = rms_scaled(projected[:, RANK + STATE:], c_gain, SQUARE_FLOOR, 0.0).astype(jnp.bfloat16)
        step_size = jax.nn.softplus(jnp.dot(dt_low, dt_proj_weight, preferred_element_type=jnp.float32) + dt_bias)
        step_size = step_size.reshape(REQ_DEV, STEPS, INNER)
        conv_float = conv_out.astype(jnp.float32)
        in_float = input_map.astype(jnp.float32).reshape(REQ_DEV, STEPS, STATE)
        out_float = output_map.astype(jnp.float32).reshape(REQ_DEV, STEPS, STATE)
        initial = state_block.astype(jnp.float32)
        kept_first = jnp.where((accept_block == 0)[:, None, None], initial, jnp.zeros_like(initial))

        def advance(running, position):
            hidden, kept_state = running
            size_now = step_size[:, position, :]
            conv_now = conv_float[:, position, :]
            decay_now = jnp.exp(size_now[:, None, :] * decay_rate[None, :, :])
            hidden = decay_now * hidden + (size_now * conv_now)[:, None, :] * in_float[:, position, :, None]
            output_now = lax.optimization_barrier(jnp.sum(out_float[:, position, :, None] * hidden, axis=1)) + skip * conv_now
            kept_state = jnp.where((accept_block == position + 1)[:, None, None], hidden, kept_state)
            return ((hidden, kept_state), output_now)
        (last_state, kept_state), per_step = lax.scan(advance, (initial, kept_first), jnp.arange(STEPS, dtype=jnp.int32))
        scan_out = jnp.transpose(per_step, (1, 0, 2))
        mixed_block = (scan_out * jax.nn.silu(z_block.astype(jnp.float32))).astype(jnp.bfloat16)
        lag_index = accept_block[:, None] + jnp.arange(CONV - 1, dtype=jnp.int32)[None, :]
        kept_edge = jnp.take_along_axis(window, lag_index[:, :, None], axis=1)
        return (mixed_block, kept_state.astype(jnp.bfloat16), kept_edge)
    mixed_out, kept_state, kept_edge = lax.map(one_block, (x_in.reshape(blocks, REQ_DEV, STEPS, INNER), z_gate.reshape(blocks, REQ_DEV, STEPS, INNER), conv_edge.reshape(blocks, REQ_DEV, CONV - 1, INNER), ssm_state.reshape(blocks, REQ_DEV, STATE, INNER), accepted.reshape(blocks, REQ_DEV)))
    mixed_out = mixed_out.reshape(TOKENS, INNER)
    kept_state = kept_state.reshape(REQUESTS, STATE, INNER)
    kept_edge = kept_edge.reshape(REQUESTS, CONV - 1, INNER)
    request_ids = jnp.arange(REQUESTS, dtype=jnp.int32)
    same_owner = owner[None, :] == owner[:, None]
    before = request_ids[None, :] < request_ids[:, None]
    owner_rank = lax.optimization_barrier(jnp.sum(same_owner & before, axis=1)).astype(jnp.int32)
    dest_row = owner * OWN_MOST + owner_rank
    owned_state = jnp.zeros((OWNED, STATE, INNER), jnp.bfloat16).at[dest_row].set(kept_state)
    owned_edge = jnp.zeros((OWNED, CONV - 1, INNER), jnp.bfloat16).at[dest_row].set(kept_edge)
    inside = (request_ids[None, :] >= tenant_range[:, 0:1]) & (request_ids[None, :] < tenant_range[:, 1:2])
    accepted_float = accepted.astype(jnp.float32)
    new_length = (prompt_len + accepted + 1).astype(jnp.float32)
    accept_sum = lax.optimization_barrier(jnp.sum(jnp.where(inside, accepted_float[None, :], jnp.zeros_like(accepted_float)[None, :]), axis=1))
    length_sum = lax.optimization_barrier(jnp.sum(jnp.where(inside, new_length[None, :], jnp.zeros_like(new_length)[None, :]), axis=1))
    members = (tenant_range[:, 1] - tenant_range[:, 0]).astype(jnp.float32)
    accept_rate = accept_sum / (STEPS * members)
    length_load = length_sum / members / (jnp.sum(length_sum) / jnp.sum(members))
    tenant_stats = jnp.stack([accept_rate, length_load], axis=1)
    return (mixed_out, owned_state, owned_edge, tenant_stats)
```

```python
import functools

import jax
import jax.numpy as jnp
from jax import lax
from jax.experimental import pallas as pl
from jax.experimental.pallas import tpu as pltpu
from jax.sharding import PartitionSpec as P

EPSILON = 1e-06
SQUARE_FLOOR = 0.25
LOG2_E = 1.4426950408889634
LANES = 128
EDGE_ROWS = 4
DIGIT = 7
VMEM_BYTES = 48 * 1024 * 1024


def iota(shape, axis):
    return lax.broadcasted_iota(jnp.int32, shape, axis)


def one_hot(condition):
    return jnp.where(condition, 1.0, 0.0).astype(jnp.bfloat16)


def dot(lhs, rhs):
    return jnp.dot(lhs, rhs, preferred_element_type=jnp.float32)


def silu(value):
    return value / (1.0 + jnp.exp(-value))


def to_step_major(requests, steps):
    rows = requests * steps
    row, col = iota((rows, rows), 0), iota((rows, rows), 1)
    return one_hot(col == lax.rem(row, requests) * steps + lax.div(row, requests))


def to_request_major(requests, steps):
    rows = requests * steps
    row, col = iota((rows, rows), 0), iota((rows, rows), 1)
    return one_hot(row == lax.rem(col, requests) * steps + lax.div(col, requests))


def by_request(index, scalars):
    out = jnp.zeros_like(index)
    for request, scalar in enumerate(scalars):
        out = jnp.where(index == request, scalar, out)
    return out


def conv_kernel(
    place_ref, accepted_ref, length_ref, owner_ref,
    x_ref, edge_ref, weight_ref, bias_ref, proj_ref,
    conv_ref, partial_ref, slot_ref,
):
    requests, lags, block = edge_ref.shape
    taps = weight_ref.shape[0]
    steps = x_ref.shape[0] // requests
    slots = slot_ref.shape[0]
    base = place_ref[0] * requests
    accepted = [accepted_ref[r] for r in range(requests)]
    lengths = [length_ref[r] + accepted[r] + 1 for r in range(requests)]
    owners = [owner_ref[base + r] for r in range(requests)]

    stream = dot(to_step_major(requests, steps), x_ref[...])
    edge = edge_ref[...].astype(jnp.float32)
    window = [edge[:, k, :] for k in range(lags)]
    window += [stream[t * requests : (t + 1) * requests] for t in range(steps)]
    weight = [weight_ref[k : k + 1, :] for k in range(taps)]
    outs = []
    for t in range(steps):
        summed = bias_ref[...] + weight[0] * window[t]
        for k in range(1, taps):
            summed = summed + weight[k] * window[t + k]
        outs.append(silu(summed))
    conv_out = jnp.concatenate(outs, axis=0).astype(jnp.bfloat16)
    conv_ref[...] = conv_out
    partial = dot(conv_out, proj_ref[...])

    @pl.when(pl.program_id(0) == 0)
    def _():
        partial_ref[...] = partial

    @pl.when(pl.program_id(0) > 0)
    def _():
        partial_ref[...] += partial

    rows = jnp.concatenate(window, axis=0).astype(jnp.bfloat16)
    count = rows.shape[0]
    row, col = iota((slots * EDGE_ROWS, count), 0), iota((slots * EDGE_ROWS, count), 1)
    request = lax.rem(col, requests)
    lag = lax.rem(row, EDGE_ROWS)
    pick = (
        (lax.div(row, EDGE_ROWS) == by_request(request, owners))
        & (lax.div(col, requests) == by_request(request, accepted) + lag)
        & (lag < lags)
    )
    picked = dot(one_hot(pick), rows)
    lane = iota((slots * EDGE_ROWS, block), 1)
    low = [length & ((1 << DIGIT) - 1) for length in lengths]
    high = [length >> DIGIT for length in lengths]
    numbers = by_request(lane, accepted + low + high).astype(jnp.float32)
    last = lax.rem(iota((slots * EDGE_ROWS, block), 0), EDGE_ROWS) == lags
    picked = jnp.where(last, numbers, picked)
    for s in range(slots):
        slot_ref[s] = picked[s * EDGE_ROWS : (s + 1) * EDGE_ROWS].astype(jnp.bfloat16)


def conv_project(place, accepted, prompt_len, owner, x_in, conv_edge, conv_weight, conv_bias, proj, slots):
    rows, channels = x_in.shape
    requests, lags, _ = conv_edge.shape
    taps, width = conv_weight.shape[0], proj.shape[1]
    block = min(1024, channels)
    smem = pl.BlockSpec(memory_space=pltpu.SMEM)
    return pl.pallas_call(
        conv_kernel,
        grid=(channels // block,),
        in_specs=[
            smem, smem, smem, smem,
            pl.BlockSpec((rows, block), lambda j: (0, j)),
            pl.BlockSpec((requests, lags, block), lambda j: (0, 0, j)),
            pl.BlockSpec((taps, block), lambda j: (0, j)),
            pl.BlockSpec((1, block), lambda j: (0, j)),
            pl.BlockSpec((block, width), lambda j: (j, 0)),
        ],
        out_specs=[
            pl.BlockSpec((rows, block), lambda j: (0, j)),
            pl.BlockSpec((rows, width), lambda j: (0, 0)),
            pl.BlockSpec((slots, EDGE_ROWS, block), lambda j: (0, 0, j)),
        ],
        out_shape=[
            jax.ShapeDtypeStruct((rows, channels), jnp.bfloat16),
            jax.ShapeDtypeStruct((rows, width), jnp.float32),
            jax.ShapeDtypeStruct((slots, EDGE_ROWS, channels), jnp.bfloat16),
        ],
        compiler_params=pltpu.CompilerParams(
            dimension_semantics=("arbitrary",), vmem_limit_bytes=VMEM_BYTES
        ),
        name="conv_project",
    )(place, accepted, prompt_len, owner, x_in, conv_edge, conv_weight, conv_bias, proj)


def rms_scaled(values, gain, floor_value, eps_value):
    square = jnp.mean(values * values, axis=-1, keepdims=True)
    return (values * lax.rsqrt(jnp.maximum(square, floor_value) + eps_value) * gain).astype(jnp.bfloat16)


def scan_kernel(parts, *refs):
    place_ref, accepted_ref, owner_ref = refs[:3]
    part_refs = refs[3 : 3 + parts]
    (
        dt_gain_ref, b_gain_ref, c_gain_ref, dt_weight_ref, dt_bias_ref, a_log_ref, skip_ref,
        conv_ref, state_ref, z_ref, *_, mixed_ref, slot_ref,
        low_ref, in_ref, out_ref, size_ref, drive_ref, rate_ref, kept_ref, sum_ref,
    ) = refs[3 + parts :]
    rank, states = dt_gain_ref.shape[1], b_gain_ref.shape[1]
    requests = accepted_ref.shape[0]
    rows, block = conv_ref.shape
    steps = rows // requests
    slots = slot_ref.shape[0] // states

    @pl.when(pl.program_id(0) == 0)
    def _():
        total = part_refs[0][...]
        for part in part_refs[1:]:
            total = total + part[...]
        low_ref[...] = rms_scaled(total[:, :rank], dt_gain_ref[...], 0.0, EPSILON)
        in_map = rms_scaled(total[:, rank : rank + states], b_gain_ref[...], SQUARE_FLOOR, 0.0)
        out_map = rms_scaled(total[:, rank + states :], c_gain_ref[...], SQUARE_FLOOR, 0.0)
        wide = states * LANES
        spread = one_hot(lax.div(iota((states, wide), 1), LANES) == iota((states, wide), 0))
        in_ref[...] = dot(in_map, spread)
        out_ref[...] = dot(out_map, spread)

    conv = conv_ref[...].astype(jnp.float32)
    raw = dot(low_ref[...], dt_weight_ref[...]) + dt_bias_ref[...]
    size = jnp.maximum(raw, 0.0) + jnp.log1p(jnp.exp(-jnp.abs(raw)))
    size_ref[...] = size
    drive_ref[...] = size * conv
    kept_ref[...] = dot(to_step_major(requests, states), state_ref[...])
    rate = jnp.exp(a_log_ref[...]) * (-LOG2_E)
    for n in range(states):
        rate_ref[n * requests : (n + 1) * requests, :] = jnp.broadcast_to(
            rate[n : n + 1, :], (requests, block)
        )

    accepted = by_request(
        iota((requests, LANES), 0), [accepted_ref[r] for r in range(requests)]
    )
    pair = 2 if block % (2 * LANES) == 0 else 1

    def columns(c, carry):
        spans = [pl.ds(pl.multiple_of((c * pair + i) * LANES, LANES), LANES) for i in range(pair)]
        start = tuple(
            tuple(kept_ref[n * requests : (n + 1) * requests, s] for s in spans)
            for n in range(states)
        )

        def step(t, hidden):
            at = pl.ds(pl.multiple_of(t * requests, requests), requests)
            sizes = [size_ref[at, s] for s in spans]
            drives = [drive_ref[at, s] for s in spans]
            stop = accepted == t + 1
            sums = [None] * pair
            new = []
            for n in range(states):
                b = in_ref[at, n * LANES : (n + 1) * LANES]
                c_map = out_ref[at, n * LANES : (n + 1) * LANES]
                own = slice(n * requests, (n + 1) * requests)
                mine = []
                for i, s in enumerate(spans):
                    decay = jnp.exp2(sizes[i] * rate_ref[own, s])
                    h = decay * hidden[n][i] + drives[i] * b
                    pltpu.store(kept_ref.at[own, s], h, mask=stop)
                    term = c_map * h
                    sums[i] = term if sums[i] is None else sums[i] + term
                    mine.append(h)
                new.append(tuple(mine))
            for i, s in enumerate(spans):
                sum_ref[at, s] = sums[i]
            return tuple(new)

        lax.fori_loop(0, steps, step, start, unroll=2)
        return carry

    lax.fori_loop(0, block // (pair * LANES), columns, 0)

    gate = silu(dot(to_step_major(requests, steps), z_ref[...]))
    mixed = ((sum_ref[...] + skip_ref[...] * conv) * gate).astype(jnp.bfloat16)
    mixed_ref[...] = dot(to_request_major(requests, steps), mixed).astype(jnp.bfloat16)

    base = place_ref[0] * requests
    shape = (slots * states, states * requests)
    row, col = iota(shape, 0), iota(shape, 1)
    owners = by_request(lax.rem(col, requests), [owner_ref[base + r] for r in range(requests)])
    pick = (lax.rem(row, states) == lax.div(col, requests)) & (lax.div(row, states) == owners)
    slot_ref[...] = dot(one_hot(pick), kept_ref[...].astype(jnp.bfloat16)).astype(jnp.bfloat16)


def scan_chunk(first, width, scalars, partials, gains, dt_weight, channel_rows, conv, state, z_gate, mixed, slots):
    rows, channels = conv.shape
    dt_bias, a_log, skip = channel_rows
    states = a_log.shape[0]
    rank = dt_weight.shape[0]
    block = min(512, width)
    skipped = first // block
    smem = pl.BlockSpec(memory_space=pltpu.SMEM)

    def whole(array):
        return pl.BlockSpec(array.shape, lambda j: (0, 0))

    def columns(height):
        return pl.BlockSpec((height, block), lambda j: (0, j + skipped))

    operands = [*scalars, *partials, *gains, dt_weight, dt_bias, a_log, skip, conv, state, z_gate]
    in_specs = [smem] * len(scalars) + [whole(a) for a in (*partials, *gains)]
    in_specs += [columns(a.shape[0]) for a in operands[len(in_specs) :]]
    aliases = {}
    if mixed is not None:
        aliases[len(operands)] = 0
        operands.append(mixed)
        in_specs.append(pl.BlockSpec(memory_space=pl.ANY))
    return pl.pallas_call(
        functools.partial(scan_kernel, len(partials)),
        grid=(width // block,),
        in_specs=in_specs,
        out_specs=[
            columns(rows),
            pl.BlockSpec((slots * states, block), lambda j: (0, j)),
        ],
        out_shape=[
            jax.ShapeDtypeStruct((rows, channels), jnp.bfloat16),
            jax.ShapeDtypeStruct((slots * states, width), jnp.bfloat16),
        ],
        scratch_shapes=[
            pltpu.VMEM((rows, rank), jnp.bfloat16),
            pltpu.VMEM((rows, states * LANES), jnp.float32),
            pltpu.VMEM((rows, states * LANES), jnp.float32),
            pltpu.VMEM((rows, block), jnp.float32),
            pltpu.VMEM((rows, block), jnp.float32),
            pltpu.VMEM((states * scalars[1].shape[0], block), jnp.float32),
            pltpu.VMEM((states * scalars[1].shape[0], block), jnp.float32),
            pltpu.VMEM((rows, block), jnp.float32),
        ],
        input_output_aliases=aliases,
        compiler_params=pltpu.CompilerParams(
            dimension_semantics=("arbitrary",), vmem_limit_bytes=VMEM_BYTES
        ),
        name="scan_chunk",
    )(*operands)


def edge_kernel(steps, source_ref, count_ref, range_ref, got_ref, edge_ref, stats_ref):
    slots, _, channels = got_ref.shape
    own_most, lags, _ = edge_ref.shape
    for i in range(own_most):

        @pl.when(i < count_ref[0])
        def _():
            edge_ref[i] = got_ref[source_ref[i], :lags, :]

        @pl.when(i >= count_ref[0])
        def _():
            edge_ref[i] = jnp.zeros((lags, channels), jnp.bfloat16)

    requests = count_ref.shape[0] - 1
    numbers = got_ref[:, lags, :LANES].astype(jnp.float32)
    lane, slot = iota((slots, LANES), 1), iota((slots, LANES), 0)
    request = slot * requests + lax.rem(lane, requests)
    counts = jnp.where(lane < requests, numbers, 0.0)
    digit = lax.div(lane, requests)
    lengths = jnp.where(digit == 1, numbers, 0.0) + jnp.where(
        digit == 2, numbers * float(1 << DIGIT), 0.0
    )
    tenants = range_ref.shape[0]
    tiles = (tenants, 2)
    sums, loads, members = [], [], []
    for k in range(tenants):
        start, end = range_ref[k, 0], range_ref[k, 1]
        inside = (request >= start) & (request < end)
        sums.append(jnp.sum(jnp.where(inside, counts, 0.0), keepdims=True))
        loads.append(jnp.sum(jnp.where(inside, lengths, 0.0), keepdims=True))
        members.append(jnp.full((1, 1), 1, jnp.int32) * (end - start))
    members = [m.astype(jnp.float32) for m in members]
    mean = sum(loads[1:], loads[0]) / sum(members[1:], members[0])
    out = jnp.zeros(tiles, jnp.float32)
    row, col = iota(tiles, 0), iota(tiles, 1)
    for k in range(tenants):
        rate = sums[k] / (float(steps) * members[k])
        load = loads[k] / members[k] / mean
        out = jnp.where(row == k, jnp.where(col == 0, rate, load), out)
    stats_ref[...] = out


def settle_edges(source, count, tenant_range, got, own_most, lags, steps):
    smem = pl.BlockSpec(memory_space=pltpu.SMEM)
    vmem = pl.BlockSpec(memory_space=pltpu.VMEM)
    return pl.pallas_call(
        functools.partial(edge_kernel, steps),
        in_specs=[smem, smem, smem, vmem],
        out_specs=[vmem, vmem],
        out_shape=[
            jax.ShapeDtypeStruct((own_most, lags, got.shape[2]), jnp.bfloat16),
            jax.ShapeDtypeStruct((tenant_range.shape[0], 2), jnp.float32),
        ],
        compiler_params=pltpu.CompilerParams(vmem_limit_bytes=VMEM_BYTES),
        name="settle_edges",
    )(source, count, tenant_range, got)


def settle_kernel(first, source_ref, count_ref, got_ref, *refs):
    owned_ref, blank_ref, sems = refs[-3:]
    own_most = owned_ref.shape[0]
    width = got_ref.shape[2]
    blank_ref[...] = jnp.zeros_like(blank_ref)

    def copy(i, filled):
        origin = got_ref.at[source_ref[i]] if filled else blank_ref
        return pltpu.make_async_copy(
            origin, owned_ref.at[i, :, first : first + width], sems.at[i]
        )

    for act in ("start", "wait"):
        for i in range(own_most):
            for filled in (True, False):

                @pl.when((i < count_ref[0]) == filled)
                def _():
                    getattr(copy(i, filled), act)()


def settle_states(first, source, count, got, owned, shape):
    smem = pl.BlockSpec(memory_space=pltpu.SMEM)
    anywhere = pl.BlockSpec(memory_space=pl.ANY)
    before = () if owned is None else (owned,)
    return pl.pallas_call(
        functools.partial(settle_kernel, first),
        in_specs=[smem, smem, anywhere] + [anywhere] * len(before),
        out_specs=anywhere,
        out_shape=jax.ShapeDtypeStruct(shape, got.dtype),
        scratch_shapes=[
            pltpu.VMEM(got.shape[1:], got.dtype),
            pltpu.SemaphoreType.DMA((shape[0],)),
        ],
        input_output_aliases={3: 0} if before else {},
        compiler_params=pltpu.CompilerParams(vmem_limit_bytes=VMEM_BYTES),
        name="settle_states",
    )(source, count, got, *before)


def per_device(
    x_in, z_gate, conv_edge, conv_weight, conv_bias, x_proj_weight, dt_gain, b_gain, c_gain,
    dt_proj_weight, dt_bias, a_log, skip, ssm_state, accepted, prompt_len, tenant_range, owner,
):
    requests, states, channels = ssm_state.shape
    lags = conv_edge.shape[1]
    owners = lax.axis_size("req")
    own_most = min(requests + requests // 2, owners)
    place = lax.axis_index("req").astype(jnp.int32).reshape(1)

    conv, partial, edge_slots = conv_project(
        place, accepted, prompt_len, owner, x_in, conv_edge, conv_weight,
        conv_bias.reshape(1, -1), x_proj_weight, owners,
    )
    if lax.axis_size("tp") == 2:
        partials = (partial, lax.ppermute(partial, "tp", [(0, 1), (1, 0)]))
    else:
        partials = (lax.psum(partial, "tp"),)

    def exchange(slots):
        return lax.all_to_all(slots, "req", split_axis=0, concat_axis=0, tiled=True)

    got_edges = exchange(edge_slots)

    hits = jnp.any(owner.reshape(owners, requests) == place, axis=1)
    ids = jnp.arange(owners, dtype=jnp.int32)
    ranks = jnp.sum((hits[None, :] & (ids[None, :] < ids[:, None])).astype(jnp.int32), axis=1)
    at = hits[None, :] & (ranks[None, :] == jnp.arange(own_most, dtype=jnp.int32)[:, None])
    source = jnp.sum(jnp.where(at, ids[None, :], 0), axis=1)
    count = jnp.broadcast_to(jnp.sum(hits.astype(jnp.int32)), (requests + 1,))

    gains = (dt_gain.reshape(1, -1), b_gain.reshape(1, -1), c_gain.reshape(1, -1))
    rows = (dt_bias.reshape(1, -1), a_log, skip.reshape(1, -1))
    scalars = (place, accepted, owner)
    state = ssm_state.reshape(requests * states, channels)
    mixed, owned = None, None
    cut = channels // 4
    chunks = ((0, cut), (cut, channels - cut)) if cut % 512 == 0 else ((0, channels),)
    received = []
    for first, width in chunks:
        mixed, slots = scan_chunk(
            first, width, scalars, partials, gains, dt_proj_weight, rows, conv, state, z_gate,
            mixed, owners,
        )
        received.append((first, exchange(slots.reshape(owners, states, width))))
    owned_edge, tenant_stats = settle_edges(
        source, count, tenant_range, got_edges, own_most, lags, x_in.shape[0] // requests
    )
    for first, got in received:
        owned = settle_states(first, source, count, got, owned, (own_most, states, channels))
    return (mixed, owned, owned_edge, tenant_stats)


def solution(mesh):
    placed = (
        P("req", "tp"),
        P("req", "tp"),
        P("req", None, "tp"),
        P(None, "tp"),
        P("tp"),
        P("tp", None),
        P(),
        P(),
        P(),
        P(None, "tp"),
        P("tp"),
        P(None, "tp"),
        P("tp"),
        P("req", None, "tp"),
        P("req"),
        P("req"),
        P(),
        P(),
    )
    return jax.shard_map(
        per_device,
        mesh=mesh,
        in_specs=placed,
        out_specs=(P("req", "tp"), P("req", None, "tp"), P("req", None, "tp"), P()),
        check_vma=False,
    )
```

```python
import functools

import jax
import jax.numpy as jnp
from jax import lax
from jax.experimental import pallas as pl
from jax.experimental.pallas import tpu as pltpu
from jax.sharding import PartitionSpec as P

EPSILON = 1e-06
SQUARE_FLOOR = 0.25
LOG2_E = 1.4426950408889634
LANES = 128
EDGE_ROWS = 4
DIGIT = 7
VMEM_BYTES = 48 * 1024 * 1024
VECTOR_WEIGHT = 30000


def iota(shape, axis):
    return lax.broadcasted_iota(jnp.int32, shape, axis)


def one_hot(condition):
    return jnp.where(condition, 1.0, 0.0).astype(jnp.bfloat16)


def dot(lhs, rhs):
    return jnp.dot(lhs, rhs, preferred_element_type=jnp.float32)


def in_hbm(array):
    return pltpu.with_memory_space_constraint(array, pltpu.HBM)


def silu(value):
    return value / (1.0 + jnp.exp(-value))


def to_step_major(requests, steps):
    rows = requests * steps
    row, col = iota((rows, rows), 0), iota((rows, rows), 1)
    return one_hot(col == lax.rem(row, requests) * steps + lax.div(row, requests))


def to_request_major(requests, steps):
    rows = requests * steps
    row, col = iota((rows, rows), 0), iota((rows, rows), 1)
    return one_hot(row == lax.rem(col, requests) * steps + lax.div(col, requests))


def by_request(index, scalars):
    out = jnp.zeros_like(index)
    for request, scalar in enumerate(scalars):
        out = jnp.where(index == request, scalar, out)
    return out


def conv_kernel(x_ref, edge_ref, weight_ref, bias_ref, proj_ref, conv_ref, partial_ref):
    lags, requests, _ = edge_ref.shape
    taps = weight_ref.shape[0]
    steps = x_ref.shape[0] // requests
    stream = dot(to_step_major(requests, steps), x_ref[...])
    window = [edge_ref[k].astype(jnp.float32) for k in range(lags)]
    window += [stream[t * requests : (t + 1) * requests] for t in range(steps)]
    weight = [weight_ref[k : k + 1, :] for k in range(taps)]
    outs = []
    for t in range(steps):
        summed = bias_ref[...] + weight[0] * window[t]
        for k in range(1, taps):
            summed = summed + weight[k] * window[t + k]
        outs.append(silu(summed))
    conv_out = jnp.concatenate(outs, axis=0).astype(jnp.bfloat16)
    conv_ref[...] = conv_out
    partial = lax.dot_general(
        conv_out, proj_ref[...], (((1,), (1,)), ((), ())), preferred_element_type=jnp.float32
    )

    @pl.when(pl.program_id(0) == 0)
    def _():
        partial_ref[...] = partial

    @pl.when(pl.program_id(0) > 0)
    def _():
        partial_ref[...] += partial


def conv_project(x_in, conv_edge, conv_weight, conv_bias, proj):
    rows, channels = x_in.shape
    lags, requests, _ = conv_edge.shape
    taps, width = conv_weight.shape[0], proj.shape[0]
    block = min(1024, channels)
    return pl.pallas_call(
        conv_kernel,
        grid=(channels // block,),
        in_specs=[
            pl.BlockSpec((rows, block), lambda j: (0, j)),
            pl.BlockSpec((lags, requests, block), lambda j: (0, 0, j)),
            pl.BlockSpec((taps, block), lambda j: (0, j)),
            pl.BlockSpec((1, block), lambda j: (0, j)),
            pl.BlockSpec((width, block), lambda j: (0, j)),
        ],
        out_specs=[
            pl.BlockSpec((rows, block), lambda j: (0, j)),
            pl.BlockSpec((rows, width), lambda j: (0, 0)),
        ],
        out_shape=[
            pltpu.HBM((rows, channels), jnp.bfloat16),
            pltpu.HBM((rows, width), jnp.float32),
        ],
        compiler_params=pltpu.CompilerParams(
            dimension_semantics=("arbitrary",), vmem_limit_bytes=VMEM_BYTES
        ),
        name="conv_project",
    )(in_hbm(x_in), in_hbm(conv_edge), conv_weight, conv_bias, in_hbm(proj))


def kept_edge_kernel(
    place_ref, accepted_ref, length_ref, owner_ref, x_ref, edge_ref, _, slot_ref
):
    lags, requests, block = edge_ref.shape
    steps = x_ref.shape[0] // requests
    slots = slot_ref.shape[0]
    base = place_ref[0] * requests
    accepted = [accepted_ref[r] for r in range(requests)]
    lengths = [length_ref[r] + accepted[r] + 1 for r in range(requests)]
    owners = [owner_ref[base + r] for r in range(requests)]
    height = slots * EDGE_ROWS

    def pick(count, request_of, place_of):
        row, col = iota((height, count), 0), iota((height, count), 1)
        request, lag = request_of(col), lax.rem(row, EDGE_ROWS)
        return one_hot(
            (lax.div(row, EDGE_ROWS) == by_request(request, owners))
            & (place_of(col) == by_request(request, accepted) + lag)
            & (lag < lags)
        )

    picked = dot(
        pick(requests * steps, lambda c: lax.div(c, steps), lambda c: lax.rem(c, steps) + lags),
        x_ref[...],
    )
    edge = jnp.concatenate([edge_ref[k].astype(jnp.float32) for k in range(lags)], axis=0)
    picked += dot(
        pick(lags * requests, lambda c: lax.rem(c, requests), lambda c: lax.div(c, requests)),
        edge.astype(jnp.bfloat16),
    )
    low = [length & ((1 << DIGIT) - 1) for length in lengths]
    high = [length >> DIGIT for length in lengths]
    numbers = by_request(iota((1, block), 1), accepted + low + high).astype(jnp.float32)
    last = lax.rem(iota((height, block), 0), EDGE_ROWS) == lags
    picked = jnp.where(last, jnp.broadcast_to(numbers, (height, block)), picked)
    for s in range(slots):
        slot_ref[s] = picked[s * EDGE_ROWS : (s + 1) * EDGE_ROWS].astype(jnp.bfloat16)


def kept_edges(scalars, x_in, conv_edge, after, slots):
    rows, channels = x_in.shape
    lags, requests, _ = conv_edge.shape
    block = min(1024, channels)
    smem = pl.BlockSpec(memory_space=pltpu.SMEM)
    return pl.pallas_call(
        kept_edge_kernel,
        grid=(channels // block,),
        in_specs=[smem] * len(scalars)
        + [
            pl.BlockSpec((rows, block), lambda j: (0, j)),
            pl.BlockSpec((lags, requests, block), lambda j: (0, 0, j)),
            pl.BlockSpec(memory_space=pl.ANY),
        ],
        out_specs=pl.BlockSpec((slots, EDGE_ROWS, block), lambda j: (0, 0, j)),
        out_shape=pltpu.HBM((slots, EDGE_ROWS, channels), jnp.bfloat16),
        compiler_params=pltpu.CompilerParams(
            dimension_semantics=("arbitrary",), vmem_limit_bytes=VMEM_BYTES
        ),
        name="kept_edges",
    )(*scalars, in_hbm(x_in), in_hbm(conv_edge), in_hbm(after))


def rms_scaled(values, gain, floor_value, eps_value):
    square = jnp.mean(values * values, axis=-1, keepdims=True)
    return (values * lax.rsqrt(jnp.maximum(square, floor_value) + eps_value) * gain).astype(jnp.bfloat16)


def scan_kernel(parts, *refs):
    place_ref, accepted_ref, owner_ref = refs[:3]
    part_refs = refs[3 : 3 + parts]
    (
        dt_gain_ref, b_gain_ref, c_gain_ref, dt_weight_ref, dt_bias_ref, a_log_ref, skip_ref,
        conv_ref, state_ref, z_ref, *_, mixed_ref, slot_ref,
        low_ref, in_ref, out_ref, size_ref, drive_ref, rate_ref, kept_ref, sum_ref,
    ) = refs[3 + parts :]
    rank, states = dt_gain_ref.shape[1], b_gain_ref.shape[1]
    requests = accepted_ref.shape[0]
    rows, block = conv_ref.shape
    steps = rows // requests
    slots = slot_ref.shape[0] // states

    @pl.when(pl.program_id(0) == 0)
    def _():
        total = part_refs[0][...]
        for part in part_refs[1:]:
            total = total + part[...]
        low_ref[...] = rms_scaled(total[:, :rank], dt_gain_ref[...], 0.0, EPSILON)
        in_map = rms_scaled(total[:, rank : rank + states], b_gain_ref[...], SQUARE_FLOOR, 0.0)
        out_map = rms_scaled(total[:, rank + states :], c_gain_ref[...], SQUARE_FLOOR, 0.0)
        wide = states * LANES
        spread = one_hot(lax.div(iota((states, wide), 1), LANES) == iota((states, wide), 0))
        in_ref[...] = dot(in_map, spread)
        out_ref[...] = dot(out_map, spread)

    conv = conv_ref[...].astype(jnp.float32)
    raw = dot(low_ref[...], dt_weight_ref[...]) + dt_bias_ref[...]
    size = jnp.maximum(raw, 0.0) + jnp.log1p(jnp.exp(-jnp.abs(raw)))
    size_ref[...] = size
    drive_ref[...] = size * conv
    kept_ref[...] = dot(to_step_major(requests, states), state_ref[...])
    rate = jnp.exp(a_log_ref[...]) * (-LOG2_E)
    for n in range(states):
        rate_ref[n * requests : (n + 1) * requests, :] = jnp.broadcast_to(
            rate[n : n + 1, :], (requests, block)
        )

    accepted = by_request(
        iota((requests, LANES), 0), [accepted_ref[r] for r in range(requests)]
    )
    pair = 2 if block % (2 * LANES) == 0 else 1

    def columns(c, carry):
        spans = [pl.ds(pl.multiple_of((c * pair + i) * LANES, LANES), LANES) for i in range(pair)]
        start = tuple(
            tuple(kept_ref[n * requests : (n + 1) * requests, s] for s in spans)
            for n in range(states)
        )

        def step(t, hidden):
            at = pl.ds(pl.multiple_of(t * requests, requests), requests)
            sizes = [size_ref[at, s] for s in spans]
            drives = [drive_ref[at, s] for s in spans]
            stop = accepted == t + 1
            sums = [None] * pair
            new = []
            for n in range(states):
                b = in_ref[at, n * LANES : (n + 1) * LANES]
                c_map = out_ref[at, n * LANES : (n + 1) * LANES]
                own = slice(n * requests, (n + 1) * requests)
                mine = []
                for i, s in enumerate(spans):
                    decay = jnp.exp2(sizes[i] * rate_ref[own, s])
                    h = decay * hidden[n][i] + drives[i] * b
                    pltpu.store(kept_ref.at[own, s], h, mask=stop)
                    term = c_map * h
                    sums[i] = term if sums[i] is None else sums[i] + term
                    mine.append(h)
                new.append(tuple(mine))
            for i, s in enumerate(spans):
                sum_ref[at, s] = sums[i]
            return tuple(new)

        lax.fori_loop(0, steps, step, start, unroll=2)
        return carry

    lax.fori_loop(0, block // (pair * LANES), columns, 0)

    gate = silu(dot(to_step_major(requests, steps), z_ref[...]))
    mixed = ((sum_ref[...] + skip_ref[...] * conv) * gate).astype(jnp.bfloat16)
    mixed_ref[...] = dot(to_request_major(requests, steps), mixed).astype(jnp.bfloat16)

    base = place_ref[0] * requests
    shape = (slots * states, states * requests)
    row, col = iota(shape, 0), iota(shape, 1)
    owners = by_request(lax.rem(col, requests), [owner_ref[base + r] for r in range(requests)])
    pick = (lax.rem(row, states) == lax.div(col, requests)) & (lax.div(row, states) == owners)
    slot_ref[...] = dot(one_hot(pick), kept_ref[...].astype(jnp.bfloat16)).astype(jnp.bfloat16)


def scan_chunk(first, width, scalars, partials, gains, dt_weight, channel_rows, conv, state, z_gate, mixed, slots):
    rows, channels = conv.shape
    dt_bias, a_log, skip = channel_rows
    states = a_log.shape[0]
    rank = dt_weight.shape[0]
    block = min(512, width)
    skipped = first // block
    smem = pl.BlockSpec(memory_space=pltpu.SMEM)

    def whole(array):
        return pl.BlockSpec(array.shape, lambda j: (0, 0))

    def columns(height):
        return pl.BlockSpec((height, block), lambda j: (0, j + skipped))

    operands = [*scalars, *partials, *gains, in_hbm(dt_weight), dt_bias, in_hbm(a_log), skip]
    operands += [in_hbm(conv), in_hbm(state), in_hbm(z_gate)]
    in_specs = [smem] * len(scalars) + [whole(a) for a in (*partials, *gains)]
    in_specs += [columns(a.shape[0]) for a in operands[len(in_specs) :]]
    aliases = {}
    if mixed is not None:
        aliases[len(operands)] = 0
        operands.append(mixed)
        in_specs.append(pl.BlockSpec(memory_space=pl.ANY))
    return pl.pallas_call(
        functools.partial(scan_kernel, len(partials)),
        grid=(width // block,),
        in_specs=in_specs,
        out_specs=[
            columns(rows),
            pl.BlockSpec((slots * states, block), lambda j: (0, j)),
        ],
        out_shape=[
            jax.ShapeDtypeStruct((rows, channels), jnp.bfloat16),
            pltpu.HBM((slots * states, width), jnp.bfloat16),
        ],
        scratch_shapes=[
            pltpu.VMEM((rows, rank), jnp.bfloat16),
            pltpu.VMEM((rows, states * LANES), jnp.float32),
            pltpu.VMEM((rows, states * LANES), jnp.float32),
            pltpu.VMEM((rows, block), jnp.float32),
            pltpu.VMEM((rows, block), jnp.float32),
            pltpu.VMEM((states * scalars[1].shape[0], block), jnp.float32),
            pltpu.VMEM((states * scalars[1].shape[0], block), jnp.float32),
            pltpu.VMEM((rows, block), jnp.float32),
        ],
        input_output_aliases=aliases,
        compiler_params=pltpu.CompilerParams(
            dimension_semantics=("arbitrary",), vmem_limit_bytes=VMEM_BYTES
        ),
        cost_estimate=pl.CostEstimate(
            flops=VECTOR_WEIGHT * 8 * rows * states * width,
            transcendentals=rows * states * width,
            bytes_accessed=2 * width * (3 * rows + rank + states * slots),
        ),
        name="scan_chunk",
    )(*operands)


def edge_kernel(steps, source_ref, count_ref, range_ref, got_ref, edge_ref, stats_ref):
    slots, _, channels = got_ref.shape
    own_most, lags, _ = edge_ref.shape
    for i in range(own_most):

        @pl.when(i < count_ref[0])
        def _():
            edge_ref[i] = got_ref[source_ref[i], :lags, :]

        @pl.when(i >= count_ref[0])
        def _():
            edge_ref[i] = jnp.zeros((lags, channels), jnp.bfloat16)

    requests = count_ref.shape[0] - 1
    numbers = got_ref[:, lags, :LANES].astype(jnp.float32)
    lane, slot = iota((slots, LANES), 1), iota((slots, LANES), 0)
    request = slot * requests + lax.rem(lane, requests)
    counts = jnp.where(lane < requests, numbers, 0.0)
    digit = lax.div(lane, requests)
    lengths = jnp.where(digit == 1, numbers, 0.0) + jnp.where(
        digit == 2, numbers * float(1 << DIGIT), 0.0
    )
    tenants = range_ref.shape[0]
    tiles = (tenants, 2)
    sums, loads, members = [], [], []
    for k in range(tenants):
        start, end = range_ref[k, 0], range_ref[k, 1]
        inside = (request >= start) & (request < end)
        sums.append(jnp.sum(jnp.where(inside, counts, 0.0), keepdims=True))
        loads.append(jnp.sum(jnp.where(inside, lengths, 0.0), keepdims=True))
        members.append(jnp.full((1, 1), 1, jnp.int32) * (end - start))
    members = [m.astype(jnp.float32) for m in members]
    mean = sum(loads[1:], loads[0]) / sum(members[1:], members[0])
    out = jnp.zeros(tiles, jnp.float32)
    row, col = iota(tiles, 0), iota(tiles, 1)
    for k in range(tenants):
        rate = sums[k] / (float(steps) * members[k])
        load = loads[k] / members[k] / mean
        out = jnp.where(row == k, jnp.where(col == 0, rate, load), out)
    stats_ref[...] = out


def settle_edges(source, count, tenant_range, got, own_most, lags, steps):
    smem = pl.BlockSpec(memory_space=pltpu.SMEM)
    vmem = pl.BlockSpec(memory_space=pltpu.VMEM)
    return pl.pallas_call(
        functools.partial(edge_kernel, steps),
        in_specs=[smem, smem, smem, vmem],
        out_specs=[vmem, vmem],
        out_shape=[
            jax.ShapeDtypeStruct((own_most, lags, got.shape[2]), jnp.bfloat16),
            jax.ShapeDtypeStruct((tenant_range.shape[0], 2), jnp.float32),
        ],
        compiler_params=pltpu.CompilerParams(vmem_limit_bytes=VMEM_BYTES),
        name="settle_edges",
    )(source, count, tenant_range, got)


def settle_kernel(first, source_ref, count_ref, got_ref, *refs):
    owned_ref, blank_ref, sems = refs[-3:]
    own_most = owned_ref.shape[0]
    width = got_ref.shape[2]
    blank_ref[...] = jnp.zeros_like(blank_ref)

    def copy(i, filled):
        origin = got_ref.at[source_ref[i]] if filled else blank_ref
        return pltpu.make_async_copy(
            origin, owned_ref.at[i, :, first : first + width], sems.at[i]
        )

    for act in ("start", "wait"):
        for i in range(own_most):
            for filled in (True, False):

                @pl.when((i < count_ref[0]) == filled)
                def _():
                    getattr(copy(i, filled), act)()


def settle_states(first, source, count, got, owned, shape):
    smem = pl.BlockSpec(memory_space=pltpu.SMEM)
    anywhere = pl.BlockSpec(memory_space=pl.ANY)
    before = () if owned is None else (owned,)
    return pl.pallas_call(
        functools.partial(settle_kernel, first),
        in_specs=[smem, smem, anywhere] + [anywhere] * len(before),
        out_specs=anywhere,
        out_shape=jax.ShapeDtypeStruct(shape, got.dtype),
        scratch_shapes=[
            pltpu.VMEM(got.shape[1:], got.dtype),
            pltpu.SemaphoreType.DMA((shape[0],)),
        ],
        input_output_aliases={3: 0} if before else {},
        compiler_params=pltpu.CompilerParams(vmem_limit_bytes=VMEM_BYTES),
        name="settle_states",
    )(source, count, got, *before)


def per_device(
    x_in, z_gate, conv_edge, conv_weight, conv_bias, x_proj_weight, dt_gain, b_gain, c_gain,
    dt_proj_weight, dt_bias, a_log, skip, ssm_state, accepted, prompt_len, tenant_range, owner,
):
    requests, states, channels = ssm_state.shape
    lags = conv_edge.shape[1]
    owners = lax.axis_size("req")
    own_most = min(requests + requests // 2, owners)
    place = lax.axis_index("req").astype(jnp.int32).reshape(1)

    by_lag = jnp.transpose(conv_edge, (1, 0, 2))
    conv, partial = conv_project(
        x_in, by_lag, conv_weight, conv_bias.reshape(1, -1), x_proj_weight.T
    )
    edge_slots = kept_edges((place, accepted, prompt_len, owner), x_in, by_lag, partial, owners)
    if lax.axis_size("tp") == 2:
        partials = (partial, lax.ppermute(partial, "tp", [(0, 1), (1, 0)]))
    else:
        partials = (lax.psum(partial, "tp"),)

    def exchange(slots):
        return lax.all_to_all(slots, "req", split_axis=0, concat_axis=0, tiled=True)

    got_edges = exchange(edge_slots)

    hits = jnp.any(owner.reshape(owners, requests) == place, axis=1)
    ids = jnp.arange(owners, dtype=jnp.int32)
    ranks = jnp.sum((hits[None, :] & (ids[None, :] < ids[:, None])).astype(jnp.int32), axis=1)
    at = hits[None, :] & (ranks[None, :] == jnp.arange(own_most, dtype=jnp.int32)[:, None])
    source = jnp.sum(jnp.where(at, ids[None, :], 0), axis=1)
    count = jnp.broadcast_to(jnp.sum(hits.astype(jnp.int32)), (requests + 1,))

    gains = (dt_gain.reshape(1, -1), b_gain.reshape(1, -1), c_gain.reshape(1, -1))
    rows = (dt_bias.reshape(1, -1), a_log, skip.reshape(1, -1))
    scalars = (place, accepted, owner)
    state = ssm_state.reshape(requests * states, channels)
    mixed, owned = None, None
    cut = channels // 4
    chunks = ((0, cut), (cut, channels - cut)) if cut % 512 == 0 else ((0, channels),)
    received = []
    for first, width in chunks:
        mixed, slots = scan_chunk(
            first, width, scalars, partials, gains, dt_proj_weight, rows, conv, state, z_gate,
            mixed, owners,
        )
        received.append((first, exchange(slots.reshape(owners, states, width))))
    owned_edge, tenant_stats = settle_edges(
        source, count, tenant_range, got_edges, own_most, lags, x_in.shape[0] // requests
    )
    for first, got in received:
        owned = settle_states(first, source, count, got, owned, (own_most, states, channels))
    return (mixed, owned, owned_edge, tenant_stats)


def solution(mesh):
    placed = (
        P("req", "tp"),
        P("req", "tp"),
        P("req", None, "tp"),
        P(None, "tp"),
        P("tp"),
        P("tp", None),
        P(),
        P(),
        P(),
        P(None, "tp"),
        P("tp"),
        P(None, "tp"),
        P("tp"),
        P("req", None, "tp"),
        P("req"),
        P("req"),
        P(),
        P(),
    )
    return jax.shard_map(
        per_device,
        mesh=mesh,
        in_specs=placed,
        out_specs=(P("req", "tp"), P("req", None, "tp"), P("req", None, "tp"), P()),
        check_vma=False,
    )
```

```python
import functools

import jax
import jax.numpy as jnp
from jax import lax
from jax.experimental import pallas as pl
from jax.experimental.pallas import tpu as pltpu
from jax.sharding import PartitionSpec as P

EPSILON = 1e-06
SQUARE_FLOOR = 0.25
LOG2_E = 1.4426950408889634
LANES = 128
EDGE_ROWS = 4
DIGIT = 7
VMEM_BYTES = 48 * 1024 * 1024
ROUND = 4
VECTOR_WEIGHT = 30000


def iota(shape, axis):
    return lax.broadcasted_iota(jnp.int32, shape, axis)


def one_hot(condition):
    return jnp.where(condition, 1.0, 0.0).astype(jnp.bfloat16)


def dot(lhs, rhs):
    return jnp.dot(lhs, rhs, preferred_element_type=jnp.float32)


def in_hbm(array):
    return pltpu.with_memory_space_constraint(array, pltpu.HBM)


def silu(value):
    return value * (0.5 + 0.5 * jnp.tanh(0.5 * value))


def to_step_major(requests, steps):
    rows = requests * steps
    row, col = iota((rows, rows), 0), iota((rows, rows), 1)
    return one_hot(col == lax.rem(row, requests) * steps + lax.div(row, requests))


def to_request_major(requests, steps):
    rows = requests * steps
    row, col = iota((rows, rows), 0), iota((rows, rows), 1)
    return one_hot(row == lax.rem(col, requests) * steps + lax.div(col, requests))


def by_request(index, scalars):
    out = jnp.zeros_like(index)
    for request, scalar in enumerate(scalars):
        out = jnp.where(index == request, scalar, out)
    return out


def conv_kernel(
    place_ref, accepted_ref, length_ref, owner_ref, x_ref, edge_ref, weight_ref, bias_ref, proj_ref,
    conv_ref, partial_ref, slot_ref,
):
    lags, requests, block = edge_ref.shape
    taps = weight_ref.shape[0]
    steps = x_ref.shape[0] // requests
    slots = slot_ref.shape[0]
    stream = dot(to_step_major(requests, steps), x_ref[...])
    window = [edge_ref[k].astype(jnp.float32) for k in range(lags)]
    window += [stream[t * requests : (t + 1) * requests] for t in range(steps)]
    weight = [weight_ref[k : k + 1, :] for k in range(taps)]
    outs = []
    for t in range(steps):
        summed = bias_ref[...] + weight[0] * window[t]
        for k in range(1, taps):
            summed = summed + weight[k] * window[t + k]
        outs.append(silu(summed))
    conv_out = jnp.concatenate(outs, axis=0).astype(jnp.bfloat16)
    conv_ref[...] = conv_out
    partial = lax.dot_general(
        conv_out, proj_ref[...], (((1,), (1,)), ((), ())), preferred_element_type=jnp.float32
    )

    @pl.when(pl.program_id(0) == 0)
    def _():
        partial_ref[...] = partial

    @pl.when(pl.program_id(0) > 0)
    def _():
        partial_ref[...] += partial

    base = place_ref[0] * requests
    accepted = [accepted_ref[r] for r in range(requests)]
    lengths = [length_ref[r] + accepted[r] + 1 for r in range(requests)]
    owners = [owner_ref[base + r] for r in range(requests)]
    rows = jnp.concatenate(window, axis=0).astype(jnp.bfloat16)
    height, count = slots * EDGE_ROWS, rows.shape[0]
    row, col = iota((height, count), 0), iota((1, count), 1)
    request, lag = lax.rem(col, requests), lax.rem(row, EDGE_ROWS)
    pick = (
        (lax.div(row, EDGE_ROWS) == by_request(request, owners))
        & (lax.div(col, requests) - by_request(request, accepted) == lag)
        & (lag < lags)
    )
    picked = dot(one_hot(pick), rows)
    low = [length & ((1 << DIGIT) - 1) for length in lengths]
    high = [length >> DIGIT for length in lengths]
    numbers = by_request(iota((1, block), 1), accepted + low + high).astype(jnp.float32)
    last = lax.rem(iota((height, block), 0), EDGE_ROWS) == lags
    picked = jnp.where(last, jnp.broadcast_to(numbers, (height, block)), picked)
    for s in range(slots):
        slot_ref[s] = picked[s * EDGE_ROWS : (s + 1) * EDGE_ROWS].astype(jnp.bfloat16)


def conv_project(scalars, x_in, conv_edge, conv_weight, conv_bias, proj, slots):
    rows, channels = x_in.shape
    lags, requests, _ = conv_edge.shape
    taps, width = conv_weight.shape[0], proj.shape[0]
    block = min(1024, channels)
    return pl.pallas_call(
        conv_kernel,
        grid=(channels // block,),
        in_specs=[pl.BlockSpec(memory_space=pltpu.SMEM)] * len(scalars)
        + [
            pl.BlockSpec((rows, block), lambda j: (0, j)),
            pl.BlockSpec((lags, requests, block), lambda j: (0, 0, j)),
            pl.BlockSpec((taps, block), lambda j: (0, j)),
            pl.BlockSpec((1, block), lambda j: (0, j)),
            pl.BlockSpec((width, block), lambda j: (0, j)),
        ],
        out_specs=[
            pl.BlockSpec((rows, block), lambda j: (0, j)),
            pl.BlockSpec((rows, width), lambda j: (0, 0)),
            pl.BlockSpec((slots, EDGE_ROWS, block), lambda j: (0, 0, j)),
        ],
        out_shape=[
            pltpu.HBM((rows, channels), jnp.bfloat16),
            pltpu.HBM((rows, width), jnp.float32),
            pltpu.HBM((slots, EDGE_ROWS, channels), jnp.bfloat16),
        ],
        compiler_params=pltpu.CompilerParams(
            dimension_semantics=("arbitrary",), vmem_limit_bytes=VMEM_BYTES
        ),
        name="conv_project",
    )(*scalars, *(in_hbm(a) for a in (x_in, conv_edge, conv_weight, conv_bias, proj)))


def rms_scaled(values, gain, floor_value, eps_value):
    square = jnp.mean(values * values, axis=-1, keepdims=True)
    return (values * lax.rsqrt(jnp.maximum(square, floor_value) + eps_value) * gain).astype(jnp.bfloat16)


def summed(part_refs):
    total = part_refs[0][...]
    for part in part_refs[1:]:
        total = total + part[...]
    return total


def softplus(raw):
    return jnp.maximum(raw, 0.0) + jnp.log1p(jnp.exp(-jnp.abs(raw)))


def kept_kernel(parts, *refs):
    place_ref, accepted_ref, owner_ref = refs[:3]
    (
        dt_gain_ref, b_gain_ref, dt_weight_ref, dt_bias_ref, a_log_ref, conv_ref, state_ref,
        slot_ref, low_ref, in_ref, size_ref, drive_ref, rate_ref,
    ) = refs[3 + parts :]
    rank, states = dt_gain_ref.shape[1], b_gain_ref.shape[1]
    requests = accepted_ref.shape[0]
    rows, block = conv_ref.shape
    steps = rows // requests

    @pl.when(pl.program_id(0) == 0)
    def _():
        total = summed(refs[3 : 3 + parts])
        low_ref[...] = rms_scaled(total[:, :rank], dt_gain_ref[...], 0.0, EPSILON)
        in_map = rms_scaled(total[:, rank : rank + states], b_gain_ref[...], SQUARE_FLOOR, 0.0)
        turned = jnp.transpose(in_map.astype(jnp.float32))
        for row in range(rows):
            t, r = divmod(row, requests)
            in_ref[r * states : (r + 1) * states, t * LANES : (t + 1) * LANES] = (
                jnp.broadcast_to(turned[:, row : row + 1], (states, LANES))
            )

    row = iota((rows, 1), 0)
    live = lax.div(row, requests) < by_request(
        lax.rem(row, requests), [accepted_ref[r] for r in range(requests)]
    )
    size = softplus(dot(low_ref[...], dt_weight_ref[...]) + dt_bias_ref[...])
    size = jnp.where(live, size, 0.0)
    drive = size * conv_ref[...].astype(jnp.float32)
    for c in range(block // LANES):
        size_ref[c] = size[:, c * LANES : (c + 1) * LANES]
        drive_ref[c] = drive[:, c * LANES : (c + 1) * LANES]
    rate_ref[...] = jnp.exp(a_log_ref[...]) * (-LOG2_E)

    span = min(1024, block)
    halves = states // 8
    for r in range(requests):
        slot = owner_ref[place_ref[0] * requests + r]
        rounds = lax.div(accepted_ref[r] + (ROUND - 1), ROUND)
        for first in range(0, block, span):
            tiles = [slice(c, c + LANES) for c in range(first, first + span, LANES)]

            def one_round(i, hidden):
                hidden = [list(h) for h in hidden]
                for u in range(ROUND):
                    t = i * ROUND + u
                    at = pl.ds(t * requests + r, 8, stride=0)
                    b = [
                        in_ref[
                            r * states + 8 * h : r * states + 8 * (h + 1),
                            pl.ds(pl.multiple_of(t * LANES, LANES), LANES),
                        ]
                        for h in range(halves)
                    ]
                    for c, tile in enumerate(tiles):
                        place = first // LANES + c
                        now, drive = size_ref[place, at, :], drive_ref[place, at, :]
                        for h in range(halves):
                            decay = jnp.exp2(now * rate_ref[8 * h : 8 * (h + 1), tile])
                            hidden[h][c] = decay * hidden[h][c] + drive * b[h]
                return tuple(tuple(h) for h in hidden)

            old = state_ref[r * states : (r + 1) * states, first : first + span].astype(jnp.float32)
            start = tuple(
                tuple(
                    old[8 * h : 8 * (h + 1), c * LANES : (c + 1) * LANES] for c in range(len(tiles))
                )
                for h in range(halves)
            )
            done = lax.fori_loop(0, rounds, one_round, start)
            new = jnp.concatenate([jnp.concatenate(h, axis=1) for h in done], axis=0)
            slot_ref[slot, :, first : first + span] = new.astype(jnp.bfloat16)


def kept_states(scalars, partials, gains, dt_weight, dt_bias, a_log, conv, state, slots):
    rows, channels = conv.shape
    states, rank = a_log.shape[0], dt_weight.shape[0]
    requests = scalars[1].shape[0]
    block = min(1024, channels)

    def whole(array):
        return pl.BlockSpec(array.shape, lambda j: (0, 0))

    wide = [in_hbm(dt_weight), dt_bias, in_hbm(a_log), in_hbm(conv), in_hbm(state)]
    return pl.pallas_call(
        functools.partial(kept_kernel, len(partials)),
        grid=(channels // block,),
        in_specs=[pl.BlockSpec(memory_space=pltpu.SMEM)] * len(scalars)
        + [whole(a) for a in (*partials, *gains)]
        + [pl.BlockSpec((a.shape[0], block), lambda j: (0, j)) for a in wide],
        out_specs=pl.BlockSpec((slots, states, block), lambda j: (0, 0, j)),
        out_shape=pltpu.HBM((slots, states, channels), jnp.bfloat16),
        scratch_shapes=[
            pltpu.VMEM((rows, rank), jnp.bfloat16),
            pltpu.VMEM((requests * states, rows // requests * LANES), jnp.float32),
            pltpu.VMEM((block // LANES, rows, LANES), jnp.float32),
            pltpu.VMEM((block // LANES, rows, LANES), jnp.float32),
            pltpu.VMEM((states, block), jnp.float32),
        ],
        compiler_params=pltpu.CompilerParams(
            dimension_semantics=("arbitrary",), vmem_limit_bytes=VMEM_BYTES
        ),
        cost_estimate=pl.CostEstimate(
            flops=VECTOR_WEIGHT * 4 * rows * states * channels,
            transcendentals=rows * states * channels,
            bytes_accessed=2 * channels * (rows + rank + states * (requests + slots)),
        ),
        name="kept_states",
    )(*scalars, *partials, *gains, *wide)


def scan_kernel(parts, *refs):
    (
        dt_gain_ref, b_gain_ref, c_gain_ref, dt_weight_ref, dt_bias_ref, a_log_ref, skip_ref,
        conv_ref, state_ref, z_ref, mixed_ref,
        low_ref, in_ref, out_ref, size_ref, drive_ref, rate_ref, start_ref, sum_ref,
    ) = refs[parts:]
    rank, states = dt_gain_ref.shape[1], b_gain_ref.shape[1]
    rows, block = conv_ref.shape
    requests = state_ref.shape[0] // states
    steps = rows // requests

    @pl.when(pl.program_id(0) == 0)
    def _():
        total = summed(refs[:parts])
        low_ref[...] = rms_scaled(total[:, :rank], dt_gain_ref[...], 0.0, EPSILON)
        in_map = rms_scaled(total[:, rank : rank + states], b_gain_ref[...], SQUARE_FLOOR, 0.0)
        out_map = rms_scaled(total[:, rank + states :], c_gain_ref[...], SQUARE_FLOOR, 0.0)
        wide = states * LANES
        spread = one_hot(lax.div(iota((states, wide), 1), LANES) == iota((states, wide), 0))
        in_ref[...] = dot(in_map, spread)
        out_ref[...] = dot(out_map, spread)

    conv = conv_ref[...].astype(jnp.float32)
    size = softplus(dot(low_ref[...], dt_weight_ref[...]) + dt_bias_ref[...])
    size_ref[...] = size
    drive_ref[...] = size * conv
    start_ref[...] = dot(to_step_major(requests, states), state_ref[...])
    rate = jnp.exp(a_log_ref[...]) * (-LOG2_E)
    for n in range(states):
        rate_ref[n * requests : (n + 1) * requests, :] = jnp.broadcast_to(
            rate[n : n + 1, :], (requests, block)
        )

    pair = 2 if block % (2 * LANES) == 0 else 1

    def columns(c, carry):
        spans = [pl.ds(pl.multiple_of((c * pair + i) * LANES, LANES), LANES) for i in range(pair)]
        start = tuple(
            tuple(start_ref[n * requests : (n + 1) * requests, s] for s in spans)
            for n in range(states)
        )

        def step(t, hidden):
            at = pl.ds(pl.multiple_of(t * requests, requests), requests)
            sizes = [size_ref[at, s] for s in spans]
            drives = [drive_ref[at, s] for s in spans]
            sums = [None] * pair
            new = []
            for n in range(states):
                b = in_ref[at, n * LANES : (n + 1) * LANES]
                c_map = out_ref[at, n * LANES : (n + 1) * LANES]
                own = slice(n * requests, (n + 1) * requests)
                mine = []
                for i, s in enumerate(spans):
                    h = jnp.exp2(sizes[i] * rate_ref[own, s]) * hidden[n][i] + drives[i] * b
                    term = c_map * h
                    sums[i] = term if sums[i] is None else sums[i] + term
                    mine.append(h)
                new.append(tuple(mine))
            for i, s in enumerate(spans):
                sum_ref[at, s] = sums[i]
            return tuple(new)

        lax.fori_loop(0, steps, step, start, unroll=2)
        return carry

    lax.fori_loop(0, block // (pair * LANES), columns, 0)

    gate = silu(dot(to_step_major(requests, steps), z_ref[...]))
    mixed = ((sum_ref[...] + skip_ref[...] * conv) * gate).astype(jnp.bfloat16)
    mixed_ref[...] = dot(to_request_major(requests, steps), mixed).astype(jnp.bfloat16)


def scan(partials, gains, dt_weight, dt_bias, a_log, skip, conv, state, z_gate):
    rows, channels = conv.shape
    states, rank = a_log.shape[0], dt_weight.shape[0]
    block = min(512, channels)

    def whole(array):
        return pl.BlockSpec(array.shape, lambda j: (0, 0))

    wide = [in_hbm(dt_weight), dt_bias, in_hbm(a_log), skip, in_hbm(conv), in_hbm(state), in_hbm(z_gate)]
    tall = pltpu.VMEM((rows, block), jnp.float32)
    table = pltpu.VMEM((rows, states * LANES), jnp.float32)
    return pl.pallas_call(
        functools.partial(scan_kernel, len(partials)),
        grid=(channels // block,),
        in_specs=[whole(a) for a in (*partials, *gains)]
        + [pl.BlockSpec((a.shape[0], block), lambda j: (0, j)) for a in wide],
        out_specs=pl.BlockSpec((rows, block), lambda j: (0, j)),
        out_shape=jax.ShapeDtypeStruct((rows, channels), jnp.bfloat16),
        scratch_shapes=[
            pltpu.VMEM((rows, rank), jnp.bfloat16), table, table, tall, tall,
            pltpu.VMEM((state.shape[0], block), jnp.float32),
            pltpu.VMEM((state.shape[0], block), jnp.float32),
            tall,
        ],
        compiler_params=pltpu.CompilerParams(
            dimension_semantics=("arbitrary",), vmem_limit_bytes=VMEM_BYTES
        ),
        cost_estimate=pl.CostEstimate(
            flops=VECTOR_WEIGHT * 8 * rows * states * channels,
            transcendentals=rows * states * channels,
            bytes_accessed=2 * channels * (3 * rows + rank),
        ),
        name="scan",
    )(*partials, *gains, *wide)


def edge_kernel(steps, source_ref, count_ref, range_ref, got_ref, edge_ref, stats_ref):
    slots, _, channels = got_ref.shape
    own_most, lags, _ = edge_ref.shape
    for i in range(own_most):

        @pl.when(i < count_ref[0])
        def _():
            edge_ref[i] = got_ref[source_ref[i], :lags, :]

        @pl.when(i >= count_ref[0])
        def _():
            edge_ref[i] = jnp.zeros((lags, channels), jnp.bfloat16)

    requests = count_ref.shape[0] - 1
    numbers = got_ref[:, lags, :LANES].astype(jnp.float32)
    lane, slot = iota((slots, LANES), 1), iota((slots, LANES), 0)
    request = slot * requests + lax.rem(lane, requests)
    counts = jnp.where(lane < requests, numbers, 0.0)
    digit = lax.div(lane, requests)
    lengths = jnp.where(digit == 1, numbers, 0.0) + jnp.where(
        digit == 2, numbers * float(1 << DIGIT), 0.0
    )
    tenants = range_ref.shape[0]
    tiles = (tenants, 2)
    sums, loads, members = [], [], []
    for k in range(tenants):
        start, end = range_ref[k, 0], range_ref[k, 1]
        inside = (request >= start) & (request < end)
        sums.append(jnp.sum(jnp.where(inside, counts, 0.0), keepdims=True))
        loads.append(jnp.sum(jnp.where(inside, lengths, 0.0), keepdims=True))
        members.append(jnp.full((1, 1), 1, jnp.int32) * (end - start))
    members = [m.astype(jnp.float32) for m in members]
    mean = sum(loads[1:], loads[0]) / sum(members[1:], members[0])
    out = jnp.zeros(tiles, jnp.float32)
    row, col = iota(tiles, 0), iota(tiles, 1)
    for k in range(tenants):
        rate = sums[k] / (float(steps) * members[k])
        load = loads[k] / members[k] / mean
        out = jnp.where(row == k, jnp.where(col == 0, rate, load), out)
    stats_ref[...] = out


def settle_edges(source, count, tenant_range, got, own_most, lags, steps):
    smem = pl.BlockSpec(memory_space=pltpu.SMEM)
    vmem = pl.BlockSpec(memory_space=pltpu.VMEM)
    return pl.pallas_call(
        functools.partial(edge_kernel, steps),
        in_specs=[smem, smem, smem, vmem],
        out_specs=[vmem, vmem],
        out_shape=[
            jax.ShapeDtypeStruct((own_most, lags, got.shape[2]), jnp.bfloat16),
            jax.ShapeDtypeStruct((tenant_range.shape[0], 2), jnp.float32),
        ],
        compiler_params=pltpu.CompilerParams(vmem_limit_bytes=VMEM_BYTES),
        name="settle_edges",
    )(source, count, tenant_range, got)


def settle_kernel(source_ref, count_ref, got_ref, owned_ref, blank_ref, sems):
    own_most = owned_ref.shape[0]
    blank_ref[...] = jnp.zeros_like(blank_ref)

    def copy(i, filled):
        origin = got_ref.at[source_ref[i]] if filled else blank_ref
        return pltpu.make_async_copy(origin, owned_ref.at[i], sems.at[i])

    for act in ("start", "wait"):
        for i in range(own_most):
            for filled in (True, False):

                @pl.when((i < count_ref[0]) == filled)
                def _():
                    getattr(copy(i, filled), act)()


def settle_states(source, count, got, own_most):
    smem = pl.BlockSpec(memory_space=pltpu.SMEM)
    anywhere = pl.BlockSpec(memory_space=pl.ANY)
    return pl.pallas_call(
        settle_kernel,
        in_specs=[smem, smem, anywhere],
        out_specs=anywhere,
        out_shape=jax.ShapeDtypeStruct((own_most, *got.shape[1:]), got.dtype),
        scratch_shapes=[
            pltpu.VMEM(got.shape[1:], got.dtype),
            pltpu.SemaphoreType.DMA((own_most,)),
        ],
        compiler_params=pltpu.CompilerParams(vmem_limit_bytes=VMEM_BYTES),
        name="settle_states",
    )(source, count, in_hbm(got))


def per_device(
    x_in, z_gate, conv_edge, conv_weight, conv_bias, x_proj_weight, dt_gain, b_gain, c_gain,
    dt_proj_weight, dt_bias, a_log, skip, ssm_state, accepted, prompt_len, tenant_range, owner,
):
    requests, states, channels = ssm_state.shape
    lags = conv_edge.shape[1]
    owners = lax.axis_size("req")
    own_most = min(requests + requests // 2, owners)
    place = lax.axis_index("req").astype(jnp.int32).reshape(1)

    conv, partial, edge_slots = conv_project(
        (place, accepted, prompt_len, owner), x_in, jnp.transpose(conv_edge, (1, 0, 2)),
        conv_weight, conv_bias.reshape(1, -1), x_proj_weight.T, owners,
    )
    if lax.axis_size("tp") == 2:
        partials = (partial, lax.ppermute(partial, "tp", [(0, 1), (1, 0)]))
    else:
        partials = (lax.psum(partial, "tp"),)

    def exchange(slots):
        return lax.all_to_all(slots, "req", split_axis=0, concat_axis=0, tiled=True)

    got_edges = exchange(edge_slots)

    hits = jnp.any(owner.reshape(owners, requests) == place, axis=1)
    ids = jnp.arange(owners, dtype=jnp.int32)
    ranks = jnp.sum((hits[None, :] & (ids[None, :] < ids[:, None])).astype(jnp.int32), axis=1)
    at = hits[None, :] & (ranks[None, :] == jnp.arange(own_most, dtype=jnp.int32)[:, None])
    source = jnp.sum(jnp.where(at, ids[None, :], 0), axis=1)
    count = jnp.broadcast_to(jnp.sum(hits.astype(jnp.int32)), (requests + 1,))

    gains = (dt_gain.reshape(1, -1), b_gain.reshape(1, -1), c_gain.reshape(1, -1))
    bias = dt_bias.reshape(1, -1)
    state = ssm_state.reshape(requests * states, channels)
    slots = kept_states(
        (place, accepted, owner), partials, gains[:2], dt_proj_weight, bias, a_log, conv, state, owners
    )
    got = exchange(slots)
    mixed = scan(
        partials, gains, dt_proj_weight, bias, a_log, skip.reshape(1, -1), conv, state, z_gate
    )
    owned_edge, tenant_stats = settle_edges(
        source, count, tenant_range, got_edges, own_most, lags, x_in.shape[0] // requests
    )
    owned = settle_states(source, count, got, own_most)
    return (mixed, owned, owned_edge, tenant_stats)


def solution(mesh):
    placed = (
        P("req", "tp"),
        P("req", "tp"),
        P("req", None, "tp"),
        P(None, "tp"),
        P("tp"),
        P("tp", None),
        P(),
        P(),
        P(),
        P(None, "tp"),
        P("tp"),
        P(None, "tp"),
        P("tp"),
        P("req", None, "tp"),
        P("req"),
        P("req"),
        P(),
        P(),
    )
    return jax.shard_map(
        per_device,
        mesh=mesh,
        in_specs=placed,
        out_specs=(P("req", "tp"), P("req", None, "tp"), P("req", None, "tp"), P()),
        check_vma=False,
    )
```

```python
import functools

import jax
import jax.numpy as jnp
from jax import lax
from jax.experimental import pallas as pl
from jax.experimental.pallas import tpu as pltpu
from jax.sharding import PartitionSpec as P

EPSILON = 1e-06
SQUARE_FLOOR = 0.25
LOG2_E = 1.4426950408889634
LANES = 128
EDGE_ROWS = 4
PLANE = 4
DIGIT = 7
VMEM_BYTES = 48 * 1024 * 1024
ROUND = 4
VECTOR_WEIGHT = 30000


def iota(shape, axis):
    return lax.broadcasted_iota(jnp.int32, shape, axis)


def one_hot(condition):
    return jnp.where(condition, 1.0, 0.0).astype(jnp.bfloat16)


def dot(lhs, rhs):
    return jnp.dot(lhs, rhs, preferred_element_type=jnp.float32)


def in_hbm(array):
    return pltpu.with_memory_space_constraint(array, pltpu.HBM)


def silu(value):
    return value * (0.5 + 0.5 * jnp.tanh(0.5 * value))


def to_step_major(requests, steps):
    rows = requests * steps
    row, col = iota((rows, rows), 0), iota((rows, rows), 1)
    return one_hot(col == lax.rem(row, requests) * steps + lax.div(row, requests))


def to_request_major(requests, steps):
    rows = requests * steps
    row, col = iota((rows, rows), 0), iota((rows, rows), 1)
    return one_hot(row == lax.rem(col, requests) * steps + lax.div(col, requests))


def by_request(index, scalars):
    out = jnp.zeros_like(index)
    for request, scalar in enumerate(scalars):
        out = jnp.where(index == request, scalar, out)
    return out


def conv_kernel(x_ref, edge_ref, weight_ref, bias_ref, proj_ref, conv_ref, partial_ref):
    lags, requests, _ = edge_ref.shape
    taps = weight_ref.shape[0]
    steps = x_ref.shape[0] // requests
    stream = dot(to_step_major(requests, steps), x_ref[...])
    window = [edge_ref[k].astype(jnp.float32) for k in range(lags)]
    window += [stream[t * requests : (t + 1) * requests] for t in range(steps)]
    weight = [weight_ref[k : k + 1, :] for k in range(taps)]
    outs = []
    for t in range(steps):
        summed = bias_ref[...] + weight[0] * window[t]
        for k in range(1, taps):
            summed = summed + weight[k] * window[t + k]
        outs.append(silu(summed))
    conv_out = jnp.concatenate(outs, axis=0).astype(jnp.bfloat16)
    conv_ref[...] = conv_out
    partial = lax.dot_general(
        conv_out, proj_ref[...], (((1,), (1,)), ((), ())), preferred_element_type=jnp.float32
    )

    @pl.when(pl.program_id(0) == 0)
    def _():
        partial_ref[...] = partial

    @pl.when(pl.program_id(0) > 0)
    def _():
        partial_ref[...] += partial


def conv_project(x_in, conv_edge, conv_weight, conv_bias, proj):
    rows, channels = x_in.shape
    lags, requests, _ = conv_edge.shape
    taps, width = conv_weight.shape[0], proj.shape[0]
    block = min(1024, channels)
    return pl.pallas_call(
        conv_kernel,
        grid=(channels // block,),
        in_specs=[
            pl.BlockSpec((rows, block), lambda j: (0, j)),
            pl.BlockSpec((lags, requests, block), lambda j: (0, 0, j)),
            pl.BlockSpec((taps, block), lambda j: (0, j)),
            pl.BlockSpec((1, block), lambda j: (0, j)),
            pl.BlockSpec((width, block), lambda j: (0, j)),
        ],
        out_specs=[
            pl.BlockSpec((rows, block), lambda j: (0, j)),
            pl.BlockSpec((rows, width), lambda j: (0, 0)),
        ],
        out_shape=[
            pltpu.HBM((rows, channels), jnp.bfloat16),
            pltpu.HBM((rows, width), jnp.float32),
        ],
        compiler_params=pltpu.CompilerParams(
            dimension_semantics=("arbitrary",), vmem_limit_bytes=VMEM_BYTES
        ),
        name="conv_project",
    )(*(in_hbm(a) for a in (x_in, conv_edge, conv_weight, conv_bias, proj)))


def kept_edge_kernel(
    place_ref, accepted_ref, length_ref, owner_ref, x_ref, edge_ref, _, *group_refs
):
    lags, requests, block = edge_ref.shape
    steps = x_ref.shape[0] // requests
    place = place_ref[0]
    accepted = [accepted_ref[r] for r in range(requests)]
    lengths = [length_ref[r] + accepted[r] + 1 for r in range(requests)]
    deltas = [owner_ref[place * requests + r] ^ place for r in range(requests)]
    height = len(group_refs) * PLANE * EDGE_ROWS
    slot = lax.div(iota((height, 1), 0), EDGE_ROWS)
    lag = lax.rem(iota((height, 1), 0), EDGE_ROWS)

    def pick(request, position):
        return one_hot(
            (slot == by_request(request, deltas))
            & (position - by_request(request, accepted) == lag)
            & (lag < lags)
        )

    col = iota((1, requests * steps), 1)
    picked = dot(pick(lax.div(col, steps), lax.rem(col, steps) + lags), x_ref[...])
    col = iota((1, lags * requests), 1)
    edge = jnp.concatenate([edge_ref[k].astype(jnp.float32) for k in range(lags)], axis=0)
    picked += dot(pick(lax.rem(col, requests), lax.div(col, requests)), edge.astype(jnp.bfloat16))
    low = [length & ((1 << DIGIT) - 1) for length in lengths]
    high = [length >> DIGIT for length in lengths]
    numbers = by_request(iota((1, block), 1), accepted + low + high).astype(jnp.float32)
    picked = jnp.where(lag == lags, numbers, picked).astype(jnp.bfloat16)
    group = PLANE * EDGE_ROWS
    for d, ref in enumerate(group_refs):
        ref[...] = picked[d * group : (d + 1) * group]


def kept_edges(scalars, x_in, conv_edge, after, owners):
    rows, channels = x_in.shape
    lags, requests, _ = conv_edge.shape
    block = min(2048, channels)
    groups = owners // PLANE
    return pl.pallas_call(
        kept_edge_kernel,
        grid=(channels // block,),
        in_specs=[pl.BlockSpec(memory_space=pltpu.SMEM)] * len(scalars)
        + [
            pl.BlockSpec((rows, block), lambda j: (0, j)),
            pl.BlockSpec((lags, requests, block), lambda j: (0, 0, j)),
            pl.BlockSpec(memory_space=pl.ANY),
        ],
        out_specs=[pl.BlockSpec((PLANE * EDGE_ROWS, block), lambda j: (0, j))] * groups,
        out_shape=[pltpu.HBM((PLANE * EDGE_ROWS, channels), jnp.bfloat16)] * groups,
        compiler_params=pltpu.CompilerParams(
            dimension_semantics=("arbitrary",), vmem_limit_bytes=VMEM_BYTES
        ),
        name="kept_edges",
    )(*scalars, in_hbm(x_in), in_hbm(conv_edge), in_hbm(after))


def regroup_kernel(*refs):
    groups = len(refs) - 1 - PLANE
    rows = jnp.concatenate([ref[...].astype(jnp.float32) for ref in refs[:groups]], axis=0)
    for p, out_ref in enumerate(refs[-PLANE:]):
        parts = [
            rows[(d * PLANE + p) * EDGE_ROWS : (d * PLANE + p + 1) * EDGE_ROWS] for d in range(groups)
        ]
        out_ref[...] = jnp.concatenate(parts, axis=0).astype(jnp.bfloat16)


def regroup(arrived, after):
    rows, channels = arrived[0].shape
    block = min(1024, channels)
    height = len(arrived) * EDGE_ROWS
    return pl.pallas_call(
        regroup_kernel,
        grid=(channels // block,),
        in_specs=[pl.BlockSpec((rows, block), lambda j: (0, j))] * len(arrived)
        + [pl.BlockSpec(memory_space=pl.ANY)],
        out_specs=[pl.BlockSpec((height, block), lambda j: (0, j))] * PLANE,
        out_shape=[pltpu.HBM((height, channels), jnp.bfloat16)] * PLANE,
        compiler_params=pltpu.CompilerParams(
            dimension_semantics=("arbitrary",), vmem_limit_bytes=VMEM_BYTES
        ),
        name="regroup",
    )(*arrived, in_hbm(after))


def rms_scaled(values, gain, floor_value, eps_value):
    square = jnp.mean(values * values, axis=-1, keepdims=True)
    return (values * lax.rsqrt(jnp.maximum(square, floor_value) + eps_value) * gain).astype(jnp.bfloat16)


def summed(part_refs):
    total = part_refs[0][...]
    for part in part_refs[1:]:
        total = total + part[...]
    return total


def softplus(raw):
    return jnp.maximum(raw, 0.0) + jnp.log1p(jnp.exp(-jnp.abs(raw)))


def kept_kernel(parts, *refs):
    place_ref, accepted_ref, owner_ref = refs[:3]
    (
        dt_gain_ref, b_gain_ref, dt_weight_ref, dt_bias_ref, a_log_ref, conv_ref, state_ref,
        slot_ref, low_ref, in_ref, size_ref, drive_ref, rate_ref,
    ) = refs[3 + parts :]
    rank, states = dt_gain_ref.shape[1], b_gain_ref.shape[1]
    requests = accepted_ref.shape[0]
    rows, block = conv_ref.shape
    steps = rows // requests

    @pl.when(pl.program_id(0) == 0)
    def _():
        total = summed(refs[3 : 3 + parts])
        low_ref[...] = rms_scaled(total[:, :rank], dt_gain_ref[...], 0.0, EPSILON)
        in_map = rms_scaled(total[:, rank : rank + states], b_gain_ref[...], SQUARE_FLOOR, 0.0)
        turned = jnp.transpose(in_map.astype(jnp.float32))
        for row in range(rows):
            t, r = divmod(row, requests)
            in_ref[r * states : (r + 1) * states, t * LANES : (t + 1) * LANES] = (
                jnp.broadcast_to(turned[:, row : row + 1], (states, LANES))
            )

    row = iota((rows, 1), 0)
    live = lax.div(row, requests) < by_request(
        lax.rem(row, requests), [accepted_ref[r] for r in range(requests)]
    )
    size = softplus(dot(low_ref[...], dt_weight_ref[...]) + dt_bias_ref[...])
    size = jnp.where(live, size, 0.0)
    drive = size * conv_ref[...].astype(jnp.float32)
    for c in range(block // LANES):
        size_ref[c] = size[:, c * LANES : (c + 1) * LANES]
        drive_ref[c] = drive[:, c * LANES : (c + 1) * LANES]
    rate_ref[...] = jnp.exp(a_log_ref[...]) * (-LOG2_E)

    span = min(1024, block)
    halves = states // 8
    for r in range(requests):
        slot = owner_ref[place_ref[0] * requests + r]
        rounds = lax.div(accepted_ref[r] + (ROUND - 1), ROUND)
        for first in range(0, block, span):
            tiles = [slice(c, c + LANES) for c in range(first, first + span, LANES)]

            def one_round(i, hidden):
                hidden = [list(h) for h in hidden]
                for u in range(ROUND):
                    t = i * ROUND + u
                    at = pl.ds(t * requests + r, 8, stride=0)
                    b = [
                        in_ref[
                            r * states + 8 * h : r * states + 8 * (h + 1),
                            pl.ds(pl.multiple_of(t * LANES, LANES), LANES),
                        ]
                        for h in range(halves)
                    ]
                    for c, tile in enumerate(tiles):
                        place = first // LANES + c
                        now, drive = size_ref[place, at, :], drive_ref[place, at, :]
                        for h in range(halves):
                            decay = jnp.exp2(now * rate_ref[8 * h : 8 * (h + 1), tile])
                            hidden[h][c] = decay * hidden[h][c] + drive * b[h]
                return tuple(tuple(h) for h in hidden)

            old = state_ref[r * states : (r + 1) * states, first : first + span].astype(jnp.float32)
            start = tuple(
                tuple(
                    old[8 * h : 8 * (h + 1), c * LANES : (c + 1) * LANES] for c in range(len(tiles))
                )
                for h in range(halves)
            )
            done = lax.fori_loop(0, rounds, one_round, start)
            new = jnp.concatenate([jnp.concatenate(h, axis=1) for h in done], axis=0)
            slot_ref[slot, :, first : first + span] = new.astype(jnp.bfloat16)


def kept_states(scalars, partials, gains, dt_weight, dt_bias, a_log, conv, state, slots):
    rows, channels = conv.shape
    states, rank = a_log.shape[0], dt_weight.shape[0]
    requests = scalars[1].shape[0]
    block = min(1024, channels)

    def whole(array):
        return pl.BlockSpec(array.shape, lambda j: (0, 0))

    wide = [in_hbm(dt_weight), dt_bias, in_hbm(a_log), in_hbm(conv), in_hbm(state)]
    return pl.pallas_call(
        functools.partial(kept_kernel, len(partials)),
        grid=(channels // block,),
        in_specs=[pl.BlockSpec(memory_space=pltpu.SMEM)] * len(scalars)
        + [whole(a) for a in (*partials, *gains)]
        + [pl.BlockSpec((a.shape[0], block), lambda j: (0, j)) for a in wide],
        out_specs=pl.BlockSpec((slots, states, block), lambda j: (0, 0, j)),
        out_shape=pltpu.HBM((slots, states, channels), jnp.bfloat16),
        scratch_shapes=[
            pltpu.VMEM((rows, rank), jnp.bfloat16),
            pltpu.VMEM((requests * states, rows // requests * LANES), jnp.float32),
            pltpu.VMEM((block // LANES, rows, LANES), jnp.float32),
            pltpu.VMEM((block // LANES, rows, LANES), jnp.float32),
            pltpu.VMEM((states, block), jnp.float32),
        ],
        compiler_params=pltpu.CompilerParams(
            dimension_semantics=("arbitrary",), vmem_limit_bytes=VMEM_BYTES
        ),
        cost_estimate=pl.CostEstimate(
            flops=VECTOR_WEIGHT * 4 * rows * states * channels,
            transcendentals=rows * states * channels,
            bytes_accessed=2 * channels * (rows + rank + states * (requests + slots)),
        ),
        name="kept_states",
    )(*scalars, *partials, *gains, *wide)


def scan_kernel(parts, *refs):
    (
        dt_gain_ref, b_gain_ref, c_gain_ref, dt_weight_ref, dt_bias_ref, a_log_ref, skip_ref,
        conv_ref, state_ref, z_ref, mixed_ref,
        low_ref, in_ref, out_ref, size_ref, drive_ref, rate_ref, start_ref, sum_ref,
    ) = refs[parts:]
    rank, states = dt_gain_ref.shape[1], b_gain_ref.shape[1]
    rows, block = conv_ref.shape
    requests = state_ref.shape[0] // states
    steps = rows // requests

    @pl.when(pl.program_id(0) == 0)
    def _():
        total = summed(refs[:parts])
        low_ref[...] = rms_scaled(total[:, :rank], dt_gain_ref[...], 0.0, EPSILON)
        in_map = rms_scaled(total[:, rank : rank + states], b_gain_ref[...], SQUARE_FLOOR, 0.0)
        out_map = rms_scaled(total[:, rank + states :], c_gain_ref[...], SQUARE_FLOOR, 0.0)
        wide = states * LANES
        spread = one_hot(lax.div(iota((states, wide), 1), LANES) == iota((states, wide), 0))
        in_ref[...] = dot(in_map, spread)
        out_ref[...] = dot(out_map, spread)

    conv = conv_ref[...].astype(jnp.float32)
    size = softplus(dot(low_ref[...], dt_weight_ref[...]) + dt_bias_ref[...])
    size_ref[...] = size
    drive_ref[...] = size * conv
    start_ref[...] = dot(to_step_major(requests, states), state_ref[...])
    rate = jnp.exp(a_log_ref[...]) * (-LOG2_E)
    for n in range(states):
        rate_ref[n * requests : (n + 1) * requests, :] = jnp.broadcast_to(
            rate[n : n + 1, :], (requests, block)
        )

    pair = 2 if block % (2 * LANES) == 0 else 1

    def columns(c, carry):
        spans = [pl.ds(pl.multiple_of((c * pair + i) * LANES, LANES), LANES) for i in range(pair)]
        start = tuple(
            tuple(start_ref[n * requests : (n + 1) * requests, s] for s in spans)
            for n in range(states)
        )

        def step(t, hidden):
            at = pl.ds(pl.multiple_of(t * requests, requests), requests)
            sizes = [size_ref[at, s] for s in spans]
            drives = [drive_ref[at, s] for s in spans]
            sums = [None] * pair
            new = []
            for n in range(states):
                b = in_ref[at, n * LANES : (n + 1) * LANES]
                c_map = out_ref[at, n * LANES : (n + 1) * LANES]
                own = slice(n * requests, (n + 1) * requests)
                mine = []
                for i, s in enumerate(spans):
                    h = jnp.exp2(sizes[i] * rate_ref[own, s]) * hidden[n][i] + drives[i] * b
                    term = c_map * h
                    sums[i] = term if sums[i] is None else sums[i] + term
                    mine.append(h)
                new.append(tuple(mine))
            for i, s in enumerate(spans):
                sum_ref[at, s] = sums[i]
            return tuple(new)

        lax.fori_loop(0, steps, step, start, unroll=2)
        return carry

    lax.fori_loop(0, block // (pair * LANES), columns, 0)

    gate = silu(dot(to_step_major(requests, steps), z_ref[...]))
    mixed = ((sum_ref[...] + skip_ref[...] * conv) * gate).astype(jnp.bfloat16)
    mixed_ref[...] = dot(to_request_major(requests, steps), mixed).astype(jnp.bfloat16)


def scan(partials, gains, dt_weight, dt_bias, a_log, skip, conv, state, z_gate):
    rows, channels = conv.shape
    states, rank = a_log.shape[0], dt_weight.shape[0]
    block = min(512, channels)

    def whole(array):
        return pl.BlockSpec(array.shape, lambda j: (0, 0))

    wide = [in_hbm(dt_weight), dt_bias, in_hbm(a_log), skip, in_hbm(conv), in_hbm(state), in_hbm(z_gate)]
    tall = pltpu.VMEM((rows, block), jnp.float32)
    table = pltpu.VMEM((rows, states * LANES), jnp.float32)
    return pl.pallas_call(
        functools.partial(scan_kernel, len(partials)),
        grid=(channels // block,),
        in_specs=[whole(a) for a in (*partials, *gains)]
        + [pl.BlockSpec((a.shape[0], block), lambda j: (0, j)) for a in wide],
        out_specs=pl.BlockSpec((rows, block), lambda j: (0, j)),
        out_shape=jax.ShapeDtypeStruct((rows, channels), jnp.bfloat16),
        scratch_shapes=[
            pltpu.VMEM((rows, rank), jnp.bfloat16), table, table, tall, tall,
            pltpu.VMEM((state.shape[0], block), jnp.float32),
            pltpu.VMEM((state.shape[0], block), jnp.float32),
            tall,
        ],
        compiler_params=pltpu.CompilerParams(
            dimension_semantics=("arbitrary",), vmem_limit_bytes=VMEM_BYTES
        ),
        cost_estimate=pl.CostEstimate(
            flops=VECTOR_WEIGHT * 8 * rows * states * channels,
            transcendentals=rows * states * channels,
            bytes_accessed=2 * channels * (3 * rows + rank),
        ),
        name="scan",
    )(*partials, *gains, *wide)


def edge_kernel(steps, requests, place_ref, source_ref, count_ref, range_ref, *refs):
    group_refs, edge_ref, stats_ref = refs[:-2], refs[-2], refs[-1]
    own_most, lags, block = edge_ref.shape
    groups = group_refs[0].shape[0] // EDGE_ROWS
    height = len(group_refs) * groups * EDGE_ROWS
    place = place_ref[0]

    def sender(index):
        p, d = lax.div(index, groups * EDGE_ROWS), lax.rem(lax.div(index, EDGE_ROWS), groups)
        return (d * PLANE + p) ^ place

    got = jnp.concatenate([ref[...] for ref in group_refs], axis=0)
    sources = [jnp.where(i < count_ref[0], source_ref[i], -1) for i in range(own_most)]
    row, col = iota((own_most * 8, 1), 0), iota((1, height), 1)
    wanted = jnp.full((own_most * 8, 1), -1, jnp.int32)
    for i, source in enumerate(sources):
        wanted = jnp.where(lax.div(row, 8) == i, source, wanted)
    pick = (sender(col) == wanted) & (lax.rem(col, EDGE_ROWS) == lax.rem(row, 8))
    picked = dot(one_hot(pick), got)
    for i in range(own_most):
        edge_ref[i] = picked[i * 8 : i * 8 + lags].astype(jnp.bfloat16)

    @pl.when(pl.program_id(0) == 0)
    def _():
        numbers = got[:, :LANES].astype(jnp.float32)
        row, lane = iota((height, LANES), 0), iota((height, LANES), 1)
        mine = lax.rem(row, EDGE_ROWS) == lags
        request = sender(row) * requests + lax.rem(lane, requests)
        digit = lax.div(lane, requests)
        counts = jnp.where(digit == 0, numbers, 0.0)
        lengths = jnp.where(digit == 1, numbers, 0.0) + jnp.where(
            digit == 2, numbers * float(1 << DIGIT), 0.0
        )
        tenants = range_ref.shape[0]
        sums, loads, members = [], [], []
        for k in range(tenants):
            start, end = range_ref[k, 0], range_ref[k, 1]
            inside = mine & (request >= start) & (request < end)
            sums.append(jnp.sum(jnp.where(inside, counts, 0.0), keepdims=True))
            loads.append(jnp.sum(jnp.where(inside, lengths, 0.0), keepdims=True))
            members.append((jnp.zeros((1, 1), jnp.int32) + (end - start)).astype(jnp.float32))
        mean = sum(loads[1:], loads[0]) / sum(members[1:], members[0])
        out = jnp.zeros((tenants, 2), jnp.float32)
        row, col = iota((tenants, 2), 0), iota((tenants, 2), 1)
        for k in range(tenants):
            rate = sums[k] / (float(steps) * members[k])
            load = loads[k] / members[k] / mean
            out = jnp.where(row == k, jnp.where(col == 0, rate, load), out)
        stats_ref[...] = out


def settle_edges(place, source, count, tenant_range, got, own_most, lags, steps, requests):
    smem = pl.BlockSpec(memory_space=pltpu.SMEM)
    height, channels = got[0].shape
    block = min(2048, channels)
    stats = (tenant_range.shape[0], 2)
    return pl.pallas_call(
        functools.partial(edge_kernel, steps, requests),
        grid=(channels // block,),
        in_specs=[smem] * 4 + [pl.BlockSpec((height, block), lambda j: (0, j))] * len(got),
        out_specs=[
            pl.BlockSpec((own_most, lags, block), lambda j: (0, 0, j)),
            pl.BlockSpec(stats, lambda j: (0, 0)),
        ],
        out_shape=[
            jax.ShapeDtypeStruct((own_most, lags, channels), jnp.bfloat16),
            jax.ShapeDtypeStruct(stats, jnp.float32),
        ],
        compiler_params=pltpu.CompilerParams(
            dimension_semantics=("arbitrary",), vmem_limit_bytes=VMEM_BYTES
        ),
        name="settle_edges",
    )(place, source, count, tenant_range, *got)


def settle_kernel(source_ref, count_ref, got_ref, owned_ref, blank_ref, sems):
    own_most = owned_ref.shape[0]
    blank_ref[...] = jnp.zeros_like(blank_ref)

    def copy(i, filled):
        origin = got_ref.at[source_ref[i]] if filled else blank_ref
        return pltpu.make_async_copy(origin, owned_ref.at[i], sems.at[i])

    for act in ("start", "wait"):
        for i in range(own_most):
            for filled in (True, False):

                @pl.when((i < count_ref[0]) == filled)
                def _():
                    getattr(copy(i, filled), act)()


def settle_states(source, count, got, own_most):
    smem = pl.BlockSpec(memory_space=pltpu.SMEM)
    anywhere = pl.BlockSpec(memory_space=pl.ANY)
    return pl.pallas_call(
        settle_kernel,
        in_specs=[smem, smem, pl.BlockSpec(memory_space=pltpu.VMEM)],
        out_specs=anywhere,
        out_shape=jax.ShapeDtypeStruct((own_most, *got.shape[1:]), got.dtype),
        scratch_shapes=[
            pltpu.VMEM(got.shape[1:], got.dtype),
            pltpu.SemaphoreType.DMA((own_most,)),
        ],
        compiler_params=pltpu.CompilerParams(vmem_limit_bytes=VMEM_BYTES),
        name="settle_states",
    )(source, count, got)


def per_device(
    x_in, z_gate, conv_edge, conv_weight, conv_bias, x_proj_weight, dt_gain, b_gain, c_gain,
    dt_proj_weight, dt_bias, a_log, skip, ssm_state, accepted, prompt_len, tenant_range, owner,
):
    requests, states, channels = ssm_state.shape
    lags = conv_edge.shape[1]
    owners = lax.axis_size("req")
    own_most = min(requests + requests // 2, owners)
    place = lax.axis_index("req").astype(jnp.int32).reshape(1)

    by_lag = jnp.transpose(conv_edge, (1, 0, 2))
    conv, partial = conv_project(
        x_in, by_lag, conv_weight, conv_bias.reshape(1, -1), x_proj_weight.T
    )
    if lax.axis_size("tp") == 2:
        partials = (in_hbm(partial), lax.ppermute(partial, "tp", [(0, 1), (1, 0)]))
    else:
        partials = (lax.psum(partial, "tp"),)

    def swap(rows, delta):
        return lax.ppermute(rows, "req", [(i, i ^ delta) for i in range(owners)]) if delta else rows

    groups = kept_edges((place, accepted, prompt_len, owner), x_in, by_lag, partial, owners)
    groups = [swap(rows, d * PLANE) for d, rows in enumerate(groups)]

    hits = jnp.any(owner.reshape(owners, requests) == place, axis=1)
    ids = jnp.arange(owners, dtype=jnp.int32)
    ranks = jnp.sum((hits[None, :] & (ids[None, :] < ids[:, None])).astype(jnp.int32), axis=1)
    at = hits[None, :] & (ranks[None, :] == jnp.arange(own_most, dtype=jnp.int32)[:, None])
    source = jnp.sum(jnp.where(at, ids[None, :], 0), axis=1)
    count = jnp.sum(hits.astype(jnp.int32)).reshape(1)

    gains = (dt_gain.reshape(1, -1), b_gain.reshape(1, -1), c_gain.reshape(1, -1))
    bias = dt_bias.reshape(1, -1)
    state = ssm_state.reshape(requests * states, channels)
    slots = kept_states(
        (place, accepted, owner), partials, gains[:2], dt_proj_weight, bias, a_log, conv, state, owners
    )
    got = lax.all_to_all(slots, "req", split_axis=0, concat_axis=0, tiled=True)
    mixed = scan(
        partials, gains, dt_proj_weight, bias, a_log, skip.reshape(1, -1), conv, state, z_gate
    )
    groups = [swap(rows, p) for p, rows in enumerate(regroup(groups, mixed))]
    owned_edge, tenant_stats = settle_edges(
        place, source, count, tenant_range, groups, own_most, lags, x_in.shape[0] // requests,
        requests,
    )
    owned = settle_states(source, count, got, own_most)
    return (mixed, owned, owned_edge, tenant_stats)


def solution(mesh):
    placed = (
        P("req", "tp"),
        P("req", "tp"),
        P("req", None, "tp"),
        P(None, "tp"),
        P("tp"),
        P("tp", None),
        P(),
        P(),
        P(),
        P(None, "tp"),
        P("tp"),
        P(None, "tp"),
        P("tp"),
        P("req", None, "tp"),
        P("req"),
        P("req"),
        P(),
        P(),
    )
    return jax.shard_map(
        per_device,
        mesh=mesh,
        in_specs=placed,
        out_specs=(P("req", "tp"), P("req", None, "tp"), P("req", None, "tp"), P()),
        check_vma=False,
    )
```

```python
import functools

import jax
import jax.numpy as jnp
from jax import lax
from jax.experimental import pallas as pl
from jax.experimental.pallas import tpu as pltpu
from jax.sharding import PartitionSpec as P

EPSILON = 1e-06
SQUARE_FLOOR = 0.25
LOG2_E = 1.4426950408889634
LANES = 128
EDGE_ROWS = 4
PLANE = 4
DIGIT = 7
VMEM_BYTES = 24 * 1024 * 1024
ROUND = 4
VECTOR_WEIGHT = 30000


def iota(shape, axis):
    return lax.broadcasted_iota(jnp.int32, shape, axis)


def one_hot(condition):
    return jnp.where(condition, 1.0, 0.0).astype(jnp.bfloat16)


def dot(lhs, rhs):
    return jnp.dot(lhs, rhs, preferred_element_type=jnp.float32)


def in_hbm(array):
    return pltpu.with_memory_space_constraint(array, pltpu.HBM)


def silu(value):
    return value * (0.5 + 0.5 * jnp.tanh(0.5 * value))


def to_step_major(requests, steps):
    rows = requests * steps
    row, col = iota((rows, rows), 0), iota((rows, rows), 1)
    return one_hot(col == lax.rem(row, requests) * steps + lax.div(row, requests))


def to_request_major(requests, steps):
    rows = requests * steps
    row, col = iota((rows, rows), 0), iota((rows, rows), 1)
    return one_hot(row == lax.rem(col, requests) * steps + lax.div(col, requests))


def by_request(index, scalars):
    out = jnp.zeros_like(index)
    for request, scalar in enumerate(scalars):
        out = jnp.where(index == request, scalar, out)
    return out


def conv_kernel(
    x_hbm, edge_hbm, weight_hbm, bias_hbm, proj_hbm, conv_hbm, partial_ref,
    x_ref, edge_ref, weight_ref, bias_ref, proj_ref, conv_ref, sems, out_sems,
):
    lags, requests, channels = edge_ref.shape
    taps = weight_ref.shape[0]
    steps = x_ref.shape[0] // requests
    block = min(1024, channels)
    pieces = [slice(c, c + block) for c in range(0, channels, block)]
    small = [(weight_hbm, weight_ref), (bias_hbm, bias_ref), (edge_hbm, edge_ref)]
    copies = [pltpu.make_async_copy(*pair, sems.at[i]) for i, pair in enumerate(small)]
    for piece in pieces:
        for pair in ((x_hbm, x_ref), (proj_hbm, proj_ref)):
            copies.append(
                pltpu.make_async_copy(*(ref.at[:, piece] for ref in pair), sems.at[len(copies)])
            )
    for copy in copies:
        copy.start()
    results = [
        pltpu.make_async_copy(conv_ref.at[:, piece], conv_hbm.at[:, piece], out_sems.at[i])
        for i, piece in enumerate(pieces)
    ]
    order = to_step_major(requests, steps)
    for copy in copies[: len(small)]:
        copy.wait()
    for i, piece in enumerate(pieces):
        copies[len(small) + 2 * i].wait()
        stream = dot(order, x_ref[:, piece])
        window = [edge_ref[k, :, piece].astype(jnp.float32) for k in range(lags)]
        window += [stream[t * requests : (t + 1) * requests] for t in range(steps)]
        weight = [weight_ref[k : k + 1, piece] for k in range(taps)]
        outs = []
        for t in range(steps):
            added = bias_ref[:, piece] + weight[0] * window[t]
            for k in range(1, taps):
                added = added + weight[k] * window[t + k]
            outs.append(silu(added))
        conv_out = jnp.concatenate(outs, axis=0).astype(jnp.bfloat16)
        conv_ref[:, piece] = conv_out
        results[i].start()
        copies[len(small) + 2 * i + 1].wait()
        partial = lax.dot_general(
            conv_out, proj_ref[:, piece], (((1,), (1,)), ((), ())),
            preferred_element_type=jnp.float32,
        )
        partial_ref[...] = partial if i == 0 else partial_ref[...] + partial
    for result in results:
        result.wait()


def conv_project(x_in, conv_edge, conv_weight, conv_bias, proj):
    rows, channels = x_in.shape
    operands = (x_in, conv_edge, conv_weight, conv_bias, proj)
    pieces = channels // min(1024, channels)
    return pl.pallas_call(
        conv_kernel,
        in_specs=[pl.BlockSpec(memory_space=pl.ANY)] * len(operands),
        out_specs=[pl.BlockSpec(memory_space=pl.ANY), pl.BlockSpec(memory_space=pltpu.VMEM)],
        out_shape=[
            pltpu.HBM((rows, channels), jnp.bfloat16),
            pltpu.HBM((rows, proj.shape[0]), jnp.float32),
        ],
        scratch_shapes=[pltpu.VMEM(a.shape, a.dtype) for a in operands]
        + [
            pltpu.VMEM((rows, channels), jnp.bfloat16),
            pltpu.SemaphoreType.DMA((3 + 2 * pieces,)),
            pltpu.SemaphoreType.DMA((pieces,)),
        ],
        compiler_params=pltpu.CompilerParams(vmem_limit_bytes=VMEM_BYTES),
        name="conv_project",
    )(*(in_hbm(a) for a in operands))


def kept_edge_kernel(
    place_ref, accepted_ref, length_ref, owner_ref, x_ref, edge_ref, _, *group_refs
):
    lags, requests, block = edge_ref.shape
    steps = x_ref.shape[0] // requests
    place = place_ref[0]
    accepted = [accepted_ref[r] for r in range(requests)]
    lengths = [length_ref[r] + accepted[r] + 1 for r in range(requests)]
    deltas = [owner_ref[place * requests + r] ^ place for r in range(requests)]
    height = len(group_refs) * PLANE * EDGE_ROWS
    slot = lax.div(iota((height, 1), 0), EDGE_ROWS)
    lag = lax.rem(iota((height, 1), 0), EDGE_ROWS)

    def pick(request, position):
        return one_hot(
            (slot == by_request(request, deltas))
            & (position - by_request(request, accepted) == lag)
            & (lag < lags)
        )

    col = iota((1, requests * steps), 1)
    picked = dot(pick(lax.div(col, steps), lax.rem(col, steps) + lags), x_ref[...])
    col = iota((1, lags * requests), 1)
    edge = jnp.concatenate([edge_ref[k].astype(jnp.float32) for k in range(lags)], axis=0)
    picked += dot(pick(lax.rem(col, requests), lax.div(col, requests)), edge.astype(jnp.bfloat16))
    low = [length & ((1 << DIGIT) - 1) for length in lengths]
    high = [length >> DIGIT for length in lengths]
    numbers = by_request(iota((1, block), 1), accepted + low + high).astype(jnp.float32)
    picked = jnp.where(lag == lags, numbers, picked).astype(jnp.bfloat16)
    group = PLANE * EDGE_ROWS
    for d, ref in enumerate(group_refs):
        ref[...] = picked[d * group : (d + 1) * group]


def kept_edges(scalars, x_in, conv_edge, after, owners):
    rows, channels = x_in.shape
    lags, requests, _ = conv_edge.shape
    block = min(2048, channels)
    groups = owners // PLANE
    return pl.pallas_call(
        kept_edge_kernel,
        grid=(channels // block,),
        in_specs=[pl.BlockSpec(memory_space=pltpu.SMEM)] * len(scalars)
        + [
            pl.BlockSpec((rows, block), lambda j: (0, j)),
            pl.BlockSpec((lags, requests, block), lambda j: (0, 0, j)),
            pl.BlockSpec(memory_space=pl.ANY),
        ],
        out_specs=[pl.BlockSpec((PLANE * EDGE_ROWS, block), lambda j: (0, j))] * groups,
        out_shape=[pltpu.HBM((PLANE * EDGE_ROWS, channels), jnp.bfloat16)] * groups,
        compiler_params=pltpu.CompilerParams(
            dimension_semantics=("arbitrary",), vmem_limit_bytes=VMEM_BYTES
        ),
        name="kept_edges",
    )(*scalars, in_hbm(x_in), in_hbm(conv_edge), in_hbm(after))


def regroup_kernel(*refs):
    groups = len(refs) - 1 - PLANE
    rows = jnp.concatenate([ref[...].astype(jnp.float32) for ref in refs[:groups]], axis=0)
    for p, out_ref in enumerate(refs[-PLANE:]):
        parts = [
            rows[(d * PLANE + p) * EDGE_ROWS : (d * PLANE + p + 1) * EDGE_ROWS] for d in range(groups)
        ]
        out_ref[...] = jnp.concatenate(parts, axis=0).astype(jnp.bfloat16)


def regroup(arrived, after):
    rows, channels = arrived[0].shape
    block = min(1024, channels)
    height = len(arrived) * EDGE_ROWS
    return pl.pallas_call(
        regroup_kernel,
        grid=(channels // block,),
        in_specs=[pl.BlockSpec((rows, block), lambda j: (0, j))] * len(arrived)
        + [pl.BlockSpec(memory_space=pl.ANY)],
        out_specs=[pl.BlockSpec((height, block), lambda j: (0, j))] * PLANE,
        out_shape=[pltpu.HBM((height, channels), jnp.bfloat16)] * PLANE,
        compiler_params=pltpu.CompilerParams(
            dimension_semantics=("arbitrary",), vmem_limit_bytes=VMEM_BYTES
        ),
        name="regroup",
    )(*arrived, in_hbm(after))


def rms_scaled(values, gain, floor_value, eps_value):
    square = jnp.mean(values * values, axis=-1, keepdims=True)
    return (values * lax.rsqrt(jnp.maximum(square, floor_value) + eps_value) * gain).astype(jnp.bfloat16)


def summed(part_refs):
    total = part_refs[0][...]
    for part in part_refs[1:]:
        total = total + part[...]
    return total


def softplus(raw):
    return jnp.maximum(raw, 0.0) + jnp.log1p(jnp.exp(-jnp.abs(raw)))


def kept_kernel(parts, *refs):
    place_ref, accepted_ref, owner_ref = refs[:3]
    (
        dt_gain_ref, b_gain_ref, dt_weight_ref, dt_bias_ref, state_ref, a_log_hbm, conv_hbm,
        slot_ref, part_ref, a_log_ref, conv_ref, in_ref, size_ref, drive_ref, rate_ref, new_ref,
        in_sems, sems,
    ) = refs[3 + parts :]
    pairs = ((refs[3], part_ref), (a_log_hbm, a_log_ref), (conv_hbm, conv_ref))
    copies = [pltpu.make_async_copy(*pair, in_sems.at[i]) for i, pair in enumerate(pairs)]
    for copy in copies:
        copy.start()
    rank, states = dt_gain_ref.shape[1], b_gain_ref.shape[1]
    requests = accepted_ref.shape[0]
    rows, channels = conv_ref.shape
    steps = rows // requests
    span = min(1024, channels)
    halves = states // 8

    copies[0].wait()
    total = part_ref[...]
    for part in refs[4 : 3 + parts]:
        total = total + part[...]
    low = rms_scaled(total[:, :rank], dt_gain_ref[...], 0.0, EPSILON)
    in_map = rms_scaled(total[:, rank : rank + states], b_gain_ref[...], SQUARE_FLOOR, 0.0)
    turned = jnp.transpose(in_map.astype(jnp.float32))
    for row in range(rows):
        t, r = divmod(row, requests)
        in_ref[r * states : (r + 1) * states, t * LANES : (t + 1) * LANES] = jnp.broadcast_to(
            turned[:, row : row + 1], (states, LANES)
        )

    row = iota((rows, 1), 0)
    live = lax.div(row, requests) < by_request(
        lax.rem(row, requests), [accepted_ref[r] for r in range(requests)]
    )
    copies[1].wait()
    copies[2].wait()
    for first in range(0, channels, span):
        piece = slice(first, first + span)
        size = softplus(dot(low, dt_weight_ref[:, piece]) + dt_bias_ref[:, piece])
        size = jnp.where(live, size, 0.0)
        drive = size * conv_ref[:, piece].astype(jnp.float32)
        for c in range(span // LANES):
            tile = slice(c * LANES, (c + 1) * LANES)
            size_ref[first // LANES + c, :rows, :] = size[:, tile]
            drive_ref[first // LANES + c, :rows, :] = drive[:, tile]
        rate_ref[:, piece] = jnp.exp(a_log_ref[:, piece]) * (-LOG2_E)

    def one_request(r, carry):
        own = pl.multiple_of(r * states, states)
        rounds = lax.div(accepted_ref[r] + (ROUND - 1), ROUND)

        def one_span(part, inner):
            tiles = [pl.multiple_of(part * span + c, LANES) for c in range(0, span, LANES)]

            def one_round(i, hidden):
                hidden = [list(h) for h in hidden]
                for u in range(ROUND):
                    t = i * ROUND + u
                    at = pl.ds(t * requests + r, 8, stride=0)
                    lanes = pl.ds(pl.multiple_of(t * LANES, LANES), LANES)
                    b = [in_ref[pl.ds(own + 8 * h, 8), lanes] for h in range(halves)]
                    for c, tile in enumerate(tiles):
                        place = part * (span // LANES) + c
                        now, drive = size_ref[place, at, :], drive_ref[place, at, :]
                        for h in range(halves):
                            rate = rate_ref[8 * h : 8 * (h + 1), pl.ds(tile, LANES)]
                            hidden[h][c] = jnp.exp2(now * rate) * hidden[h][c] + drive * b[h]
                return tuple(tuple(h) for h in hidden)

            lanes = pl.ds(pl.multiple_of(part * span, span), span)
            old = state_ref[pl.ds(own, states), lanes].astype(jnp.float32)
            start = tuple(
                tuple(
                    old[8 * h : 8 * (h + 1), c * LANES : (c + 1) * LANES] for c in range(len(tiles))
                )
                for h in range(halves)
            )
            done = lax.fori_loop(0, rounds, one_round, start)
            new = jnp.concatenate([jnp.concatenate(h, axis=1) for h in done], axis=0)
            new_ref[r, :, lanes] = new.astype(jnp.bfloat16)
            return inner

        lax.fori_loop(0, channels // span, one_span, 0)
        slot = owner_ref[place_ref[0] * requests + r]
        pltpu.make_async_copy(new_ref.at[r], slot_ref.at[slot], sems.at[r]).start()
        return carry

    lax.fori_loop(0, requests, one_request, 0)
    for r in range(requests):
        slot = owner_ref[place_ref[0] * requests + r]
        pltpu.make_async_copy(new_ref.at[r], slot_ref.at[slot], sems.at[r]).wait()


def kept_states(scalars, partials, gains, dt_weight, dt_bias, a_log, conv, state, slots):
    rows, channels = conv.shape
    states, rank = a_log.shape[0], dt_weight.shape[0]
    requests = scalars[1].shape[0]
    near = [*partials[1:], *gains, dt_weight, dt_bias, state]
    far = [in_hbm(a_log), in_hbm(conv)]
    anywhere = pl.BlockSpec(memory_space=pl.ANY)
    return pl.pallas_call(
        functools.partial(kept_kernel, len(partials)),
        in_specs=[pl.BlockSpec(memory_space=pltpu.SMEM)] * len(scalars)
        + [anywhere]
        + [pl.BlockSpec(memory_space=pltpu.VMEM)] * len(near)
        + [anywhere] * len(far),
        out_specs=anywhere,
        out_shape=pltpu.HBM((slots, states, channels), jnp.bfloat16),
        scratch_shapes=[
            pltpu.VMEM(partials[0].shape, jnp.float32),
            pltpu.VMEM(a_log.shape, jnp.float32),
            pltpu.VMEM(conv.shape, jnp.bfloat16),
            pltpu.VMEM((requests * states, rows // requests * LANES), jnp.float32),
            pltpu.VMEM((channels // LANES, rows + 8, LANES), jnp.float32),
            pltpu.VMEM((channels // LANES, rows + 8, LANES), jnp.float32),
            pltpu.VMEM((states, channels), jnp.float32),
            pltpu.VMEM((requests, states, channels), jnp.bfloat16),
            pltpu.SemaphoreType.DMA((1 + len(far),)),
            pltpu.SemaphoreType.DMA((requests,)),
        ],
        compiler_params=pltpu.CompilerParams(vmem_limit_bytes=VMEM_BYTES),
        cost_estimate=pl.CostEstimate(
            flops=VECTOR_WEIGHT * 4 * rows * states * channels,
            transcendentals=rows * states * channels,
            bytes_accessed=2 * channels * (rows + rank + states * (requests + slots)),
        ),
        name="kept_states",
    )(*scalars, in_hbm(partials[0]), *near, *far)


def scan_kernel(parts, *refs):
    (
        dt_gain_ref, b_gain_ref, c_gain_ref, dt_weight_ref, dt_bias_ref, a_log_ref, skip_ref,
        conv_ref, state_ref, z_ref, mixed_ref,
        low_ref, in_ref, out_ref, size_ref, drive_ref, rate_ref, start_ref, sum_ref,
    ) = refs[parts:]
    rank, states = dt_gain_ref.shape[1], b_gain_ref.shape[1]
    rows, block = conv_ref.shape
    requests = state_ref.shape[0] // states
    steps = rows // requests

    @pl.when(pl.program_id(0) == 0)
    def _():
        total = summed(refs[:parts])
        low_ref[...] = rms_scaled(total[:, :rank], dt_gain_ref[...], 0.0, EPSILON)
        in_map = rms_scaled(total[:, rank : rank + states], b_gain_ref[...], SQUARE_FLOOR, 0.0)
        out_map = rms_scaled(total[:, rank + states :], c_gain_ref[...], SQUARE_FLOOR, 0.0)
        wide = states * LANES
        spread = one_hot(lax.div(iota((states, wide), 1), LANES) == iota((states, wide), 0))
        in_ref[...] = dot(in_map, spread)
        out_ref[...] = dot(out_map, spread)

    conv = conv_ref[...].astype(jnp.float32)
    size = softplus(dot(low_ref[...], dt_weight_ref[...]) + dt_bias_ref[...])
    size_ref[...] = size
    drive_ref[...] = size * conv
    start_ref[...] = dot(to_step_major(requests, states), state_ref[...])
    rate = jnp.exp(a_log_ref[...]) * (-LOG2_E)
    for n in range(states):
        rate_ref[n * requests : (n + 1) * requests, :] = jnp.broadcast_to(
            rate[n : n + 1, :], (requests, block)
        )

    pair = 2 if block % (2 * LANES) == 0 else 1

    def columns(c, carry):
        spans = [pl.ds(pl.multiple_of((c * pair + i) * LANES, LANES), LANES) for i in range(pair)]
        start = tuple(
            tuple(start_ref[n * requests : (n + 1) * requests, s] for s in spans)
            for n in range(states)
        )

        def step(t, hidden):
            at = pl.ds(pl.multiple_of(t * requests, requests), requests)
            sizes = [size_ref[at, s] for s in spans]
            drives = [drive_ref[at, s] for s in spans]
            sums = [None] * pair
            new = []
            for n in range(states):
                b = in_ref[at, n * LANES : (n + 1) * LANES]
                c_map = out_ref[at, n * LANES : (n + 1) * LANES]
                own = slice(n * requests, (n + 1) * requests)
                mine = []
                for i, s in enumerate(spans):
                    h = jnp.exp2(sizes[i] * rate_ref[own, s]) * hidden[n][i] + drives[i] * b
                    term = c_map * h
                    sums[i] = term if sums[i] is None else sums[i] + term
                    mine.append(h)
                new.append(tuple(mine))
            for i, s in enumerate(spans):
                sum_ref[at, s] = sums[i]
            return tuple(new)

        lax.fori_loop(0, steps, step, start, unroll=2)
        return carry

    lax.fori_loop(0, block // (pair * LANES), columns, 0)

    gate = silu(dot(to_step_major(requests, steps), z_ref[...]))
    mixed = ((sum_ref[...] + skip_ref[...] * conv) * gate).astype(jnp.bfloat16)
    mixed_ref[...] = dot(to_request_major(requests, steps), mixed).astype(jnp.bfloat16)


def scan(partials, gains, dt_weight, dt_bias, a_log, skip, conv, state, z_gate):
    rows, channels = conv.shape
    states, rank = a_log.shape[0], dt_weight.shape[0]
    block = min(512, channels)

    def whole(array):
        return pl.BlockSpec(array.shape, lambda j: (0, 0))

    wide = [in_hbm(dt_weight), dt_bias, in_hbm(a_log), skip, in_hbm(conv), in_hbm(state), in_hbm(z_gate)]
    tall = pltpu.VMEM((rows, block), jnp.float32)
    table = pltpu.VMEM((rows, states * LANES), jnp.float32)
    return pl.pallas_call(
        functools.partial(scan_kernel, len(partials)),
        grid=(channels // block,),
        in_specs=[whole(a) for a in (*partials, *gains)]
        + [pl.BlockSpec((a.shape[0], block), lambda j: (0, j)) for a in wide],
        out_specs=pl.BlockSpec((rows, block), lambda j: (0, j)),
        out_shape=jax.ShapeDtypeStruct((rows, channels), jnp.bfloat16),
        scratch_shapes=[
            pltpu.VMEM((rows, rank), jnp.bfloat16), table, table, tall, tall,
            pltpu.VMEM((state.shape[0], block), jnp.float32),
            pltpu.VMEM((state.shape[0], block), jnp.float32),
            tall,
        ],
        compiler_params=pltpu.CompilerParams(
            dimension_semantics=("arbitrary",), vmem_limit_bytes=VMEM_BYTES
        ),
        cost_estimate=pl.CostEstimate(
            flops=VECTOR_WEIGHT * 8 * rows * states * channels,
            transcendentals=rows * states * channels,
            bytes_accessed=2 * channels * (3 * rows + rank),
        ),
        name="scan",
    )(*partials, *gains, *wide)


def edge_kernel(steps, requests, place_ref, source_ref, count_ref, range_ref, *refs):
    group_refs, edge_ref, stats_ref = refs[:-2], refs[-2], refs[-1]
    own_most, lags, block = edge_ref.shape
    groups = group_refs[0].shape[0] // EDGE_ROWS
    height = len(group_refs) * groups * EDGE_ROWS
    place = place_ref[0]

    def sender(index):
        p, d = lax.div(index, groups * EDGE_ROWS), lax.rem(lax.div(index, EDGE_ROWS), groups)
        return (d * PLANE + p) ^ place

    got = jnp.concatenate([ref[...] for ref in group_refs], axis=0)
    sources = [jnp.where(i < count_ref[0], source_ref[i], -1) for i in range(own_most)]
    row, col = iota((own_most * 8, 1), 0), iota((1, height), 1)
    wanted = jnp.full((own_most * 8, 1), -1, jnp.int32)
    for i, source in enumerate(sources):
        wanted = jnp.where(lax.div(row, 8) == i, source, wanted)
    pick = (sender(col) == wanted) & (lax.rem(col, EDGE_ROWS) == lax.rem(row, 8))
    picked = dot(one_hot(pick), got)
    for i in range(own_most):
        edge_ref[i] = picked[i * 8 : i * 8 + lags].astype(jnp.bfloat16)

    @pl.when(pl.program_id(0) == 0)
    def _():
        numbers = got[:, :LANES].astype(jnp.float32)
        row, lane = iota((height, LANES), 0), iota((height, LANES), 1)
        mine = lax.rem(row, EDGE_ROWS) == lags
        request = sender(row) * requests + lax.rem(lane, requests)
        digit = lax.div(lane, requests)
        counts = jnp.where(digit == 0, numbers, 0.0)
        lengths = jnp.where(digit == 1, numbers, 0.0) + jnp.where(
            digit == 2, numbers * float(1 << DIGIT), 0.0
        )
        tenants = range_ref.shape[0]
        sums, loads, members = [], [], []
        for k in range(tenants):
            start, end = range_ref[k, 0], range_ref[k, 1]
            inside = mine & (request >= start) & (request < end)
            sums.append(jnp.sum(jnp.where(inside, counts, 0.0), keepdims=True))
            loads.append(jnp.sum(jnp.where(inside, lengths, 0.0), keepdims=True))
            members.append((jnp.zeros((1, 1), jnp.int32) + (end - start)).astype(jnp.float32))
        mean = sum(loads[1:], loads[0]) / sum(members[1:], members[0])
        out = jnp.zeros((tenants, 2), jnp.float32)
        row, col = iota((tenants, 2), 0), iota((tenants, 2), 1)
        for k in range(tenants):
            rate = sums[k] / (float(steps) * members[k])
            load = loads[k] / members[k] / mean
            out = jnp.where(row == k, jnp.where(col == 0, rate, load), out)
        stats_ref[...] = out


def settle_edges(place, source, count, tenant_range, got, own_most, lags, steps, requests):
    smem = pl.BlockSpec(memory_space=pltpu.SMEM)
    height, channels = got[0].shape
    block = min(2048, channels)
    stats = (tenant_range.shape[0], 2)
    return pl.pallas_call(
        functools.partial(edge_kernel, steps, requests),
        grid=(channels // block,),
        in_specs=[smem] * 4 + [pl.BlockSpec((height, block), lambda j: (0, j))] * len(got),
        out_specs=[
            pl.BlockSpec((own_most, lags, block), lambda j: (0, 0, j)),
            pl.BlockSpec(stats, lambda j: (0, 0)),
        ],
        out_shape=[
            jax.ShapeDtypeStruct((own_most, lags, channels), jnp.bfloat16),
            jax.ShapeDtypeStruct(stats, jnp.float32),
        ],
        compiler_params=pltpu.CompilerParams(
            dimension_semantics=("arbitrary",), vmem_limit_bytes=VMEM_BYTES
        ),
        name="settle_edges",
    )(place, source, count, tenant_range, *got)


def settle_kernel(source_ref, count_ref, got_ref, owned_ref, rows_ref, in_sems, out_sems):
    own_most = owned_ref.shape[0]

    def fetch(i):
        return pltpu.make_async_copy(got_ref.at[source_ref[i]], rows_ref.at[i], in_sems.at[i])

    def put(i):
        return pltpu.make_async_copy(rows_ref.at[i], owned_ref.at[i], out_sems.at[i])

    for i in range(own_most):

        @pl.when(i < count_ref[0])
        def _():
            fetch(i).start()

    for i in range(own_most):

        @pl.when(i < count_ref[0])
        def _():
            fetch(i).wait()

        @pl.when(i >= count_ref[0])
        def _():
            rows_ref[i] = jnp.zeros(rows_ref.shape[1:], rows_ref.dtype)

        put(i).start()
    for i in range(own_most):
        put(i).wait()


def settle_states(source, count, got, own_most):
    smem = pl.BlockSpec(memory_space=pltpu.SMEM)
    anywhere = pl.BlockSpec(memory_space=pl.ANY)
    shape = (own_most, *got.shape[1:])
    return pl.pallas_call(
        settle_kernel,
        in_specs=[smem, smem, anywhere],
        out_specs=anywhere,
        out_shape=pltpu.HBM(shape, got.dtype),
        scratch_shapes=[
            pltpu.VMEM(shape, got.dtype),
            pltpu.SemaphoreType.DMA((own_most,)),
            pltpu.SemaphoreType.DMA((own_most,)),
        ],
        compiler_params=pltpu.CompilerParams(vmem_limit_bytes=VMEM_BYTES),
        name="settle_states",
    )(source, count, got)


def per_device(
    x_in, z_gate, conv_edge, conv_weight, conv_bias, x_proj_weight, dt_gain, b_gain, c_gain,
    dt_proj_weight, dt_bias, a_log, skip, ssm_state, accepted, prompt_len, tenant_range, owner,
):
    requests, states, channels = ssm_state.shape
    lags = conv_edge.shape[1]
    owners = lax.axis_size("req")
    own_most = min(requests + requests // 2, owners)
    place = lax.axis_index("req").astype(jnp.int32).reshape(1)

    by_lag = jnp.transpose(conv_edge, (1, 0, 2))
    conv, partial = conv_project(
        x_in, by_lag, conv_weight, conv_bias.reshape(1, -1), x_proj_weight.T
    )
    if lax.axis_size("tp") == 2:
        partials = (partial, lax.ppermute(partial, "tp", [(0, 1), (1, 0)]))
    else:
        partials = (lax.psum(partial, "tp"),)

    def swap(rows, delta):
        return lax.ppermute(rows, "req", [(i, i ^ delta) for i in range(owners)]) if delta else rows

    groups = kept_edges((place, accepted, prompt_len, owner), x_in, by_lag, partial, owners)
    groups = [swap(rows, d * PLANE) for d, rows in enumerate(groups)]

    hits = jnp.any(owner.reshape(owners, requests) == place, axis=1)
    ids = jnp.arange(owners, dtype=jnp.int32)
    ranks = jnp.sum((hits[None, :] & (ids[None, :] < ids[:, None])).astype(jnp.int32), axis=1)
    at = hits[None, :] & (ranks[None, :] == jnp.arange(own_most, dtype=jnp.int32)[:, None])
    source = jnp.sum(jnp.where(at, ids[None, :], 0), axis=1)
    count = jnp.sum(hits.astype(jnp.int32)).reshape(1)

    gains = (dt_gain.reshape(1, -1), b_gain.reshape(1, -1), c_gain.reshape(1, -1))
    bias = dt_bias.reshape(1, -1)
    state = ssm_state.reshape(requests * states, channels)
    slots = kept_states(
        (place, accepted, owner), partials, gains[:2], dt_proj_weight, bias, a_log, conv, state, owners
    )
    got = lax.all_to_all(slots, "req", split_axis=0, concat_axis=0, tiled=True)
    mixed = scan(
        partials, gains, dt_proj_weight, bias, a_log, skip.reshape(1, -1), conv, state, z_gate
    )
    groups = [swap(rows, p) for p, rows in enumerate(regroup(groups, mixed))]
    owned_edge, tenant_stats = settle_edges(
        place, source, count, tenant_range, groups, own_most, lags, x_in.shape[0] // requests,
        requests,
    )
    owned = settle_states(source, count, got, own_most)
    return (mixed, owned, owned_edge, tenant_stats)


def solution(mesh):
    placed = (
        P("req", "tp"),
        P("req", "tp"),
        P("req", None, "tp"),
        P(None, "tp"),
        P("tp"),
        P("tp", None),
        P(),
        P(),
        P(),
        P(None, "tp"),
        P("tp"),
        P(None, "tp"),
        P("tp"),
        P("req", None, "tp"),
        P("req"),
        P("req"),
        P(),
        P(),
    )
    return jax.shard_map(
        per_device,
        mesh=mesh,
        in_specs=placed,
        out_specs=(P("req", "tp"), P("req", None, "tp"), P("req", None, "tp"), P()),
        check_vma=False,
    )
```

```python
import functools

import jax
import jax.numpy as jnp
from jax import lax
from jax.experimental import pallas as pl
from jax.experimental.pallas import tpu as pltpu
from jax.sharding import PartitionSpec as P

EPSILON = 1e-06
SQUARE_FLOOR = 0.25
LOG2_E = 1.4426950408889634
LANES = 128
EDGE_ROWS = 4
PLANE = 4
DIGIT = 7
VMEM_BYTES = 24 * 1024 * 1024
BLOCK = 2048
ROUND = 4
VECTOR_WEIGHT = 30000


def iota(shape, axis):
    return lax.broadcasted_iota(jnp.int32, shape, axis)


def one_hot(condition):
    return jnp.where(condition, 1.0, 0.0).astype(jnp.bfloat16)


def dot(lhs, rhs):
    return jnp.dot(lhs, rhs, preferred_element_type=jnp.float32)


def in_hbm(array):
    return pltpu.with_memory_space_constraint(array, pltpu.HBM)


def silu(value):
    return value * (0.5 + 0.5 * jnp.tanh(0.5 * value))


def to_step_major(requests, steps):
    rows = requests * steps
    row, col = iota((rows, rows), 0), iota((rows, rows), 1)
    return one_hot(col == lax.rem(row, requests) * steps + lax.div(row, requests))


def to_request_major(requests, steps):
    rows = requests * steps
    row, col = iota((rows, rows), 0), iota((rows, rows), 1)
    return one_hot(row == lax.rem(col, requests) * steps + lax.div(col, requests))


def by_request(index, scalars):
    out = jnp.zeros_like(index)
    for request, scalar in enumerate(scalars):
        out = jnp.where(index == request, scalar, out)
    return out


def conv_kernel(
    x_hbm, edge_hbm, weight_hbm, bias_hbm, proj_hbm, conv_hbm, partial_ref,
    x_ref, edge_ref, weight_ref, bias_ref, proj_ref, conv_ref, sems, out_sem,
):
    lags, requests, channels = edge_ref.shape
    taps = weight_ref.shape[0]
    steps = x_ref.shape[0] // requests
    block = min(BLOCK, channels)
    pieces = [slice(c, c + block) for c in range(0, channels, block)]
    pairs = [(weight_hbm, weight_ref), (bias_hbm, bias_ref), (edge_hbm, edge_ref)]
    pairs += [(x_hbm.at[:, piece], x_ref.at[:, piece]) for piece in pieces]
    pairs.append((proj_hbm, proj_ref))
    copies = [pltpu.make_async_copy(*pair, sems.at[i]) for i, pair in enumerate(pairs)]
    for copy in copies:
        copy.start()
    order = to_step_major(requests, steps)
    for copy in copies[:3]:
        copy.wait()
    for i, piece in enumerate(pieces):
        copies[3 + i].wait()
        stream = dot(order, x_ref[:, piece])
        window = [edge_ref[k, :, piece].astype(jnp.float32) for k in range(lags)]
        window += [stream[t * requests : (t + 1) * requests] for t in range(steps)]
        weight = [weight_ref[k : k + 1, piece] for k in range(taps)]
        outs = []
        for t in range(steps):
            added = bias_ref[:, piece] + weight[0] * window[t]
            for k in range(1, taps):
                added = added + weight[k] * window[t + k]
            outs.append(silu(added))
        conv_ref[:, piece] = jnp.concatenate(outs, axis=0).astype(jnp.bfloat16)
    result = pltpu.make_async_copy(conv_ref, conv_hbm, out_sem)
    result.start()
    copies[-1].wait()
    partial_ref[...] = lax.dot_general(
        proj_ref[...], conv_ref[...], (((1,), (1,)), ((), ())), preferred_element_type=jnp.float32
    )
    result.wait()


def conv_project(x_in, conv_edge, conv_weight, conv_bias, proj):
    rows, channels = x_in.shape
    operands = (x_in, conv_edge, conv_weight, conv_bias, proj)
    pieces = channels // min(BLOCK, channels)
    return pl.pallas_call(
        conv_kernel,
        in_specs=[pl.BlockSpec(memory_space=pl.ANY)] * len(operands),
        out_specs=[pl.BlockSpec(memory_space=pl.ANY), pl.BlockSpec(memory_space=pltpu.VMEM)],
        out_shape=[
            pltpu.HBM((rows, channels), jnp.bfloat16),
            pltpu.HBM((proj.shape[0], rows), jnp.float32),
        ],
        scratch_shapes=[pltpu.VMEM(a.shape, a.dtype) for a in operands]
        + [
            pltpu.VMEM((rows, channels), jnp.bfloat16),
            pltpu.SemaphoreType.DMA((4 + pieces,)),
            pltpu.SemaphoreType.DMA,
        ],
        compiler_params=pltpu.CompilerParams(vmem_limit_bytes=VMEM_BYTES),
        name="conv_project",
    )(*(in_hbm(a) for a in operands))


def kept_edge_kernel(
    place_ref, accepted_ref, length_ref, owner_ref, x_ref, edge_ref, _, *group_refs
):
    lags, requests, block = edge_ref.shape
    steps = x_ref.shape[0] // requests
    place = place_ref[0]
    accepted = [accepted_ref[r] for r in range(requests)]
    lengths = [length_ref[r] + accepted[r] + 1 for r in range(requests)]
    deltas = [owner_ref[place * requests + r] ^ place for r in range(requests)]
    height = len(group_refs) * PLANE * EDGE_ROWS
    slot = lax.div(iota((height, 1), 0), EDGE_ROWS)
    lag = lax.rem(iota((height, 1), 0), EDGE_ROWS)

    def pick(request, position):
        return one_hot(
            (slot == by_request(request, deltas))
            & (position - by_request(request, accepted) == lag)
            & (lag < lags)
        )

    col = iota((1, requests * steps), 1)
    picked = dot(pick(lax.div(col, steps), lax.rem(col, steps) + lags), x_ref[...])
    col = iota((1, lags * requests), 1)
    edge = jnp.concatenate([edge_ref[k].astype(jnp.float32) for k in range(lags)], axis=0)
    picked += dot(pick(lax.rem(col, requests), lax.div(col, requests)), edge.astype(jnp.bfloat16))
    low = [length & ((1 << DIGIT) - 1) for length in lengths]
    high = [length >> DIGIT for length in lengths]
    numbers = by_request(iota((1, block), 1), accepted + low + high).astype(jnp.float32)
    picked = jnp.where(lag == lags, numbers, picked).astype(jnp.bfloat16)
    group = PLANE * EDGE_ROWS
    for d, ref in enumerate(group_refs):
        ref[...] = picked[d * group : (d + 1) * group]


def kept_edges(scalars, x_in, conv_edge, after, owners):
    rows, channels = x_in.shape
    lags, requests, _ = conv_edge.shape
    block = min(2048, channels)
    groups = owners // PLANE
    return pl.pallas_call(
        kept_edge_kernel,
        grid=(channels // block,),
        in_specs=[pl.BlockSpec(memory_space=pltpu.SMEM)] * len(scalars)
        + [
            pl.BlockSpec((rows, block), lambda j: (0, j)),
            pl.BlockSpec((lags, requests, block), lambda j: (0, 0, j)),
            pl.BlockSpec(memory_space=pl.ANY),
        ],
        out_specs=[pl.BlockSpec((PLANE * EDGE_ROWS, block), lambda j: (0, j))] * groups,
        out_shape=[pltpu.HBM((PLANE * EDGE_ROWS, channels), jnp.bfloat16)] * groups,
        compiler_params=pltpu.CompilerParams(
            dimension_semantics=("arbitrary",), vmem_limit_bytes=VMEM_BYTES
        ),
        name="kept_edges",
    )(*scalars, in_hbm(x_in), in_hbm(conv_edge), in_hbm(after))


def regroup_kernel(*refs):
    groups = len(refs) - 1 - PLANE
    rows = jnp.concatenate([ref[...].astype(jnp.float32) for ref in refs[:groups]], axis=0)
    for p, out_ref in enumerate(refs[-PLANE:]):
        parts = [
            rows[(d * PLANE + p) * EDGE_ROWS : (d * PLANE + p + 1) * EDGE_ROWS] for d in range(groups)
        ]
        out_ref[...] = jnp.concatenate(parts, axis=0).astype(jnp.bfloat16)


def regroup(arrived, after):
    rows, channels = arrived[0].shape
    block = min(1024, channels)
    height = len(arrived) * EDGE_ROWS
    return pl.pallas_call(
        regroup_kernel,
        grid=(channels // block,),
        in_specs=[pl.BlockSpec((rows, block), lambda j: (0, j))] * len(arrived)
        + [pl.BlockSpec(memory_space=pl.ANY)],
        out_specs=[pl.BlockSpec((height, block), lambda j: (0, j))] * PLANE,
        out_shape=[pltpu.HBM((height, channels), jnp.bfloat16)] * PLANE,
        compiler_params=pltpu.CompilerParams(
            dimension_semantics=("arbitrary",), vmem_limit_bytes=VMEM_BYTES
        ),
        name="regroup",
    )(*arrived, in_hbm(after))


def column(row):
    count = row.shape[1]
    same = iota((count, count), 0) == iota((count, count), 1)
    return jnp.sum(jnp.where(same, row, 0.0), axis=1, keepdims=True)


def normal(values, floor_value, eps_value):
    square = jnp.mean(values * values, axis=0, keepdims=True)
    return values * lax.rsqrt(jnp.maximum(square, floor_value) + eps_value)


def low_rank(total, gain):
    low = jnp.transpose(normal(total[: gain.shape[1]], 0.0, EPSILON))
    return (low * gain).astype(jnp.bfloat16)


def state_map(values, gain):
    return (normal(values, SQUARE_FLOOR, 0.0) * column(gain)).astype(jnp.bfloat16)


def summed(part_refs):
    total = part_refs[0][...]
    for part in part_refs[1:]:
        total = total + part[...]
    return total


def softplus(raw):
    return jnp.maximum(raw, 0.0) + jnp.log1p(jnp.exp(-jnp.abs(raw)))


def kept_kernel(parts, *refs):
    place_ref, accepted_ref, owner_ref = refs[:3]
    (
        dt_gain_ref, b_gain_ref, dt_weight_ref, dt_bias_ref, state_ref, a_log_hbm, conv_hbm,
        slot_ref, part_ref, a_log_ref, conv_ref, in_ref, size_ref, drive_ref, rate_ref, new_ref,
        in_sems, sems,
    ) = refs[3 + parts :]
    pairs = ((refs[3], part_ref), (a_log_hbm, a_log_ref), (conv_hbm, conv_ref))
    copies = [pltpu.make_async_copy(*pair, in_sems.at[i]) for i, pair in enumerate(pairs)]
    for copy in copies:
        copy.start()
    rank, states = dt_gain_ref.shape[1], b_gain_ref.shape[1]
    requests = accepted_ref.shape[0]
    rows, channels = conv_ref.shape
    steps = rows // requests
    span = min(2048, channels)
    halves = states // 8

    copies[0].wait()
    total = part_ref[...]
    for part in refs[4 : 3 + parts]:
        total = total + part[...]
    turned = state_map(total[rank : rank + states], b_gain_ref[...]).astype(jnp.float32)
    for row in range(rows):
        t, r = divmod(row, requests)
        in_ref[r * states : (r + 1) * states, t * LANES : (t + 1) * LANES] = jnp.broadcast_to(
            turned[:, row : row + 1], (states, LANES)
        )

    low = low_rank(total, dt_gain_ref[...])
    row = iota((rows, 1), 0)
    live = lax.div(row, requests) < by_request(
        lax.rem(row, requests), [accepted_ref[r] for r in range(requests)]
    )
    copies[1].wait()
    copies[2].wait()
    for first in range(0, channels, span):
        piece = slice(first, first + span)
        size = softplus(dot(low, dt_weight_ref[:, piece]) + dt_bias_ref[:, piece])
        size = jnp.where(live, size, 0.0)
        drive = size * conv_ref[:, piece].astype(jnp.float32)
        for c in range(span // LANES):
            tile = slice(c * LANES, (c + 1) * LANES)
            size_ref[first // LANES + c, :rows, :] = size[:, tile]
            drive_ref[first // LANES + c, :rows, :] = drive[:, tile]
        rate_ref[:, piece] = jnp.exp(a_log_ref[:, piece]) * (-LOG2_E)

    def one_request(r, carry):
        own = pl.multiple_of(r * states, states)
        rounds = lax.div(accepted_ref[r] + (ROUND - 1), ROUND)

        def one_span(part, inner):
            tiles = [pl.multiple_of(part * span + c, LANES) for c in range(0, span, LANES)]

            def one_round(i, hidden):
                hidden = [list(h) for h in hidden]
                for u in range(ROUND):
                    t = i * ROUND + u
                    at = pl.ds(t * requests + r, 8, stride=0)
                    lanes = pl.ds(pl.multiple_of(t * LANES, LANES), LANES)
                    b = [in_ref[pl.ds(own + 8 * h, 8), lanes] for h in range(halves)]
                    for c, tile in enumerate(tiles):
                        place = part * (span // LANES) + c
                        now, drive = size_ref[place, at, :], drive_ref[place, at, :]
                        for h in range(halves):
                            rate = rate_ref[8 * h : 8 * (h + 1), pl.ds(tile, LANES)]
                            hidden[h][c] = jnp.exp2(now * rate) * hidden[h][c] + drive * b[h]
                return tuple(tuple(h) for h in hidden)

            lanes = pl.ds(pl.multiple_of(part * span, span), span)
            old = state_ref[pl.ds(own, states), lanes].astype(jnp.float32)
            start = tuple(
                tuple(
                    old[8 * h : 8 * (h + 1), c * LANES : (c + 1) * LANES] for c in range(len(tiles))
                )
                for h in range(halves)
            )
            done = lax.fori_loop(0, rounds, one_round, start)
            new = jnp.concatenate([jnp.concatenate(h, axis=1) for h in done], axis=0)
            new_ref[r, :, lanes] = new.astype(jnp.bfloat16)
            return inner

        lax.fori_loop(0, channels // span, one_span, 0)
        slot = owner_ref[place_ref[0] * requests + r]
        pltpu.make_async_copy(new_ref.at[r], slot_ref.at[slot], sems.at[r]).start()
        return carry

    lax.fori_loop(0, requests, one_request, 0)
    for r in range(requests):
        slot = owner_ref[place_ref[0] * requests + r]
        pltpu.make_async_copy(new_ref.at[r], slot_ref.at[slot], sems.at[r]).wait()


def kept_states(scalars, partials, gains, dt_weight, dt_bias, a_log, conv, state, slots):
    rows, channels = conv.shape
    states, rank = a_log.shape[0], dt_weight.shape[0]
    requests = scalars[1].shape[0]
    near = [*partials[1:], *gains, dt_weight, dt_bias, state]
    far = [in_hbm(a_log), in_hbm(conv)]
    anywhere = pl.BlockSpec(memory_space=pl.ANY)
    return pl.pallas_call(
        functools.partial(kept_kernel, len(partials)),
        in_specs=[pl.BlockSpec(memory_space=pltpu.SMEM)] * len(scalars)
        + [anywhere]
        + [pl.BlockSpec(memory_space=pltpu.VMEM)] * len(near)
        + [anywhere] * len(far),
        out_specs=anywhere,
        out_shape=pltpu.HBM((slots, states, channels), jnp.bfloat16),
        scratch_shapes=[
            pltpu.VMEM(partials[0].shape, jnp.float32),
            pltpu.VMEM(a_log.shape, jnp.float32),
            pltpu.VMEM(conv.shape, jnp.bfloat16),
            pltpu.VMEM((requests * states, rows // requests * LANES), jnp.float32),
            pltpu.VMEM((channels // LANES, rows + 8, LANES), jnp.float32),
            pltpu.VMEM((channels // LANES, rows + 8, LANES), jnp.float32),
            pltpu.VMEM((states, channels), jnp.float32),
            pltpu.VMEM((requests, states, channels), jnp.bfloat16),
            pltpu.SemaphoreType.DMA((1 + len(far),)),
            pltpu.SemaphoreType.DMA((requests,)),
        ],
        compiler_params=pltpu.CompilerParams(vmem_limit_bytes=VMEM_BYTES),
        cost_estimate=pl.CostEstimate(
            flops=VECTOR_WEIGHT * 4 * rows * states * channels,
            transcendentals=rows * states * channels,
            bytes_accessed=2 * channels * (rows + rank + states * (requests + slots)),
        ),
        name="kept_states",
    )(*scalars, in_hbm(partials[0]), *near, *far)


def scan_kernel(parts, *refs):
    (
        dt_gain_ref, b_gain_ref, c_gain_ref, dt_weight_ref, dt_bias_ref, a_log_ref, skip_ref,
        conv_ref, state_ref, z_ref, mixed_ref,
        low_ref, in_ref, out_ref, size_ref, drive_ref, rate_ref, start_ref, sum_ref,
    ) = refs[parts:]
    rank, states = dt_gain_ref.shape[1], b_gain_ref.shape[1]
    rows, block = conv_ref.shape
    requests = state_ref.shape[0] // states
    steps = rows // requests

    @pl.when(pl.program_id(0) == 0)
    def _():
        total = summed(refs[:parts])
        low_ref[...] = low_rank(total, dt_gain_ref[...])
        in_map = state_map(total[rank : rank + states], b_gain_ref[...])
        out_map = state_map(total[rank + states :], c_gain_ref[...])
        wide = states * LANES
        spread = one_hot(lax.div(iota((states, wide), 1), LANES) == iota((states, wide), 0))
        turn = (((0,), (0,)), ((), ()))
        in_ref[...] = lax.dot_general(in_map, spread, turn, preferred_element_type=jnp.float32)
        out_ref[...] = lax.dot_general(out_map, spread, turn, preferred_element_type=jnp.float32)

    conv = conv_ref[...].astype(jnp.float32)
    size = softplus(dot(low_ref[...], dt_weight_ref[...]) + dt_bias_ref[...])
    size_ref[...] = size
    drive_ref[...] = size * conv
    start_ref[...] = dot(to_step_major(requests, states), state_ref[...])
    rate = jnp.exp(a_log_ref[...]) * (-LOG2_E)
    for n in range(states):
        rate_ref[n * requests : (n + 1) * requests, :] = jnp.broadcast_to(
            rate[n : n + 1, :], (requests, block)
        )

    pair = 2 if block % (2 * LANES) == 0 else 1

    def columns(c, carry):
        spans = [pl.ds(pl.multiple_of((c * pair + i) * LANES, LANES), LANES) for i in range(pair)]
        start = tuple(
            tuple(start_ref[n * requests : (n + 1) * requests, s] for s in spans)
            for n in range(states)
        )

        def step(t, hidden):
            at = pl.ds(pl.multiple_of(t * requests, requests), requests)
            sizes = [size_ref[at, s] for s in spans]
            drives = [drive_ref[at, s] for s in spans]
            sums = [None] * pair
            new = []
            for n in range(states):
                b = in_ref[at, n * LANES : (n + 1) * LANES]
                c_map = out_ref[at, n * LANES : (n + 1) * LANES]
                own = slice(n * requests, (n + 1) * requests)
                mine = []
                for i, s in enumerate(spans):
                    h = jnp.exp2(sizes[i] * rate_ref[own, s]) * hidden[n][i] + drives[i] * b
                    term = c_map * h
                    sums[i] = term if sums[i] is None else sums[i] + term
                    mine.append(h)
                new.append(tuple(mine))
            for i, s in enumerate(spans):
                sum_ref[at, s] = sums[i]
            return tuple(new)

        lax.fori_loop(0, steps, step, start, unroll=2)
        return carry

    lax.fori_loop(0, block // (pair * LANES), columns, 0)

    gate = silu(dot(to_step_major(requests, steps), z_ref[...]))
    mixed = ((sum_ref[...] + skip_ref[...] * conv) * gate).astype(jnp.bfloat16)
    mixed_ref[...] = dot(to_request_major(requests, steps), mixed).astype(jnp.bfloat16)


def scan(partials, gains, dt_weight, dt_bias, a_log, skip, conv, state, z_gate):
    rows, channels = conv.shape
    states, rank = a_log.shape[0], dt_weight.shape[0]
    block = min(512, channels)

    def whole(array):
        return pl.BlockSpec(array.shape, lambda j: (0, 0))

    wide = [in_hbm(dt_weight), dt_bias, in_hbm(a_log), skip, in_hbm(conv), in_hbm(state), in_hbm(z_gate)]
    tall = pltpu.VMEM((rows, block), jnp.float32)
    table = pltpu.VMEM((rows, states * LANES), jnp.float32)
    return pl.pallas_call(
        functools.partial(scan_kernel, len(partials)),
        grid=(channels // block,),
        in_specs=[whole(a) for a in (*partials, *gains)]
        + [pl.BlockSpec((a.shape[0], block), lambda j: (0, j)) for a in wide],
        out_specs=pl.BlockSpec((rows, block), lambda j: (0, j)),
        out_shape=jax.ShapeDtypeStruct((rows, channels), jnp.bfloat16),
        scratch_shapes=[
            pltpu.VMEM((rows, rank), jnp.bfloat16), table, table, tall, tall,
            pltpu.VMEM((state.shape[0], block), jnp.float32),
            pltpu.VMEM((state.shape[0], block), jnp.float32),
            tall,
        ],
        compiler_params=pltpu.CompilerParams(
            dimension_semantics=("arbitrary",), vmem_limit_bytes=VMEM_BYTES
        ),
        cost_estimate=pl.CostEstimate(
            flops=VECTOR_WEIGHT * 8 * rows * states * channels,
            transcendentals=rows * states * channels,
            bytes_accessed=2 * channels * (3 * rows + rank),
        ),
        name="scan",
    )(*partials, *gains, *wide)


def edge_kernel(steps, requests, place_ref, source_ref, range_ref, *refs):
    group_refs, edge_ref, stats_ref = refs[:-2], refs[-2], refs[-1]
    own_most, lags, block = edge_ref.shape
    groups = group_refs[0].shape[0] // EDGE_ROWS
    height = len(group_refs) * groups * EDGE_ROWS
    place = place_ref[0]

    def sender(index):
        p, d = lax.div(index, groups * EDGE_ROWS), lax.rem(lax.div(index, EDGE_ROWS), groups)
        return (d * PLANE + p) ^ place

    got = jnp.concatenate([ref[...] for ref in group_refs], axis=0)
    row, col = iota((own_most * 8, 1), 0), iota((1, height), 1)
    wanted = jnp.full((own_most * 8, 1), -1, jnp.int32)
    for i in range(own_most):
        wanted = jnp.where(lax.div(row, 8) == i, source_ref[i], wanted)
    pick = (sender(col) == wanted) & (lax.rem(col, EDGE_ROWS) == lax.rem(row, 8))
    picked = dot(one_hot(pick), got)
    for i in range(own_most):
        edge_ref[i] = picked[i * 8 : i * 8 + lags].astype(jnp.bfloat16)

    @pl.when(pl.program_id(0) == 0)
    def _():
        numbers = got[:, :LANES].astype(jnp.float32)
        row, lane = iota((height, LANES), 0), iota((height, LANES), 1)
        mine = lax.rem(row, EDGE_ROWS) == lags
        request = sender(row) * requests + lax.rem(lane, requests)
        digit = lax.div(lane, requests)
        counts = jnp.where(digit == 0, numbers, 0.0)
        lengths = jnp.where(digit == 1, numbers, 0.0) + jnp.where(
            digit == 2, numbers * float(1 << DIGIT), 0.0
        )
        tenants = range_ref.shape[0]
        sums, loads, members = [], [], []
        for k in range(tenants):
            start, end = range_ref[k, 0], range_ref[k, 1]
            inside = mine & (request >= start) & (request < end)
            sums.append(jnp.sum(jnp.where(inside, counts, 0.0), keepdims=True))
            loads.append(jnp.sum(jnp.where(inside, lengths, 0.0), keepdims=True))
            members.append((jnp.zeros((1, 1), jnp.int32) + (end - start)).astype(jnp.float32))
        mean = sum(loads[1:], loads[0]) / sum(members[1:], members[0])
        out = jnp.zeros((tenants, 2), jnp.float32)
        row, col = iota((tenants, 2), 0), iota((tenants, 2), 1)
        for k in range(tenants):
            rate = sums[k] / (float(steps) * members[k])
            load = loads[k] / members[k] / mean
            out = jnp.where(row == k, jnp.where(col == 0, rate, load), out)
        stats_ref[...] = out


def settle_edges(place, source, tenant_range, got, own_most, lags, steps, requests):
    smem = pl.BlockSpec(memory_space=pltpu.SMEM)
    height, channels = got[0].shape
    block = min(2048, channels)
    stats = (tenant_range.shape[0], 2)
    return pl.pallas_call(
        functools.partial(edge_kernel, steps, requests),
        grid=(channels // block,),
        in_specs=[smem] * 3 + [pl.BlockSpec((height, block), lambda j: (0, j))] * len(got),
        out_specs=[
            pl.BlockSpec((own_most, lags, block), lambda j: (0, 0, j)),
            pl.BlockSpec(stats, lambda j: (0, 0)),
        ],
        out_shape=[
            jax.ShapeDtypeStruct((own_most, lags, channels), jnp.bfloat16),
            jax.ShapeDtypeStruct(stats, jnp.float32),
        ],
        compiler_params=pltpu.CompilerParams(
            dimension_semantics=("arbitrary",), vmem_limit_bytes=VMEM_BYTES
        ),
        name="settle_edges",
    )(place, source, tenant_range, *got)


def settle_kernel(source_ref, got_hbm, owned_hbm, rows_ref, in_sem, sems):
    slots = got_hbm.shape[0]
    fetch = pltpu.make_async_copy(got_hbm, rows_ref.at[:slots], in_sem)
    fetch.start()
    rows_ref[slots] = jnp.zeros(rows_ref.shape[1:], rows_ref.dtype)
    fetch.wait()
    puts = [
        pltpu.make_async_copy(rows_ref.at[source_ref[i]], owned_hbm.at[i], sems.at[i])
        for i in range(owned_hbm.shape[0])
    ]
    for put in puts:
        put.start()
    for put in puts:
        put.wait()


def settle_states(source, got, own_most):
    anywhere = pl.BlockSpec(memory_space=pl.ANY)
    slots, *rest = got.shape
    return pl.pallas_call(
        settle_kernel,
        in_specs=[pl.BlockSpec(memory_space=pltpu.SMEM), anywhere],
        out_specs=anywhere,
        out_shape=pltpu.HBM((own_most, *rest), got.dtype),
        scratch_shapes=[
            pltpu.VMEM((slots + 1, *rest), got.dtype),
            pltpu.SemaphoreType.DMA,
            pltpu.SemaphoreType.DMA((own_most,)),
        ],
        compiler_params=pltpu.CompilerParams(vmem_limit_bytes=VMEM_BYTES),
        name="settle_states",
    )(source, in_hbm(got))


def per_device(
    x_in, z_gate, conv_edge, conv_weight, conv_bias, x_proj_weight, dt_gain, b_gain, c_gain,
    dt_proj_weight, dt_bias, a_log, skip, ssm_state, accepted, prompt_len, tenant_range, owner,
):
    requests, states, channels = ssm_state.shape
    lags = conv_edge.shape[1]
    owners = lax.axis_size("req")
    own_most = min(requests + requests // 2, owners)
    place = lax.axis_index("req").astype(jnp.int32).reshape(1)

    by_lag = jnp.transpose(conv_edge, (1, 0, 2))
    conv, partial = conv_project(
        x_in, by_lag, conv_weight, conv_bias.reshape(1, -1), x_proj_weight.T
    )
    if lax.axis_size("tp") == 2:
        partials = (partial, lax.ppermute(partial, "tp", [(0, 1), (1, 0)]))
    else:
        partials = (lax.psum(partial, "tp"),)

    def swap(rows, delta):
        return lax.ppermute(rows, "req", [(i, i ^ delta) for i in range(owners)]) if delta else rows

    groups = kept_edges((place, accepted, prompt_len, owner), x_in, by_lag, partial, owners)
    groups = [swap(rows, d * PLANE) for d, rows in enumerate(groups)]

    hits = jnp.any(owner.reshape(owners, requests) == place, axis=1)
    ids = jnp.arange(owners, dtype=jnp.int32)
    ranks = jnp.sum((hits[None, :] & (ids[None, :] < ids[:, None])).astype(jnp.int32), axis=1)
    at = hits[None, :] & (ranks[None, :] == jnp.arange(own_most, dtype=jnp.int32)[:, None])
    source = owners - jnp.sum(jnp.where(at, owners - ids[None, :], 0), axis=1)

    gains = (dt_gain.reshape(1, -1), b_gain.reshape(1, -1), c_gain.reshape(1, -1))
    bias = dt_bias.reshape(1, -1)
    state = ssm_state.reshape(requests * states, channels)
    slots = kept_states(
        (place, accepted, owner), partials, gains[:2], dt_proj_weight, bias, a_log, conv, state, owners
    )
    got = lax.all_to_all(slots, "req", split_axis=0, concat_axis=0, tiled=True)
    mixed = scan(
        partials, gains, dt_proj_weight, bias, a_log, skip.reshape(1, -1), conv, state, z_gate
    )
    groups = [swap(rows, p) for p, rows in enumerate(regroup(groups, mixed))]
    owned_edge, tenant_stats = settle_edges(
        place, source, tenant_range, groups, own_most, lags, x_in.shape[0] // requests,
        requests,
    )
    owned = settle_states(source, got, own_most)
    return (mixed, owned, owned_edge, tenant_stats)


def solution(mesh):
    placed = (
        P("req", "tp"),
        P("req", "tp"),
        P("req", None, "tp"),
        P(None, "tp"),
        P("tp"),
        P("tp", None),
        P(),
        P(),
        P(),
        P(None, "tp"),
        P("tp"),
        P(None, "tp"),
        P("tp"),
        P("req", None, "tp"),
        P("req"),
        P("req"),
        P(),
        P(),
    )
    return jax.shard_map(
        per_device,
        mesh=mesh,
        in_specs=placed,
        out_specs=(P("req", "tp"), P("req", None, "tp"), P("req", None, "tp"), P()),
        check_vma=False,
    )
```

```python
import functools

import jax
import jax.numpy as jnp
from jax import lax
from jax.experimental import pallas as pl
from jax.experimental.pallas import tpu as pltpu
from jax.sharding import PartitionSpec as P

EPSILON = 1e-06
SQUARE_FLOOR = 0.25
LOG2_E = 1.4426950408889634
LANES = 128
EDGE_ROWS = 4
PLANE = 4
DIGIT = 7
VMEM_BYTES = 24 * 1024 * 1024
BLOCK = 2048
ROUND = 4
VECTOR_WEIGHT = 30000


def iota(shape, axis):
    return lax.broadcasted_iota(jnp.int32, shape, axis)


def one_hot(condition):
    return jnp.where(condition, 1.0, 0.0).astype(jnp.bfloat16)


def dot(lhs, rhs):
    return jnp.dot(lhs, rhs, preferred_element_type=jnp.float32)


def in_hbm(array):
    return pltpu.with_memory_space_constraint(array, pltpu.HBM)


def silu(value):
    return value * (0.5 + 0.5 * jnp.tanh(0.5 * value))


def to_step_major(requests, steps):
    rows = requests * steps
    row, col = iota((rows, rows), 0), iota((rows, rows), 1)
    return one_hot(col == lax.rem(row, requests) * steps + lax.div(row, requests))


def to_request_major(requests, steps):
    rows = requests * steps
    row, col = iota((rows, rows), 0), iota((rows, rows), 1)
    return one_hot(row == lax.rem(col, requests) * steps + lax.div(col, requests))


def by_request(index, scalars):
    out = jnp.zeros_like(index)
    for request, scalar in enumerate(scalars):
        out = jnp.where(index == request, scalar, out)
    return out


def conv_kernel(
    x_hbm, edge_hbm, weight_hbm, bias_hbm, proj_hbm, conv_hbm, partial_ref,
    x_ref, edge_ref, weight_ref, bias_ref, proj_ref, conv_ref, sems, out_sem,
):
    lags, requests, channels = edge_ref.shape
    taps = weight_ref.shape[0]
    steps = x_ref.shape[0] // requests
    block = min(BLOCK, channels)
    pieces = [slice(c, c + block) for c in range(0, channels, block)]
    pairs = [(weight_hbm, weight_ref), (bias_hbm, bias_ref), (edge_hbm, edge_ref)]
    pairs += [(x_hbm.at[:, piece], x_ref.at[:, piece]) for piece in pieces]
    pairs.append((proj_hbm, proj_ref))
    copies = [pltpu.make_async_copy(*pair, sems.at[i]) for i, pair in enumerate(pairs)]
    for copy in copies:
        copy.start()
    order = to_step_major(requests, steps)
    for copy in copies[:3]:
        copy.wait()
    for i, piece in enumerate(pieces):
        copies[3 + i].wait()
        stream = dot(order, x_ref[:, piece])
        window = [edge_ref[k, :, piece].astype(jnp.float32) for k in range(lags)]
        window += [stream[t * requests : (t + 1) * requests] for t in range(steps)]
        weight = [weight_ref[k : k + 1, piece] for k in range(taps)]
        outs = []
        for t in range(steps):
            added = bias_ref[:, piece] + weight[0] * window[t]
            for k in range(1, taps):
                added = added + weight[k] * window[t + k]
            outs.append(silu(added))
        conv_ref[:, piece] = jnp.concatenate(outs, axis=0).astype(jnp.bfloat16)
    result = pltpu.make_async_copy(conv_ref, conv_hbm, out_sem)
    result.start()
    copies[-1].wait()
    partial_ref[...] = lax.dot_general(
        proj_ref[...], conv_ref[...], (((1,), (1,)), ((), ())), preferred_element_type=jnp.float32
    )
    result.wait()


def conv_project(x_in, conv_edge, conv_weight, conv_bias, proj):
    rows, channels = x_in.shape
    operands = (x_in, conv_edge, conv_weight, conv_bias, proj)
    pieces = channels // min(BLOCK, channels)
    return pl.pallas_call(
        conv_kernel,
        in_specs=[pl.BlockSpec(memory_space=pl.ANY)] * len(operands),
        out_specs=[pl.BlockSpec(memory_space=pl.ANY), pl.BlockSpec(memory_space=pltpu.VMEM)],
        out_shape=[
            pltpu.HBM((rows, channels), jnp.bfloat16),
            pltpu.HBM((proj.shape[0], rows), jnp.float32),
        ],
        scratch_shapes=[pltpu.VMEM(a.shape, a.dtype) for a in operands]
        + [
            pltpu.VMEM((rows, channels), jnp.bfloat16),
            pltpu.SemaphoreType.DMA((4 + pieces,)),
            pltpu.SemaphoreType.DMA,
        ],
        compiler_params=pltpu.CompilerParams(vmem_limit_bytes=VMEM_BYTES),
        name="conv_project",
    )(*(in_hbm(a) for a in operands))


def kept_edge_kernel(
    place_ref, accepted_ref, length_ref, owner_ref, x_ref, edge_ref, _, *group_refs
):
    lags, requests, block = edge_ref.shape
    steps = x_ref.shape[0] // requests
    place = place_ref[0]
    accepted = [accepted_ref[r] for r in range(requests)]
    lengths = [length_ref[r] + accepted[r] + 1 for r in range(requests)]
    deltas = [owner_ref[place * requests + r] ^ place for r in range(requests)]
    height = len(group_refs) * PLANE * EDGE_ROWS
    slot = lax.div(iota((height, 1), 0), EDGE_ROWS)
    lag = lax.rem(iota((height, 1), 0), EDGE_ROWS)

    def pick(request, position):
        return one_hot(
            (slot == by_request(request, deltas))
            & (position - by_request(request, accepted) == lag)
            & (lag < lags)
        )

    col = iota((1, requests * steps), 1)
    picked = dot(pick(lax.div(col, steps), lax.rem(col, steps) + lags), x_ref[...])
    col = iota((1, lags * requests), 1)
    edge = jnp.concatenate([edge_ref[k].astype(jnp.float32) for k in range(lags)], axis=0)
    picked += dot(pick(lax.rem(col, requests), lax.div(col, requests)), edge.astype(jnp.bfloat16))
    low = [length & ((1 << DIGIT) - 1) for length in lengths]
    high = [length >> DIGIT for length in lengths]
    numbers = by_request(iota((1, block), 1), accepted + low + high).astype(jnp.float32)
    picked = jnp.where(lag == lags, numbers, picked).astype(jnp.bfloat16)
    group = PLANE * EDGE_ROWS
    for d, ref in enumerate(group_refs):
        ref[...] = picked[d * group : (d + 1) * group]


def kept_edges(scalars, x_in, conv_edge, after, owners):
    channels = x_in.shape[1]
    groups = owners // PLANE
    vmem = pl.BlockSpec(memory_space=pltpu.VMEM)
    return pl.pallas_call(
        kept_edge_kernel,
        in_specs=[pl.BlockSpec(memory_space=pltpu.SMEM)] * len(scalars)
        + [vmem, vmem, pl.BlockSpec(memory_space=pl.ANY)],
        out_specs=[vmem] * groups,
        out_shape=[pltpu.HBM((PLANE * EDGE_ROWS, channels), jnp.bfloat16)] * groups,
        compiler_params=pltpu.CompilerParams(vmem_limit_bytes=VMEM_BYTES),
        name="kept_edges",
    )(*scalars, x_in, conv_edge, in_hbm(after))


def regroup_kernel(*refs):
    groups = len(refs) - 1 - PLANE
    rows = jnp.concatenate([ref[...].astype(jnp.float32) for ref in refs[:groups]], axis=0)
    for p, out_ref in enumerate(refs[-PLANE:]):
        parts = [
            rows[(d * PLANE + p) * EDGE_ROWS : (d * PLANE + p + 1) * EDGE_ROWS] for d in range(groups)
        ]
        out_ref[...] = jnp.concatenate(parts, axis=0).astype(jnp.bfloat16)


def regroup(arrived, after):
    rows, channels = arrived[0].shape
    block = min(1024, channels)
    height = len(arrived) * EDGE_ROWS
    return pl.pallas_call(
        regroup_kernel,
        grid=(channels // block,),
        in_specs=[pl.BlockSpec((rows, block), lambda j: (0, j))] * len(arrived)
        + [pl.BlockSpec(memory_space=pl.ANY)],
        out_specs=[pl.BlockSpec((height, block), lambda j: (0, j))] * PLANE,
        out_shape=[pltpu.HBM((height, channels), jnp.bfloat16)] * PLANE,
        compiler_params=pltpu.CompilerParams(
            dimension_semantics=("arbitrary",), vmem_limit_bytes=VMEM_BYTES
        ),
        name="regroup",
    )(*arrived, in_hbm(after))


def column(row):
    count = row.shape[1]
    same = iota((count, count), 0) == iota((count, count), 1)
    return jnp.sum(jnp.where(same, row, 0.0), axis=1, keepdims=True)


def normal(values, floor_value, eps_value):
    square = jnp.mean(values * values, axis=0, keepdims=True)
    return values * lax.rsqrt(jnp.maximum(square, floor_value) + eps_value)


def low_rank(total, gain):
    low = jnp.transpose(normal(total[: gain.shape[1]], 0.0, EPSILON))
    return (low * gain).astype(jnp.bfloat16)


def state_map(values, gain):
    return (normal(values, SQUARE_FLOOR, 0.0) * column(gain)).astype(jnp.bfloat16)


def summed(part_refs):
    total = part_refs[0][...]
    for part in part_refs[1:]:
        total = total + part[...]
    return total


def softplus(raw):
    return jnp.maximum(raw, 0.0) + jnp.log1p(jnp.exp(-jnp.abs(raw)))


def kept_kernel(parts, *refs):
    place_ref, accepted_ref, owner_ref = refs[:3]
    (
        dt_gain_ref, b_gain_ref, dt_weight_ref, dt_bias_ref, a_log_hbm, conv_hbm, state_hbm,
        slot_ref, part_ref, a_log_ref, conv_ref, state_ref, in_ref, size_ref, drive_ref, rate_ref, new_ref,
        in_sems, sems,
    ) = refs[3 + parts :]
    pairs = ((refs[3], part_ref), (a_log_hbm, a_log_ref), (conv_hbm, conv_ref), (state_hbm, state_ref))
    copies = [pltpu.make_async_copy(*pair, in_sems.at[i]) for i, pair in enumerate(pairs)]
    for copy in copies:
        copy.start()
    rank, states = dt_gain_ref.shape[1], b_gain_ref.shape[1]
    requests = accepted_ref.shape[0]
    rows, channels = conv_ref.shape
    steps = rows // requests
    span = min(2048, channels)
    halves = states // 8

    copies[0].wait()
    total = part_ref[...]
    for part in refs[4 : 3 + parts]:
        total = total + part[...]
    turned = state_map(total[rank : rank + states], b_gain_ref[...]).astype(jnp.float32)
    for row in range(rows):
        t, r = divmod(row, requests)
        in_ref[r * states : (r + 1) * states, t * LANES : (t + 1) * LANES] = jnp.broadcast_to(
            turned[:, row : row + 1], (states, LANES)
        )

    low = low_rank(total, dt_gain_ref[...])
    row = iota((rows, 1), 0)
    live = lax.div(row, requests) < by_request(
        lax.rem(row, requests), [accepted_ref[r] for r in range(requests)]
    )
    copies[1].wait()
    copies[2].wait()
    for first in range(0, channels, span):
        piece = slice(first, first + span)
        size = softplus(dot(low, dt_weight_ref[:, piece]) + dt_bias_ref[:, piece])
        size = jnp.where(live, size, 0.0)
        drive = size * conv_ref[:, piece].astype(jnp.float32)
        for c in range(span // LANES):
            tile = slice(c * LANES, (c + 1) * LANES)
            size_ref[first // LANES + c, :rows, :] = size[:, tile]
            drive_ref[first // LANES + c, :rows, :] = drive[:, tile]
        rate_ref[:, piece] = jnp.exp(a_log_ref[:, piece]) * (-LOG2_E)

    def one_request(r, carry):
        own = pl.multiple_of(r * states, states)
        rounds = lax.div(accepted_ref[r] + (ROUND - 1), ROUND)

        def one_span(part, inner):
            tiles = [pl.multiple_of(part * span + c, LANES) for c in range(0, span, LANES)]

            rates = [
                [rate_ref[8 * h : 8 * (h + 1), pl.ds(tile, LANES)] for tile in tiles]
                for h in range(halves)
            ]

            def one_round(i, hidden):
                hidden = [list(h) for h in hidden]
                for u in range(ROUND):
                    t = i * ROUND + u
                    at = pl.ds(t * requests + r, 8, stride=0)
                    lanes = pl.ds(pl.multiple_of(t * LANES, LANES), LANES)
                    b = [in_ref[pl.ds(own + 8 * h, 8), lanes] for h in range(halves)]
                    for c, tile in enumerate(tiles):
                        place = part * (span // LANES) + c
                        now, drive = size_ref[place, at, :], drive_ref[place, at, :]
                        for h in range(halves):
                            decay = jnp.exp2(now * rates[h][c])
                            hidden[h][c] = decay * hidden[h][c] + drive * b[h]
                return tuple(tuple(h) for h in hidden)

            lanes = pl.ds(pl.multiple_of(part * span, span), span)
            old = state_ref[pl.ds(own, states), lanes].astype(jnp.float32)
            start = tuple(
                tuple(
                    old[8 * h : 8 * (h + 1), c * LANES : (c + 1) * LANES] for c in range(len(tiles))
                )
                for h in range(halves)
            )
            done = lax.fori_loop(0, rounds, one_round, start)
            new = jnp.concatenate([jnp.concatenate(h, axis=1) for h in done], axis=0)
            new_ref[r, :, lanes] = new.astype(jnp.bfloat16)
            return inner

        lax.fori_loop(0, channels // span, one_span, 0)
        slot = owner_ref[place_ref[0] * requests + r]
        pltpu.make_async_copy(new_ref.at[r], slot_ref.at[slot], sems.at[r]).start()
        return carry

    copies[3].wait()
    lax.fori_loop(0, requests, one_request, 0)
    for r in range(requests):
        slot = owner_ref[place_ref[0] * requests + r]
        pltpu.make_async_copy(new_ref.at[r], slot_ref.at[slot], sems.at[r]).wait()


def kept_states(scalars, partials, gains, dt_weight, dt_bias, a_log, conv, state, slots):
    rows, channels = conv.shape
    states, rank = a_log.shape[0], dt_weight.shape[0]
    requests = scalars[1].shape[0]
    near = [*partials[1:], *gains, dt_weight, dt_bias]
    far = [in_hbm(a_log), in_hbm(conv), in_hbm(state)]
    anywhere = pl.BlockSpec(memory_space=pl.ANY)
    return pl.pallas_call(
        functools.partial(kept_kernel, len(partials)),
        in_specs=[pl.BlockSpec(memory_space=pltpu.SMEM)] * len(scalars)
        + [anywhere]
        + [pl.BlockSpec(memory_space=pltpu.VMEM)] * len(near)
        + [anywhere] * len(far),
        out_specs=anywhere,
        out_shape=pltpu.HBM((slots, states, channels), jnp.bfloat16),
        scratch_shapes=[
            pltpu.VMEM(partials[0].shape, jnp.float32),
            pltpu.VMEM(a_log.shape, jnp.float32),
            pltpu.VMEM(conv.shape, jnp.bfloat16),
            pltpu.VMEM(state.shape, jnp.bfloat16),
            pltpu.VMEM((requests * states, rows // requests * LANES), jnp.float32),
            pltpu.VMEM((channels // LANES, rows + 8, LANES), jnp.float32),
            pltpu.VMEM((channels // LANES, rows + 8, LANES), jnp.float32),
            pltpu.VMEM((states, channels), jnp.float32),
            pltpu.VMEM((requests, states, channels), jnp.bfloat16),
            pltpu.SemaphoreType.DMA((1 + len(far),)),
            pltpu.SemaphoreType.DMA((requests,)),
        ],
        compiler_params=pltpu.CompilerParams(vmem_limit_bytes=VMEM_BYTES),
        cost_estimate=pl.CostEstimate(
            flops=VECTOR_WEIGHT * 4 * rows * states * channels,
            transcendentals=rows * states * channels,
            bytes_accessed=2 * channels * (rows + rank + states * (requests + slots)),
        ),
        name="kept_states",
    )(*scalars, in_hbm(partials[0]), *near, *far)


def scan_kernel(parts, *refs):
    (
        dt_gain_ref, b_gain_ref, c_gain_ref, dt_weight_ref, dt_bias_ref, a_log_ref, skip_ref,
        conv_ref, state_ref, z_ref, mixed_ref,
        low_ref, in_ref, out_ref, size_ref, drive_ref, rate_ref, start_ref, sum_ref,
    ) = refs[parts:]
    rank, states = dt_gain_ref.shape[1], b_gain_ref.shape[1]
    rows, block = conv_ref.shape
    requests = state_ref.shape[0] // states
    steps = rows // requests

    @pl.when(pl.program_id(0) == 0)
    def _():
        total = summed(refs[:parts])
        low_ref[...] = low_rank(total, dt_gain_ref[...])
        in_map = state_map(total[rank : rank + states], b_gain_ref[...])
        out_map = state_map(total[rank + states :], c_gain_ref[...])
        wide = states * LANES
        spread = one_hot(lax.div(iota((states, wide), 1), LANES) == iota((states, wide), 0))
        turn = (((0,), (0,)), ((), ()))
        in_ref[...] = lax.dot_general(in_map, spread, turn, preferred_element_type=jnp.float32)
        out_ref[...] = lax.dot_general(out_map, spread, turn, preferred_element_type=jnp.float32)

    conv = conv_ref[...].astype(jnp.float32)
    size = softplus(dot(low_ref[...], dt_weight_ref[...]) + dt_bias_ref[...])
    size_ref[...] = size
    drive_ref[...] = size * conv
    start_ref[...] = dot(to_step_major(requests, states), state_ref[...])
    rate = jnp.exp(a_log_ref[...]) * (-LOG2_E)
    for n in range(states):
        rate_ref[n * requests : (n + 1) * requests, :] = jnp.broadcast_to(
            rate[n : n + 1, :], (requests, block)
        )

    pair = 2 if block % (2 * LANES) == 0 else 1

    def columns(c, carry):
        spans = [pl.ds(pl.multiple_of((c * pair + i) * LANES, LANES), LANES) for i in range(pair)]
        start = tuple(
            tuple(start_ref[n * requests : (n + 1) * requests, s] for s in spans)
            for n in range(states)
        )

        def step(t, hidden):
            at = pl.ds(pl.multiple_of(t * requests, requests), requests)
            sizes = [size_ref[at, s] for s in spans]
            drives = [drive_ref[at, s] for s in spans]
            sums = [None] * pair
            new = []
            for n in range(states):
                b = in_ref[at, n * LANES : (n + 1) * LANES]
                c_map = out_ref[at, n * LANES : (n + 1) * LANES]
                own = slice(n * requests, (n + 1) * requests)
                mine = []
                for i, s in enumerate(spans):
                    h = jnp.exp2(sizes[i] * rate_ref[own, s]) * hidden[n][i] + drives[i] * b
                    term = c_map * h
                    sums[i] = term if sums[i] is None else sums[i] + term
                    mine.append(h)
                new.append(tuple(mine))
            for i, s in enumerate(spans):
                sum_ref[at, s] = sums[i]
            return tuple(new)

        lax.fori_loop(0, steps, step, start, unroll=2)
        return carry

    lax.fori_loop(0, block // (pair * LANES), columns, 0)

    gate = silu(dot(to_step_major(requests, steps), z_ref[...]))
    mixed = ((sum_ref[...] + skip_ref[...] * conv) * gate).astype(jnp.bfloat16)
    mixed_ref[...] = dot(to_request_major(requests, steps), mixed).astype(jnp.bfloat16)


def scan(partials, gains, dt_weight, dt_bias, a_log, skip, conv, state, z_gate):
    rows, channels = conv.shape
    states, rank = a_log.shape[0], dt_weight.shape[0]
    block = min(512, channels)

    def whole(array):
        return pl.BlockSpec(array.shape, lambda j: (0, 0))

    wide = [in_hbm(dt_weight), dt_bias, in_hbm(a_log), skip, in_hbm(conv), in_hbm(state), in_hbm(z_gate)]
    tall = pltpu.VMEM((rows, block), jnp.float32)
    table = pltpu.VMEM((rows, states * LANES), jnp.float32)
    return pl.pallas_call(
        functools.partial(scan_kernel, len(partials)),
        grid=(channels // block,),
        in_specs=[whole(a) for a in (*partials, *gains)]
        + [pl.BlockSpec((a.shape[0], block), lambda j: (0, j)) for a in wide],
        out_specs=pl.BlockSpec((rows, block), lambda j: (0, j)),
        out_shape=jax.ShapeDtypeStruct((rows, channels), jnp.bfloat16),
        scratch_shapes=[
            pltpu.VMEM((rows, rank), jnp.bfloat16), table, table, tall, tall,
            pltpu.VMEM((state.shape[0], block), jnp.float32),
            pltpu.VMEM((state.shape[0], block), jnp.float32),
            tall,
        ],
        compiler_params=pltpu.CompilerParams(
            dimension_semantics=("arbitrary",), vmem_limit_bytes=VMEM_BYTES
        ),
        cost_estimate=pl.CostEstimate(
            flops=VECTOR_WEIGHT * 8 * rows * states * channels,
            transcendentals=rows * states * channels,
            bytes_accessed=2 * channels * (3 * rows + rank),
        ),
        name="scan",
    )(*partials, *gains, *wide)


def edge_kernel(steps, requests, place_ref, source_ref, range_ref, *refs):
    group_refs, edge_ref, stats_ref = refs[:-2], refs[-2], refs[-1]
    own_most, lags, block = edge_ref.shape
    groups = group_refs[0].shape[0] // EDGE_ROWS
    height = len(group_refs) * groups * EDGE_ROWS
    place = place_ref[0]

    def sender(index):
        p, d = lax.div(index, groups * EDGE_ROWS), lax.rem(lax.div(index, EDGE_ROWS), groups)
        return (d * PLANE + p) ^ place

    got = jnp.concatenate([ref[...] for ref in group_refs], axis=0)
    row, col = iota((own_most * 8, 1), 0), iota((1, height), 1)
    wanted = jnp.full((own_most * 8, 1), -1, jnp.int32)
    for i in range(own_most):
        wanted = jnp.where(lax.div(row, 8) == i, source_ref[i], wanted)
    pick = (sender(col) == wanted) & (lax.rem(col, EDGE_ROWS) == lax.rem(row, 8))
    picked = dot(one_hot(pick), got)
    for i in range(own_most):
        edge_ref[i] = picked[i * 8 : i * 8 + lags].astype(jnp.bfloat16)

    @pl.when(pl.program_id(0) == 0)
    def _():
        numbers = got[:, :LANES].astype(jnp.float32)
        row, lane = iota((height, LANES), 0), iota((height, LANES), 1)
        mine = lax.rem(row, EDGE_ROWS) == lags
        request = sender(row) * requests + lax.rem(lane, requests)
        digit = lax.div(lane, requests)
        counts = jnp.where(digit == 0, numbers, 0.0)
        lengths = jnp.where(digit == 1, numbers, 0.0) + jnp.where(
            digit == 2, numbers * float(1 << DIGIT), 0.0
        )
        tenants = range_ref.shape[0]
        sums, loads, members = [], [], []
        for k in range(tenants):
            start, end = range_ref[k, 0], range_ref[k, 1]
            inside = mine & (request >= start) & (request < end)
            sums.append(jnp.sum(jnp.where(inside, counts, 0.0), keepdims=True))
            loads.append(jnp.sum(jnp.where(inside, lengths, 0.0), keepdims=True))
            members.append((jnp.zeros((1, 1), jnp.int32) + (end - start)).astype(jnp.float32))
        mean = sum(loads[1:], loads[0]) / sum(members[1:], members[0])
        out = jnp.zeros((tenants, 2), jnp.float32)
        row, col = iota((tenants, 2), 0), iota((tenants, 2), 1)
        for k in range(tenants):
            rate = sums[k] / (float(steps) * members[k])
            load = loads[k] / members[k] / mean
            out = jnp.where(row == k, jnp.where(col == 0, rate, load), out)
        stats_ref[...] = out


def settle_edges(place, source, tenant_range, got, own_most, lags, steps, requests):
    smem = pl.BlockSpec(memory_space=pltpu.SMEM)
    height, channels = got[0].shape
    block = min(2048, channels)
    stats = (tenant_range.shape[0], 2)
    return pl.pallas_call(
        functools.partial(edge_kernel, steps, requests),
        grid=(channels // block,),
        in_specs=[smem] * 3 + [pl.BlockSpec((height, block), lambda j: (0, j))] * len(got),
        out_specs=[
            pl.BlockSpec((own_most, lags, block), lambda j: (0, 0, j)),
            pl.BlockSpec(stats, lambda j: (0, 0)),
        ],
        out_shape=[
            jax.ShapeDtypeStruct((own_most, lags, channels), jnp.bfloat16),
            jax.ShapeDtypeStruct(stats, jnp.float32),
        ],
        compiler_params=pltpu.CompilerParams(
            dimension_semantics=("arbitrary",), vmem_limit_bytes=VMEM_BYTES
        ),
        name="settle_edges",
    )(place, source, tenant_range, *got)


def settle_kernel(source_ref, got_hbm, owned_hbm, rows_ref, in_sem, sems):
    slots = got_hbm.shape[0]
    fetch = pltpu.make_async_copy(got_hbm, rows_ref.at[:slots], in_sem)
    fetch.start()
    rows_ref[slots] = jnp.zeros(rows_ref.shape[1:], rows_ref.dtype)
    fetch.wait()
    puts = [
        pltpu.make_async_copy(rows_ref.at[source_ref[i]], owned_hbm.at[i], sems.at[i])
        for i in range(owned_hbm.shape[0])
    ]
    for put in puts:
        put.start()
    for put in puts:
        put.wait()


def settle_states(source, got, own_most):
    anywhere = pl.BlockSpec(memory_space=pl.ANY)
    slots, *rest = got.shape
    return pl.pallas_call(
        settle_kernel,
        in_specs=[pl.BlockSpec(memory_space=pltpu.SMEM), anywhere],
        out_specs=anywhere,
        out_shape=pltpu.HBM((own_most, *rest), got.dtype),
        scratch_shapes=[
            pltpu.VMEM((slots + 1, *rest), got.dtype),
            pltpu.SemaphoreType.DMA,
            pltpu.SemaphoreType.DMA((own_most,)),
        ],
        compiler_params=pltpu.CompilerParams(vmem_limit_bytes=VMEM_BYTES),
        name="settle_states",
    )(source, in_hbm(got))


def per_device(
    x_in, z_gate, conv_edge, conv_weight, conv_bias, x_proj_weight, dt_gain, b_gain, c_gain,
    dt_proj_weight, dt_bias, a_log, skip, ssm_state, accepted, prompt_len, tenant_range, owner,
):
    requests, states, channels = ssm_state.shape
    lags = conv_edge.shape[1]
    owners = lax.axis_size("req")
    own_most = min(requests + requests // 2, owners)
    place = lax.axis_index("req").astype(jnp.int32).reshape(1)

    by_lag = jnp.transpose(conv_edge, (1, 0, 2))
    conv, partial = conv_project(
        x_in, by_lag, conv_weight, conv_bias.reshape(1, -1), x_proj_weight.T
    )
    if lax.axis_size("tp") == 2:
        partials = (partial, lax.ppermute(partial, "tp", [(0, 1), (1, 0)]))
    else:
        partials = (lax.psum(partial, "tp"),)

    def swap(rows, delta):
        return lax.ppermute(rows, "req", [(i, i ^ delta) for i in range(owners)]) if delta else rows

    groups = kept_edges((place, accepted, prompt_len, owner), x_in, by_lag, partial, owners)
    groups = [swap(rows, d * PLANE) for d, rows in enumerate(groups)]

    gains = (dt_gain.reshape(1, -1), b_gain.reshape(1, -1), c_gain.reshape(1, -1))
    bias = dt_bias.reshape(1, -1)
    state = ssm_state.reshape(requests * states, channels)
    slots = kept_states(
        (place, accepted, owner), partials, gains[:2], dt_proj_weight, bias, a_log, conv, state, owners
    )
    got = lax.all_to_all(slots, "req", split_axis=0, concat_axis=0, tiled=True)
    mixed = scan(
        partials, gains, dt_proj_weight, bias, a_log, skip.reshape(1, -1), conv, state, z_gate
    )
    mixed, owner = lax.optimization_barrier((mixed, owner))
    hits = jnp.any(owner.reshape(owners, requests) == place, axis=1)
    ids = jnp.arange(owners, dtype=jnp.int32)
    ranks = jnp.sum((hits[None, :] & (ids[None, :] < ids[:, None])).astype(jnp.int32), axis=1)
    at = hits[None, :] & (ranks[None, :] == jnp.arange(own_most, dtype=jnp.int32)[:, None])
    source = owners - jnp.sum(jnp.where(at, owners - ids[None, :], 0), axis=1)
    groups = [swap(rows, p) for p, rows in enumerate(regroup(groups, mixed))]
    owned_edge, tenant_stats = settle_edges(
        place, source, tenant_range, groups, own_most, lags, x_in.shape[0] // requests,
        requests,
    )
    owned = settle_states(source, got, own_most)
    return (mixed, owned, owned_edge, tenant_stats)


def solution(mesh):
    placed = (
        P("req", "tp"),
        P("req", "tp"),
        P("req", None, "tp"),
        P(None, "tp"),
        P("tp"),
        P("tp", None),
        P(),
        P(),
        P(),
        P(None, "tp"),
        P("tp"),
        P(None, "tp"),
        P("tp"),
        P("req", None, "tp"),
        P("req"),
        P("req"),
        P(),
        P(),
    )
    return jax.shard_map(
        per_device,
        mesh=mesh,
        in_specs=placed,
        out_specs=(P("req", "tp"), P("req", None, "tp"), P("req", None, "tp"), P()),
        check_vma=False,
    )
```

```python
import functools

import jax
import jax.numpy as jnp
import numpy as np
from jax import lax
from jax.experimental import pallas as pl
from jax.experimental.pallas import tpu as pltpu
from jax.sharding import PartitionSpec as P

EPSILON = 1e-06
SQUARE_FLOOR = 0.25
LOG2_E = 1.4426950408889634
LANES = 128
EDGE_ROWS = 4
PLANE = 4
DIGIT = 7
VMEM_BYTES = 24 * 1024 * 1024
BLOCK = 2048
ROUND = 4
VECTOR_WEIGHT = 30000


def iota(shape, axis):
    return lax.broadcasted_iota(jnp.int32, shape, axis)


def one_hot(condition):
    return jnp.where(condition, 1.0, 0.0).astype(jnp.bfloat16)


def dot(lhs, rhs):
    return jnp.dot(lhs, rhs, preferred_element_type=jnp.float32)


def in_hbm(array):
    return pltpu.with_memory_space_constraint(array, pltpu.HBM)


def silu(value):
    return value * (0.5 + 0.5 * jnp.tanh(0.5 * value))


def to_step_major(requests, steps):
    rows = requests * steps
    row, col = iota((rows, rows), 0), iota((rows, rows), 1)
    return one_hot(col == lax.rem(row, requests) * steps + lax.div(row, requests))


def to_request_major(requests, steps):
    rows = requests * steps
    row, col = iota((rows, rows), 0), iota((rows, rows), 1)
    return one_hot(row == lax.rem(col, requests) * steps + lax.div(col, requests))


def by_request(index, scalars):
    out = jnp.zeros_like(index)
    for request, scalar in enumerate(scalars):
        out = jnp.where(index == request, scalar, out)
    return out


def conv_kernel(
    x_hbm, edge_hbm, weight_hbm, bias_hbm, proj_hbm, conv_hbm, partial_ref, sent_ref,
    x_ref, edge_ref, weight_ref, bias_ref, proj_ref, conv_ref, sems, out_sems,
):
    lags, requests, channels = edge_ref.shape
    taps = weight_ref.shape[0]
    steps = x_ref.shape[0] // requests
    block = min(BLOCK, channels)
    pieces = [slice(c, c + block) for c in range(0, channels, block)]
    pairs = [(weight_hbm, weight_ref), (bias_hbm, bias_ref), (edge_hbm, edge_ref)]
    pairs += [(x_hbm.at[:, piece], x_ref.at[:, piece]) for piece in pieces]
    pairs.append((proj_hbm, proj_ref))
    copies = [pltpu.make_async_copy(*pair, sems.at[i]) for i, pair in enumerate(pairs)]
    for copy in copies:
        copy.start()
    results = [
        pltpu.make_async_copy(conv_ref.at[:, piece], conv_hbm.at[:, piece], out_sems.at[i])
        for i, piece in enumerate(pieces)
    ]
    order = to_step_major(requests, steps)
    for copy in copies[:3]:
        copy.wait()
    for i, piece in enumerate(pieces):
        copies[3 + i].wait()
        stream = dot(order, x_ref[:, piece])
        window = [edge_ref[k, :, piece].astype(jnp.float32) for k in range(lags)]
        window += [stream[t * requests : (t + 1) * requests] for t in range(steps)]
        weight = [weight_ref[k : k + 1, piece] for k in range(taps)]
        outs = []
        for t in range(steps):
            added = bias_ref[:, piece] + weight[0] * window[t]
            for k in range(1, taps):
                added = added + weight[k] * window[t + k]
            outs.append(silu(added))
        conv_ref[:, piece] = jnp.concatenate(outs, axis=0).astype(jnp.bfloat16)
        results[i].start()
    copies[-1].wait()
    partial = lax.dot_general(
        proj_ref[...], conv_ref[...], (((1,), (1,)), ((), ())), preferred_element_type=jnp.float32
    )
    partial_ref[...] = partial
    sent_ref[...] = partial.astype(jnp.bfloat16)
    for result in results:
        result.wait()


def conv_project(x_in, conv_edge, conv_weight, conv_bias, proj):
    rows, channels = x_in.shape
    operands = (x_in, conv_edge, conv_weight, conv_bias, proj)
    pieces = channels // min(BLOCK, channels)
    return pl.pallas_call(
        conv_kernel,
        in_specs=[pl.BlockSpec(memory_space=pl.ANY)] * len(operands),
        out_specs=[pl.BlockSpec(memory_space=pl.ANY)] + [pl.BlockSpec(memory_space=pltpu.VMEM)] * 2,
        out_shape=[
            pltpu.HBM((rows, channels), jnp.bfloat16),
            pltpu.HBM((proj.shape[0], rows), jnp.float32),
            pltpu.HBM((proj.shape[0], rows), jnp.bfloat16),
        ],
        scratch_shapes=[pltpu.VMEM(a.shape, a.dtype) for a in operands]
        + [
            pltpu.VMEM((rows, channels), jnp.bfloat16),
            pltpu.SemaphoreType.DMA((4 + pieces,)),
            pltpu.SemaphoreType.DMA((pieces,)),
        ],
        compiler_params=pltpu.CompilerParams(vmem_limit_bytes=VMEM_BYTES),
        name="conv_project",
    )(*(in_hbm(a) for a in operands))


def kept_edge_kernel(
    place_ref, accepted_ref, length_ref, owner_ref, x_ref, edge_ref, _, *group_refs
):
    lags, requests, block = edge_ref.shape
    steps = x_ref.shape[0] // requests
    place = place_ref[0]
    accepted = [accepted_ref[r] for r in range(requests)]
    lengths = [length_ref[r] + accepted[r] + 1 for r in range(requests)]
    deltas = [owner_ref[place * requests + r] ^ place for r in range(requests)]
    height = len(group_refs) * PLANE * EDGE_ROWS
    slot = lax.div(iota((height, 1), 0), EDGE_ROWS)
    lag = lax.rem(iota((height, 1), 0), EDGE_ROWS)

    def pick(request, position):
        return one_hot(
            (slot == by_request(request, deltas))
            & (position - by_request(request, accepted) == lag)
            & (lag < lags)
        )

    col = iota((1, requests * steps), 1)
    picked = dot(pick(lax.div(col, steps), lax.rem(col, steps) + lags), x_ref[...])
    col = iota((1, lags * requests), 1)
    edge = jnp.concatenate([edge_ref[k].astype(jnp.float32) for k in range(lags)], axis=0)
    picked += dot(pick(lax.rem(col, requests), lax.div(col, requests)), edge.astype(jnp.bfloat16))
    low = [length & ((1 << DIGIT) - 1) for length in lengths]
    high = [length >> DIGIT for length in lengths]
    numbers = by_request(iota((1, block), 1), accepted + low + high).astype(jnp.float32)
    picked = jnp.where(lag == lags, numbers, picked).astype(jnp.bfloat16)
    group = PLANE * EDGE_ROWS
    for d, ref in enumerate(group_refs):
        ref[...] = picked[d * group : (d + 1) * group]


def kept_edges(scalars, x_in, conv_edge, after, owners):
    channels = x_in.shape[1]
    groups = owners // PLANE
    vmem = pl.BlockSpec(memory_space=pltpu.VMEM)
    return pl.pallas_call(
        kept_edge_kernel,
        in_specs=[pl.BlockSpec(memory_space=pltpu.SMEM)] * len(scalars)
        + [vmem, vmem, pl.BlockSpec(memory_space=pl.ANY)],
        out_specs=[vmem] * groups,
        out_shape=[pltpu.HBM((PLANE * EDGE_ROWS, channels), jnp.bfloat16)] * groups,
        compiler_params=pltpu.CompilerParams(vmem_limit_bytes=VMEM_BYTES),
        name="kept_edges",
    )(*scalars, x_in, conv_edge, in_hbm(after))


def regroup_kernel(*refs):
    groups = len(refs) - 1 - PLANE
    rows = jnp.concatenate([ref[...].astype(jnp.float32) for ref in refs[:groups]], axis=0)
    for p, out_ref in enumerate(refs[-PLANE:]):
        parts = [
            rows[(d * PLANE + p) * EDGE_ROWS : (d * PLANE + p + 1) * EDGE_ROWS] for d in range(groups)
        ]
        out_ref[...] = jnp.concatenate(parts, axis=0).astype(jnp.bfloat16)


def regroup(arrived, after):
    rows, channels = arrived[0].shape
    block = min(1024, channels)
    height = len(arrived) * EDGE_ROWS
    return pl.pallas_call(
        regroup_kernel,
        grid=(channels // block,),
        in_specs=[pl.BlockSpec((rows, block), lambda j: (0, j))] * len(arrived)
        + [pl.BlockSpec(memory_space=pl.ANY)],
        out_specs=[pl.BlockSpec((height, block), lambda j: (0, j))] * PLANE,
        out_shape=[pltpu.HBM((height, channels), jnp.bfloat16)] * PLANE,
        compiler_params=pltpu.CompilerParams(
            dimension_semantics=("arbitrary",), vmem_limit_bytes=VMEM_BYTES
        ),
        name="regroup",
    )(*arrived, in_hbm(after))


def column(row):
    count = row.shape[1]
    same = iota((count, count), 0) == iota((count, count), 1)
    return jnp.sum(jnp.where(same, row, 0.0), axis=1, keepdims=True)


def normal(values, floor_value, eps_value):
    square = jnp.mean(values * values, axis=0, keepdims=True)
    return values * lax.rsqrt(jnp.maximum(square, floor_value) + eps_value)


def low_rank(total, gain):
    low = jnp.transpose(normal(total[: gain.shape[1]], 0.0, EPSILON))
    return (low * gain).astype(jnp.bfloat16)


def state_map(values, gain):
    return (normal(values, SQUARE_FLOOR, 0.0) * column(gain)).astype(jnp.bfloat16)


def summed(part_refs):
    total = part_refs[0][...]
    for part in part_refs[1:]:
        total = total + part[...].astype(jnp.float32)
    return total


def softplus(raw):
    return jnp.maximum(raw, 0.0) + jnp.log1p(jnp.exp(-jnp.abs(raw)))


def kept_kernel(parts, *refs):
    place_ref, accepted_ref, owner_ref = refs[:3]
    (
        dt_gain_ref, b_gain_ref, dt_weight_ref, dt_bias_ref, a_log_hbm, conv_hbm, state_hbm,
        slot_ref, part_ref, a_log_ref, conv_ref, state_ref, in_ref, size_ref, drive_ref, rate_ref, new_ref,
        in_sems, sems,
    ) = refs[3 + parts :]
    pairs = ((refs[3], part_ref), (a_log_hbm, a_log_ref), (conv_hbm, conv_ref), (state_hbm, state_ref))
    copies = [pltpu.make_async_copy(*pair, in_sems.at[i]) for i, pair in enumerate(pairs)]
    for copy in copies:
        copy.start()
    rank, states = dt_gain_ref.shape[1], b_gain_ref.shape[1]
    requests = accepted_ref.shape[0]
    rows, channels = conv_ref.shape
    steps = rows // requests
    span = min(2048, channels)
    halves = states // 8

    copies[0].wait()
    total = part_ref[...]
    for part in refs[4 : 3 + parts]:
        total = total + part[...].astype(jnp.float32)
    turned = state_map(total[rank : rank + states], b_gain_ref[...]).astype(jnp.float32)
    for row in range(rows):
        t, r = divmod(row, requests)
        in_ref[r * states : (r + 1) * states, t * LANES : (t + 1) * LANES] = jnp.broadcast_to(
            turned[:, row : row + 1], (states, LANES)
        )

    low = low_rank(total, dt_gain_ref[...])
    row = iota((rows, 1), 0)
    live = lax.div(row, requests) < by_request(
        lax.rem(row, requests), [accepted_ref[r] for r in range(requests)]
    )
    copies[1].wait()
    copies[2].wait()
    for first in range(0, channels, span):
        piece = slice(first, first + span)
        size = softplus(dot(low, dt_weight_ref[:, piece]) + dt_bias_ref[:, piece])
        size = jnp.where(live, size, 0.0)
        drive = size * conv_ref[:, piece].astype(jnp.float32)
        for c in range(span // LANES):
            tile = slice(c * LANES, (c + 1) * LANES)
            size_ref[first // LANES + c, :rows, :] = size[:, tile]
            drive_ref[first // LANES + c, :rows, :] = drive[:, tile]
        rate_ref[:, piece] = jnp.exp(a_log_ref[:, piece]) * (-LOG2_E)

    def one_request(r, carry):
        own = pl.multiple_of(r * states, states)
        rounds = lax.div(accepted_ref[r] + (ROUND - 1), ROUND)

        def one_span(part, inner):
            tiles = [pl.multiple_of(part * span + c, LANES) for c in range(0, span, LANES)]

            rates = [
                [rate_ref[8 * h : 8 * (h + 1), pl.ds(tile, LANES)] for tile in tiles]
                for h in range(halves)
            ]

            def one_round(i, hidden):
                hidden = [list(h) for h in hidden]
                for u in range(ROUND):
                    t = i * ROUND + u
                    at = pl.ds(t * requests + r, 8, stride=0)
                    lanes = pl.ds(pl.multiple_of(t * LANES, LANES), LANES)
                    b = [in_ref[pl.ds(own + 8 * h, 8), lanes] for h in range(halves)]
                    for c, tile in enumerate(tiles):
                        place = part * (span // LANES) + c
                        now, drive = size_ref[place, at, :], drive_ref[place, at, :]
                        for h in range(halves):
                            decay = jnp.exp2(now * rates[h][c])
                            hidden[h][c] = decay * hidden[h][c] + drive * b[h]
                return tuple(tuple(h) for h in hidden)

            lanes = pl.ds(pl.multiple_of(part * span, span), span)
            old = state_ref[pl.ds(own, states), lanes].astype(jnp.float32)
            start = tuple(
                tuple(
                    old[8 * h : 8 * (h + 1), c * LANES : (c + 1) * LANES] for c in range(len(tiles))
                )
                for h in range(halves)
            )
            done = lax.fori_loop(0, rounds, one_round, start)
            new = jnp.concatenate([jnp.concatenate(h, axis=1) for h in done], axis=0)
            new_ref[r, :, lanes] = new.astype(jnp.bfloat16)
            return inner

        lax.fori_loop(0, channels // span, one_span, 0)
        slot = owner_ref[place_ref[0] * requests + r]
        pltpu.make_async_copy(new_ref.at[r], slot_ref.at[slot], sems.at[r]).start()
        return carry

    copies[3].wait()
    lax.fori_loop(0, requests, one_request, 0)
    for r in range(requests):
        slot = owner_ref[place_ref[0] * requests + r]
        pltpu.make_async_copy(new_ref.at[r], slot_ref.at[slot], sems.at[r]).wait()


def kept_states(scalars, partials, gains, dt_weight, dt_bias, a_log, conv, state, slots):
    rows, channels = conv.shape
    states, rank = a_log.shape[0], dt_weight.shape[0]
    requests = scalars[1].shape[0]
    near = [*partials[1:], *gains, dt_weight, dt_bias]
    far = [in_hbm(a_log), in_hbm(conv), in_hbm(state)]
    anywhere = pl.BlockSpec(memory_space=pl.ANY)
    return pl.pallas_call(
        functools.partial(kept_kernel, len(partials)),
        in_specs=[pl.BlockSpec(memory_space=pltpu.SMEM)] * len(scalars)
        + [anywhere]
        + [pl.BlockSpec(memory_space=pltpu.VMEM)] * len(near)
        + [anywhere] * len(far),
        out_specs=anywhere,
        out_shape=pltpu.HBM((slots, states, channels), jnp.bfloat16),
        scratch_shapes=[
            pltpu.VMEM(partials[0].shape, jnp.float32),
            pltpu.VMEM(a_log.shape, jnp.float32),
            pltpu.VMEM(conv.shape, jnp.bfloat16),
            pltpu.VMEM(state.shape, jnp.bfloat16),
            pltpu.VMEM((requests * states, rows // requests * LANES), jnp.float32),
            pltpu.VMEM((channels // LANES, rows + 8, LANES), jnp.float32),
            pltpu.VMEM((channels // LANES, rows + 8, LANES), jnp.float32),
            pltpu.VMEM((states, channels), jnp.float32),
            pltpu.VMEM((requests, states, channels), jnp.bfloat16),
            pltpu.SemaphoreType.DMA((1 + len(far),)),
            pltpu.SemaphoreType.DMA((requests,)),
        ],
        compiler_params=pltpu.CompilerParams(vmem_limit_bytes=VMEM_BYTES),
        cost_estimate=pl.CostEstimate(
            flops=VECTOR_WEIGHT * 4 * rows * states * channels,
            transcendentals=rows * states * channels,
            bytes_accessed=2 * channels * (rows + rank + states * (requests + slots)),
        ),
        name="kept_states",
    )(*scalars, in_hbm(partials[0]), *near, *far)


def scan_kernel(parts, *refs):
    (
        dt_gain_ref, b_gain_ref, c_gain_ref, dt_weight_ref, dt_bias_ref, a_log_ref, skip_ref,
        conv_ref, state_ref, z_ref, mixed_ref,
        low_ref, in_ref, out_ref, size_ref, drive_ref, rate_ref, start_ref, sum_ref,
    ) = refs[parts:]
    rank, states = dt_gain_ref.shape[1], b_gain_ref.shape[1]
    rows, block = conv_ref.shape
    requests = state_ref.shape[0] // states
    steps = rows // requests

    @pl.when(pl.program_id(0) == 0)
    def _():
        total = summed(refs[:parts])
        low_ref[...] = low_rank(total, dt_gain_ref[...])
        in_map = state_map(total[rank : rank + states], b_gain_ref[...])
        out_map = state_map(total[rank + states :], c_gain_ref[...])
        wide = states * LANES
        spread = one_hot(lax.div(iota((states, wide), 1), LANES) == iota((states, wide), 0))
        turn = (((0,), (0,)), ((), ()))
        in_ref[...] = lax.dot_general(in_map, spread, turn, preferred_element_type=jnp.float32)
        out_ref[...] = lax.dot_general(out_map, spread, turn, preferred_element_type=jnp.float32)

    conv = conv_ref[...].astype(jnp.float32)
    size = softplus(dot(low_ref[...], dt_weight_ref[...]) + dt_bias_ref[...])
    size_ref[...] = size
    drive_ref[...] = size * conv
    start_ref[...] = dot(to_step_major(requests, states), state_ref[...])
    rate = jnp.exp(a_log_ref[...]) * (-LOG2_E)
    for n in range(states):
        rate_ref[n * requests : (n + 1) * requests, :] = jnp.broadcast_to(
            rate[n : n + 1, :], (requests, block)
        )

    pair = 2 if block % (2 * LANES) == 0 else 1

    def columns(c, carry):
        spans = [pl.ds(pl.multiple_of((c * pair + i) * LANES, LANES), LANES) for i in range(pair)]
        start = tuple(
            tuple(start_ref[n * requests : (n + 1) * requests, s] for s in spans)
            for n in range(states)
        )

        def step(t, hidden):
            at = pl.ds(pl.multiple_of(t * requests, requests), requests)
            sizes = [size_ref[at, s] for s in spans]
            drives = [drive_ref[at, s] for s in spans]
            sums = [None] * pair
            new = []
            for n in range(states):
                b = in_ref[at, n * LANES : (n + 1) * LANES]
                c_map = out_ref[at, n * LANES : (n + 1) * LANES]
                own = slice(n * requests, (n + 1) * requests)
                mine = []
                for i, s in enumerate(spans):
                    h = jnp.exp2(sizes[i] * rate_ref[own, s]) * hidden[n][i] + drives[i] * b
                    term = c_map * h
                    sums[i] = term if sums[i] is None else sums[i] + term
                    mine.append(h)
                new.append(tuple(mine))
            for i, s in enumerate(spans):
                sum_ref[at, s] = sums[i]
            return tuple(new)

        lax.fori_loop(0, steps, step, start, unroll=2)
        return carry

    lax.fori_loop(0, block // (pair * LANES), columns, 0)

    gate = silu(dot(to_step_major(requests, steps), z_ref[...]))
    mixed = ((sum_ref[...] + skip_ref[...] * conv) * gate).astype(jnp.bfloat16)
    mixed_ref[...] = dot(to_request_major(requests, steps), mixed).astype(jnp.bfloat16)


def scan(partials, gains, dt_weight, dt_bias, a_log, skip, conv, state, z_gate):
    rows, channels = conv.shape
    states, rank = a_log.shape[0], dt_weight.shape[0]
    block = min(512, channels)

    def whole(array):
        return pl.BlockSpec(array.shape, lambda j: (0, 0))

    wide = [in_hbm(dt_weight), dt_bias, in_hbm(a_log), skip, in_hbm(conv), in_hbm(state), in_hbm(z_gate)]
    tall = pltpu.VMEM((rows, block), jnp.float32)
    table = pltpu.VMEM((rows, states * LANES), jnp.float32)
    return pl.pallas_call(
        functools.partial(scan_kernel, len(partials)),
        grid=(channels // block,),
        in_specs=[whole(a) for a in (*partials, *gains)]
        + [pl.BlockSpec((a.shape[0], block), lambda j: (0, j)) for a in wide],
        out_specs=pl.BlockSpec((rows, block), lambda j: (0, j)),
        out_shape=jax.ShapeDtypeStruct((rows, channels), jnp.bfloat16),
        scratch_shapes=[
            pltpu.VMEM((rows, rank), jnp.bfloat16), table, table, tall, tall,
            pltpu.VMEM((state.shape[0], block), jnp.float32),
            pltpu.VMEM((state.shape[0], block), jnp.float32),
            tall,
        ],
        compiler_params=pltpu.CompilerParams(
            dimension_semantics=("arbitrary",), vmem_limit_bytes=VMEM_BYTES
        ),
        cost_estimate=pl.CostEstimate(
            flops=VECTOR_WEIGHT * 8 * rows * states * channels,
            transcendentals=rows * states * channels,
            bytes_accessed=2 * channels * (3 * rows + rank),
        ),
        name="scan",
    )(*partials, *gains, *wide)


def edge_kernel(steps, requests, place_ref, source_ref, range_ref, *refs):
    group_refs, edge_ref, stats_ref = refs[:-2], refs[-2], refs[-1]
    own_most, lags, block = edge_ref.shape
    groups = group_refs[0].shape[0] // EDGE_ROWS
    height = len(group_refs) * groups * EDGE_ROWS
    place = place_ref[0]

    def sender(index):
        p, d = lax.div(index, groups * EDGE_ROWS), lax.rem(lax.div(index, EDGE_ROWS), groups)
        return (d * PLANE + p) ^ place

    got = jnp.concatenate([ref[...] for ref in group_refs], axis=0)
    row, col = iota((own_most * 8, 1), 0), iota((1, height), 1)
    wanted = jnp.full((own_most * 8, 1), -1, jnp.int32)
    for i in range(own_most):
        wanted = jnp.where(lax.div(row, 8) == i, source_ref[i], wanted)
    pick = (sender(col) == wanted) & (lax.rem(col, EDGE_ROWS) == lax.rem(row, 8))
    picked = dot(one_hot(pick), got)
    for i in range(own_most):
        edge_ref[i] = picked[i * 8 : i * 8 + lags].astype(jnp.bfloat16)

    @pl.when(pl.program_id(0) == 0)
    def _():
        numbers = got[:, :LANES].astype(jnp.float32)
        row, lane = iota((height, LANES), 0), iota((height, LANES), 1)
        mine = lax.rem(row, EDGE_ROWS) == lags
        request = sender(row) * requests + lax.rem(lane, requests)
        digit = lax.div(lane, requests)
        counts = jnp.where(digit == 0, numbers, 0.0)
        lengths = jnp.where(digit == 1, numbers, 0.0) + jnp.where(
            digit == 2, numbers * float(1 << DIGIT), 0.0
        )
        tenants = range_ref.shape[0]
        sums, loads, members = [], [], []
        for k in range(tenants):
            start, end = range_ref[k, 0], range_ref[k, 1]
            inside = mine & (request >= start) & (request < end)
            sums.append(jnp.sum(jnp.where(inside, counts, 0.0), keepdims=True))
            loads.append(jnp.sum(jnp.where(inside, lengths, 0.0), keepdims=True))
            members.append((jnp.zeros((1, 1), jnp.int32) + (end - start)).astype(jnp.float32))
        mean = sum(loads[1:], loads[0]) / sum(members[1:], members[0])
        out = jnp.zeros((tenants, 2), jnp.float32)
        row, col = iota((tenants, 2), 0), iota((tenants, 2), 1)
        for k in range(tenants):
            rate = sums[k] / (float(steps) * members[k])
            load = loads[k] / members[k] / mean
            out = jnp.where(row == k, jnp.where(col == 0, rate, load), out)
        stats_ref[...] = out


def settle_edges(place, source, tenant_range, got, own_most, lags, steps, requests):
    smem = pl.BlockSpec(memory_space=pltpu.SMEM)
    height, channels = got[0].shape
    block = min(2048, channels)
    stats = (tenant_range.shape[0], 2)
    return pl.pallas_call(
        functools.partial(edge_kernel, steps, requests),
        grid=(channels // block,),
        in_specs=[smem] * 3 + [pl.BlockSpec((height, block), lambda j: (0, j))] * len(got),
        out_specs=[
            pl.BlockSpec((own_most, lags, block), lambda j: (0, 0, j)),
            pl.BlockSpec(stats, lambda j: (0, 0)),
        ],
        out_shape=[
            jax.ShapeDtypeStruct((own_most, lags, channels), jnp.bfloat16),
            jax.ShapeDtypeStruct(stats, jnp.float32),
        ],
        compiler_params=pltpu.CompilerParams(
            dimension_semantics=("arbitrary",), vmem_limit_bytes=VMEM_BYTES
        ),
        name="settle_edges",
    )(place, source, tenant_range, *got)


def settle_kernel(source_ref, got_hbm, owned_hbm, rows_ref, in_sem, sems):
    slots = got_hbm.shape[0]
    fetch = pltpu.make_async_copy(got_hbm, rows_ref.at[:slots], in_sem)
    fetch.start()
    rows_ref[slots] = jnp.zeros(rows_ref.shape[1:], rows_ref.dtype)
    fetch.wait()
    puts = [
        pltpu.make_async_copy(rows_ref.at[source_ref[i]], owned_hbm.at[i], sems.at[i])
        for i in range(owned_hbm.shape[0])
    ]
    for put in puts:
        put.start()
    for put in puts:
        put.wait()


def settle_states(source, got, own_most):
    anywhere = pl.BlockSpec(memory_space=pl.ANY)
    slots, *rest = got.shape
    return pl.pallas_call(
        settle_kernel,
        in_specs=[pl.BlockSpec(memory_space=pltpu.SMEM), anywhere],
        out_specs=anywhere,
        out_shape=pltpu.HBM((own_most, *rest), got.dtype),
        scratch_shapes=[
            pltpu.VMEM((slots + 1, *rest), got.dtype),
            pltpu.SemaphoreType.DMA,
            pltpu.SemaphoreType.DMA((own_most,)),
        ],
        compiler_params=pltpu.CompilerParams(vmem_limit_bytes=VMEM_BYTES),
        name="settle_states",
    )(source, in_hbm(got))


def per_device(
    x_in, z_gate, conv_edge, conv_weight, conv_bias, x_proj_weight, dt_gain, b_gain, c_gain,
    dt_proj_weight, dt_bias, a_log, skip, ssm_state, accepted, prompt_len, tenant_range, owner,
):
    requests, states, channels = ssm_state.shape
    lags = conv_edge.shape[1]
    owners = lax.axis_size("req")
    own_most = min(requests + requests // 2, owners)
    place = lax.axis_index("req").astype(jnp.int32).reshape(1)

    by_lag = jnp.transpose(conv_edge, (1, 0, 2))
    conv, partial, sent = conv_project(
        x_in, by_lag, conv_weight, conv_bias.reshape(1, -1), x_proj_weight.T
    )
    if lax.axis_size("tp") == 2:
        partials = (partial, lax.ppermute(sent, "tp", [(0, 1), (1, 0)]))
    else:
        partials = (lax.psum(partial, "tp"),)

    def swap(rows, delta):
        return lax.ppermute(rows, "req", [(i, i ^ delta) for i in range(owners)]) if delta else rows

    groups = kept_edges((place, accepted, prompt_len, owner), x_in, by_lag, partial, owners)
    groups = [swap(rows, d * PLANE) for d, rows in enumerate(groups)]

    gains = (dt_gain.reshape(1, -1), b_gain.reshape(1, -1), c_gain.reshape(1, -1))
    bias = dt_bias.reshape(1, -1)
    state = ssm_state.reshape(requests * states, channels)
    slots = kept_states(
        (place, accepted, owner), partials, gains[:2], dt_proj_weight, bias, a_log, conv, state, owners
    )
    got = lax.all_to_all(slots, "req", split_axis=0, concat_axis=0, tiled=True)
    mixed = scan(
        partials, gains, dt_proj_weight, bias, a_log, skip.reshape(1, -1), conv, state, z_gate
    )
    mixed, owner = lax.optimization_barrier((mixed, owner))
    hits = jnp.any(owner.reshape(owners, requests) == place, axis=1)
    ids = np.arange(owners, dtype=np.int32)
    ranks = jnp.sum((hits[None, :] & (ids[None, :] < ids[:, None])).astype(jnp.int32), axis=1)
    at = hits[None, :] & (ranks[None, :] == jnp.arange(own_most, dtype=jnp.int32)[:, None])
    source = owners - jnp.sum(jnp.where(at, owners - ids[None, :], 0), axis=1)
    groups = [swap(rows, p) for p, rows in enumerate(regroup(groups, mixed))]
    owned_edge, tenant_stats = settle_edges(
        place, source, tenant_range, groups, own_most, lags, x_in.shape[0] // requests,
        requests,
    )
    owned = settle_states(source, got, own_most)
    return (mixed, owned, owned_edge, tenant_stats)


def solution(mesh):
    placed = (
        P("req", "tp"),
        P("req", "tp"),
        P("req", None, "tp"),
        P(None, "tp"),
        P("tp"),
        P("tp", None),
        P(),
        P(),
        P(),
        P(None, "tp"),
        P("tp"),
        P(None, "tp"),
        P("tp"),
        P("req", None, "tp"),
        P("req"),
        P("req"),
        P(),
        P(),
    )
    return jax.shard_map(
        per_device,
        mesh=mesh,
        in_specs=placed,
        out_specs=(P("req", "tp"), P("req", None, "tp"), P("req", None, "tp"), P()),
        check_vma=False,
    )
```

```python
import functools

import jax
import jax.numpy as jnp
import numpy as np
from jax import lax
from jax.experimental import pallas as pl
from jax.experimental.pallas import tpu as pltpu
from jax.sharding import PartitionSpec as P

EPSILON = 1e-06
SQUARE_FLOOR = 0.25
LOG2_E = 1.4426950408889634
LANES = 128
EDGE_ROWS = 4
PLANE = 4
DIGIT = 7
VMEM_BYTES = 24 * 1024 * 1024
BLOCK = 2048
PARTS = 4
ROUND = 4
VECTOR_WEIGHT = 30000


def iota(shape, axis):
    return lax.broadcasted_iota(jnp.int32, shape, axis)


def one_hot(condition):
    return jnp.where(condition, 1.0, 0.0).astype(jnp.bfloat16)


def dot(lhs, rhs):
    return jnp.dot(lhs, rhs, preferred_element_type=jnp.float32)


def in_hbm(array):
    return pltpu.with_memory_space_constraint(array, pltpu.HBM)


def silu(value):
    return value * (0.5 + 0.5 * jnp.tanh(0.5 * value))


def to_step_major(requests, steps):
    rows = requests * steps
    row, col = iota((rows, rows), 0), iota((rows, rows), 1)
    return one_hot(col == lax.rem(row, requests) * steps + lax.div(row, requests))


def to_request_major(requests, steps):
    rows = requests * steps
    row, col = iota((rows, rows), 0), iota((rows, rows), 1)
    return one_hot(row == lax.rem(col, requests) * steps + lax.div(col, requests))


def by_request(index, scalars):
    out = jnp.zeros_like(index)
    for request, scalar in enumerate(scalars):
        out = jnp.where(index == request, scalar, out)
    return out


def conv_kernel(
    x_hbm, edge_hbm, weight_hbm, bias_hbm, proj_hbm, conv_hbm, partial_ref,
    x_ref, edge_ref, weight_ref, bias_ref, proj_ref, conv_ref, sems, out_sems,
):
    lags, requests, channels = edge_ref.shape
    taps = weight_ref.shape[0]
    steps = x_ref.shape[0] // requests
    block = min(BLOCK, channels)
    pieces = [slice(c, c + block) for c in range(0, channels, block)]
    pairs = [(weight_hbm, weight_ref), (bias_hbm, bias_ref), (edge_hbm, edge_ref)]
    pairs += [(x_hbm.at[:, piece], x_ref.at[:, piece]) for piece in pieces]
    pairs.append((proj_hbm, proj_ref))
    copies = [pltpu.make_async_copy(*pair, sems.at[i]) for i, pair in enumerate(pairs)]
    for copy in copies:
        copy.start()
    results = [
        pltpu.make_async_copy(conv_ref.at[:, piece], conv_hbm.at[:, piece], out_sems.at[i])
        for i, piece in enumerate(pieces)
    ]
    order = to_step_major(requests, steps)
    for copy in copies[:3]:
        copy.wait()
    for i, piece in enumerate(pieces):
        copies[3 + i].wait()
        stream = dot(order, x_ref[:, piece])
        window = [edge_ref[k, :, piece].astype(jnp.float32) for k in range(lags)]
        window += [stream[t * requests : (t + 1) * requests] for t in range(steps)]
        weight = [weight_ref[k : k + 1, piece] for k in range(taps)]
        outs = []
        for t in range(steps):
            added = bias_ref[:, piece] + weight[0] * window[t]
            for k in range(1, taps):
                added = added + weight[k] * window[t + k]
            outs.append(silu(added))
        conv_ref[:, piece] = jnp.concatenate(outs, axis=0).astype(jnp.bfloat16)
        results[i].start()
    copies[-1].wait()
    partial_ref[...] = lax.dot_general(
        proj_ref[...], conv_ref[...], (((1,), (1,)), ((), ())), preferred_element_type=jnp.float32
    )
    for result in results:
        result.wait()


def conv_project(x_in, conv_edge, conv_weight, conv_bias, proj):
    rows, channels = x_in.shape
    operands = (x_in, conv_edge, conv_weight, conv_bias, proj)
    pieces = channels // min(BLOCK, channels)
    return pl.pallas_call(
        conv_kernel,
        in_specs=[pl.BlockSpec(memory_space=pl.ANY)] * len(operands),
        out_specs=[pl.BlockSpec(memory_space=pl.ANY), pl.BlockSpec(memory_space=pltpu.VMEM)],
        out_shape=[
            pltpu.HBM((rows, channels), jnp.bfloat16),
            pltpu.HBM((proj.shape[0], rows), jnp.float32),
        ],
        scratch_shapes=[pltpu.VMEM(a.shape, a.dtype) for a in operands]
        + [
            pltpu.VMEM((rows, channels), jnp.bfloat16),
            pltpu.SemaphoreType.DMA((4 + pieces,)),
            pltpu.SemaphoreType.DMA((pieces,)),
        ],
        compiler_params=pltpu.CompilerParams(vmem_limit_bytes=VMEM_BYTES),
        name="conv_project",
    )(*(in_hbm(a) for a in operands))


def kept_edge_kernel(
    place_ref, accepted_ref, length_ref, owner_ref, x_ref, edge_ref, _, *group_refs
):
    lags, requests, block = edge_ref.shape
    steps = x_ref.shape[0] // requests
    place = place_ref[0]
    accepted = [accepted_ref[r] for r in range(requests)]
    lengths = [length_ref[r] + accepted[r] + 1 for r in range(requests)]
    deltas = [owner_ref[place * requests + r] ^ place for r in range(requests)]
    height = len(group_refs) * PLANE * EDGE_ROWS
    slot = lax.div(iota((height, 1), 0), EDGE_ROWS)
    lag = lax.rem(iota((height, 1), 0), EDGE_ROWS)

    def pick(request, position):
        return one_hot(
            (slot == by_request(request, deltas))
            & (position - by_request(request, accepted) == lag)
            & (lag < lags)
        )

    col = iota((1, requests * steps), 1)
    picked = dot(pick(lax.div(col, steps), lax.rem(col, steps) + lags), x_ref[...])
    col = iota((1, lags * requests), 1)
    edge = jnp.concatenate([edge_ref[k].astype(jnp.float32) for k in range(lags)], axis=0)
    picked += dot(pick(lax.rem(col, requests), lax.div(col, requests)), edge.astype(jnp.bfloat16))
    low = [length & ((1 << DIGIT) - 1) for length in lengths]
    high = [length >> DIGIT for length in lengths]
    numbers = by_request(iota((1, block), 1), accepted + low + high).astype(jnp.float32)
    picked = jnp.where(lag == lags, numbers, picked).astype(jnp.bfloat16)
    group = PLANE * EDGE_ROWS
    for d, ref in enumerate(group_refs):
        ref[...] = picked[d * group : (d + 1) * group]


def kept_edges(scalars, x_in, conv_edge, after, owners):
    channels = x_in.shape[1]
    groups = owners // PLANE
    vmem = pl.BlockSpec(memory_space=pltpu.VMEM)
    return pl.pallas_call(
        kept_edge_kernel,
        in_specs=[pl.BlockSpec(memory_space=pltpu.SMEM)] * len(scalars)
        + [vmem, vmem, pl.BlockSpec(memory_space=pl.ANY)],
        out_specs=[vmem] * groups,
        out_shape=[pltpu.HBM((PLANE * EDGE_ROWS, channels), jnp.bfloat16)] * groups,
        compiler_params=pltpu.CompilerParams(vmem_limit_bytes=VMEM_BYTES),
        name="kept_edges",
    )(*scalars, x_in, conv_edge, in_hbm(after))


def regroup_kernel(*refs):
    groups = len(refs) - 1 - PLANE
    rows = jnp.concatenate([ref[...].astype(jnp.float32) for ref in refs[:groups]], axis=0)
    for p, out_ref in enumerate(refs[-PLANE:]):
        parts = [
            rows[(d * PLANE + p) * EDGE_ROWS : (d * PLANE + p + 1) * EDGE_ROWS] for d in range(groups)
        ]
        out_ref[...] = jnp.concatenate(parts, axis=0).astype(jnp.bfloat16)


def regroup(arrived, after):
    rows, channels = arrived[0].shape
    block = min(1024, channels)
    height = len(arrived) * EDGE_ROWS
    return pl.pallas_call(
        regroup_kernel,
        grid=(channels // block,),
        in_specs=[pl.BlockSpec((rows, block), lambda j: (0, j))] * len(arrived)
        + [pl.BlockSpec(memory_space=pl.ANY)],
        out_specs=[pl.BlockSpec((height, block), lambda j: (0, j))] * PLANE,
        out_shape=[pltpu.HBM((height, channels), jnp.bfloat16)] * PLANE,
        compiler_params=pltpu.CompilerParams(
            dimension_semantics=("arbitrary",), vmem_limit_bytes=VMEM_BYTES
        ),
        name="regroup",
    )(*arrived, in_hbm(after))


def column(row):
    count = row.shape[1]
    same = iota((count, count), 0) == iota((count, count), 1)
    return jnp.sum(jnp.where(same, row, 0.0), axis=1, keepdims=True)


def normal(values, floor_value, eps_value):
    square = jnp.mean(values * values, axis=0, keepdims=True)
    return values * lax.rsqrt(jnp.maximum(square, floor_value) + eps_value)


def low_rank(total, gain):
    low = jnp.transpose(normal(total[: gain.shape[1]], 0.0, EPSILON))
    return (low * gain).astype(jnp.bfloat16)


def state_map(values, gain):
    return (normal(values, SQUARE_FLOOR, 0.0) * column(gain)).astype(jnp.bfloat16)


def summed(part_refs):
    total = part_refs[0][...]
    for part in part_refs[1:]:
        total = total + part[...]
    return total


def softplus(raw):
    return jnp.maximum(raw, 0.0) + jnp.log1p(jnp.exp(-jnp.abs(raw)))


def kept_kernel(parts, *refs):
    place_ref, accepted_ref, owner_ref = refs[:3]
    (
        dt_gain_ref, b_gain_ref, dt_weight_ref, dt_bias_ref, a_log_hbm, conv_hbm, state_hbm,
        slot_ref, part_ref, a_log_ref, conv_ref, state_ref, in_ref, size_ref, drive_ref, rate_ref, new_ref,
        in_sems, sems,
    ) = refs[3 + parts :]
    pairs = ((refs[3], part_ref), (a_log_hbm, a_log_ref), (conv_hbm, conv_ref), (state_hbm, state_ref))
    copies = [pltpu.make_async_copy(*pair, in_sems.at[i]) for i, pair in enumerate(pairs)]
    for copy in copies:
        copy.start()
    rank, states = dt_gain_ref.shape[1], b_gain_ref.shape[1]
    requests = accepted_ref.shape[0]
    rows, channels = conv_ref.shape
    steps = rows // requests
    span = min(2048, channels)
    halves = states // 8

    copies[0].wait()
    total = part_ref[...]
    for part in refs[4 : 3 + parts]:
        total = total + part[...]
    turned = state_map(total[rank : rank + states], b_gain_ref[...]).astype(jnp.float32)
    for row in range(rows):
        t, r = divmod(row, requests)
        in_ref[r * states : (r + 1) * states, t * LANES : (t + 1) * LANES] = jnp.broadcast_to(
            turned[:, row : row + 1], (states, LANES)
        )

    low = low_rank(total, dt_gain_ref[...])
    row = iota((rows, 1), 0)
    live = lax.div(row, requests) < by_request(
        lax.rem(row, requests), [accepted_ref[r] for r in range(requests)]
    )
    copies[1].wait()
    copies[2].wait()
    for first in range(0, channels, span):
        piece = slice(first, first + span)
        size = softplus(dot(low, dt_weight_ref[:, piece]) + dt_bias_ref[:, piece])
        size = jnp.where(live, size, 0.0)
        drive = size * conv_ref[:, piece].astype(jnp.float32)
        for c in range(span // LANES):
            tile = slice(c * LANES, (c + 1) * LANES)
            size_ref[first // LANES + c, :rows, :] = size[:, tile]
            drive_ref[first // LANES + c, :rows, :] = drive[:, tile]
        rate_ref[:, piece] = jnp.exp(a_log_ref[:, piece]) * (-LOG2_E)

    def one_request(r, carry):
        own = pl.multiple_of(r * states, states)
        rounds = lax.div(accepted_ref[r] + (ROUND - 1), ROUND)

        def one_span(part, inner):
            tiles = [pl.multiple_of(part * span + c, LANES) for c in range(0, span, LANES)]

            rates = [
                [rate_ref[8 * h : 8 * (h + 1), pl.ds(tile, LANES)] for tile in tiles]
                for h in range(halves)
            ]

            def one_round(i, hidden):
                hidden = [list(h) for h in hidden]
                for u in range(ROUND):
                    t = i * ROUND + u
                    at = pl.ds(t * requests + r, 8, stride=0)
                    lanes = pl.ds(pl.multiple_of(t * LANES, LANES), LANES)
                    b = [in_ref[pl.ds(own + 8 * h, 8), lanes] for h in range(halves)]
                    for c, tile in enumerate(tiles):
                        place = part * (span // LANES) + c
                        now, drive = size_ref[place, at, :], drive_ref[place, at, :]
                        for h in range(halves):
                            decay = jnp.exp2(now * rates[h][c])
                            hidden[h][c] = decay * hidden[h][c] + drive * b[h]
                return tuple(tuple(h) for h in hidden)

            lanes = pl.ds(pl.multiple_of(part * span, span), span)
            old = state_ref[pl.ds(own, states), lanes].astype(jnp.float32)
            start = tuple(
                tuple(
                    old[8 * h : 8 * (h + 1), c * LANES : (c + 1) * LANES] for c in range(len(tiles))
                )
                for h in range(halves)
            )
            done = lax.fori_loop(0, rounds, one_round, start)
            new = jnp.concatenate([jnp.concatenate(h, axis=1) for h in done], axis=0)
            new_ref[r, :, lanes] = new.astype(jnp.bfloat16)
            return inner

        lax.fori_loop(0, channels // span, one_span, 0)
        slot = owner_ref[place_ref[0] * requests + r]
        pltpu.make_async_copy(new_ref.at[r], slot_ref.at[slot], sems.at[r]).start()
        return carry

    copies[3].wait()
    lax.fori_loop(0, requests, one_request, 0)
    for r in range(requests):
        slot = owner_ref[place_ref[0] * requests + r]
        pltpu.make_async_copy(new_ref.at[r], slot_ref.at[slot], sems.at[r]).wait()


def kept_states(scalars, partials, gains, dt_weight, dt_bias, a_log, conv, state, slots):
    rows, channels = conv.shape
    states, rank = a_log.shape[0], dt_weight.shape[0]
    requests = scalars[1].shape[0]
    near = [*partials[1:], *gains, dt_weight, dt_bias]
    far = [in_hbm(a_log), in_hbm(conv), in_hbm(state)]
    anywhere = pl.BlockSpec(memory_space=pl.ANY)
    return pl.pallas_call(
        functools.partial(kept_kernel, len(partials)),
        in_specs=[pl.BlockSpec(memory_space=pltpu.SMEM)] * len(scalars)
        + [anywhere]
        + [pl.BlockSpec(memory_space=pltpu.VMEM)] * len(near)
        + [anywhere] * len(far),
        out_specs=anywhere,
        out_shape=pltpu.HBM((slots, states, channels), jnp.bfloat16),
        scratch_shapes=[
            pltpu.VMEM(partials[0].shape, jnp.float32),
            pltpu.VMEM(a_log.shape, jnp.float32),
            pltpu.VMEM(conv.shape, jnp.bfloat16),
            pltpu.VMEM(state.shape, jnp.bfloat16),
            pltpu.VMEM((requests * states, rows // requests * LANES), jnp.float32),
            pltpu.VMEM((channels // LANES, rows + 8, LANES), jnp.float32),
            pltpu.VMEM((channels // LANES, rows + 8, LANES), jnp.float32),
            pltpu.VMEM((states, channels), jnp.float32),
            pltpu.VMEM((requests, states, channels), jnp.bfloat16),
            pltpu.SemaphoreType.DMA((1 + len(far),)),
            pltpu.SemaphoreType.DMA((requests,)),
        ],
        compiler_params=pltpu.CompilerParams(vmem_limit_bytes=VMEM_BYTES),
        cost_estimate=pl.CostEstimate(
            flops=VECTOR_WEIGHT * 4 * rows * states * channels,
            transcendentals=rows * states * channels,
            bytes_accessed=2 * channels * (rows + rank + states * (requests + slots)),
        ),
        name="kept_states",
    )(*scalars, in_hbm(partials[0]), *near, *far)


def scan_kernel(parts, *refs):
    (
        dt_gain_ref, b_gain_ref, c_gain_ref, dt_weight_ref, dt_bias_ref, a_log_ref, skip_ref,
        conv_ref, state_ref, z_ref, mixed_ref,
        low_ref, in_ref, out_ref, size_ref, drive_ref, rate_ref, start_ref, sum_ref,
    ) = refs[parts:]
    rank, states = dt_gain_ref.shape[1], b_gain_ref.shape[1]
    rows, block = conv_ref.shape
    requests = state_ref.shape[0] // states
    steps = rows // requests

    @pl.when(pl.program_id(0) == 0)
    def _():
        total = summed(refs[:parts])
        low_ref[...] = low_rank(total, dt_gain_ref[...])
        in_map = state_map(total[rank : rank + states], b_gain_ref[...])
        out_map = state_map(total[rank + states :], c_gain_ref[...])
        wide = states * LANES
        spread = one_hot(lax.div(iota((states, wide), 1), LANES) == iota((states, wide), 0))
        turn = (((0,), (0,)), ((), ()))
        in_ref[...] = lax.dot_general(in_map, spread, turn, preferred_element_type=jnp.float32)
        out_ref[...] = lax.dot_general(out_map, spread, turn, preferred_element_type=jnp.float32)

    conv = conv_ref[...].astype(jnp.float32)
    size = softplus(dot(low_ref[...], dt_weight_ref[...]) + dt_bias_ref[...])
    size_ref[...] = size
    drive_ref[...] = size * conv
    start_ref[...] = dot(to_step_major(requests, states), state_ref[...])
    rate = jnp.exp(a_log_ref[...]) * (-LOG2_E)
    for n in range(states):
        rate_ref[n * requests : (n + 1) * requests, :] = jnp.broadcast_to(
            rate[n : n + 1, :], (requests, block)
        )

    pair = 2 if block % (2 * LANES) == 0 else 1

    def columns(c, carry):
        spans = [pl.ds(pl.multiple_of((c * pair + i) * LANES, LANES), LANES) for i in range(pair)]
        start = tuple(
            tuple(start_ref[n * requests : (n + 1) * requests, s] for s in spans)
            for n in range(states)
        )

        def step(t, hidden):
            at = pl.ds(pl.multiple_of(t * requests, requests), requests)
            sizes = [size_ref[at, s] for s in spans]
            drives = [drive_ref[at, s] for s in spans]
            sums = [None] * pair
            new = []
            for n in range(states):
                b = in_ref[at, n * LANES : (n + 1) * LANES]
                c_map = out_ref[at, n * LANES : (n + 1) * LANES]
                own = slice(n * requests, (n + 1) * requests)
                mine = []
                for i, s in enumerate(spans):
                    h = jnp.exp2(sizes[i] * rate_ref[own, s]) * hidden[n][i] + drives[i] * b
                    term = c_map * h
                    sums[i] = term if sums[i] is None else sums[i] + term
                    mine.append(h)
                new.append(tuple(mine))
            for i, s in enumerate(spans):
                sum_ref[at, s] = sums[i]
            return tuple(new)

        lax.fori_loop(0, steps, step, start, unroll=2)
        return carry

    lax.fori_loop(0, block // (pair * LANES), columns, 0)

    gate = silu(dot(to_step_major(requests, steps), z_ref[...]))
    mixed = ((sum_ref[...] + skip_ref[...] * conv) * gate).astype(jnp.bfloat16)
    mixed_ref[...] = dot(to_request_major(requests, steps), mixed).astype(jnp.bfloat16)


def scan(partials, gains, dt_weight, dt_bias, a_log, skip, conv, state, z_gate):
    rows, channels = conv.shape
    states, rank = a_log.shape[0], dt_weight.shape[0]
    block = min(512, channels)

    def whole(array):
        return pl.BlockSpec(array.shape, lambda j: (0, 0))

    wide = [in_hbm(dt_weight), dt_bias, in_hbm(a_log), skip, in_hbm(conv), in_hbm(state), in_hbm(z_gate)]
    tall = pltpu.VMEM((rows, block), jnp.float32)
    table = pltpu.VMEM((rows, states * LANES), jnp.float32)
    return pl.pallas_call(
        functools.partial(scan_kernel, len(partials)),
        grid=(channels // block,),
        in_specs=[whole(a) for a in (*partials, *gains)]
        + [pl.BlockSpec((a.shape[0], block), lambda j: (0, j)) for a in wide],
        out_specs=pl.BlockSpec((rows, block), lambda j: (0, j)),
        out_shape=jax.ShapeDtypeStruct((rows, channels), jnp.bfloat16),
        scratch_shapes=[
            pltpu.VMEM((rows, rank), jnp.bfloat16), table, table, tall, tall,
            pltpu.VMEM((state.shape[0], block), jnp.float32),
            pltpu.VMEM((state.shape[0], block), jnp.float32),
            tall,
        ],
        compiler_params=pltpu.CompilerParams(
            dimension_semantics=("arbitrary",), vmem_limit_bytes=VMEM_BYTES
        ),
        cost_estimate=pl.CostEstimate(
            flops=VECTOR_WEIGHT * 8 * rows * states * channels,
            transcendentals=rows * states * channels,
            bytes_accessed=2 * channels * (3 * rows + rank),
        ),
        name="scan",
    )(*partials, *gains, *wide)


def edge_kernel(steps, requests, place_ref, source_ref, range_ref, *refs):
    group_refs, edge_ref, stats_ref = refs[:-2], refs[-2], refs[-1]
    own_most, lags, block = edge_ref.shape
    groups = group_refs[0].shape[0] // EDGE_ROWS
    height = len(group_refs) * groups * EDGE_ROWS
    place = place_ref[0]

    def sender(index):
        p, d = lax.div(index, groups * EDGE_ROWS), lax.rem(lax.div(index, EDGE_ROWS), groups)
        return (d * PLANE + p) ^ place

    got = jnp.concatenate([ref[...] for ref in group_refs], axis=0)
    row, col = iota((own_most * 8, 1), 0), iota((1, height), 1)
    wanted = jnp.full((own_most * 8, 1), -1, jnp.int32)
    for i in range(own_most):
        wanted = jnp.where(lax.div(row, 8) == i, source_ref[i], wanted)
    pick = (sender(col) == wanted) & (lax.rem(col, EDGE_ROWS) == lax.rem(row, 8))
    picked = dot(one_hot(pick), got)
    for i in range(own_most):
        edge_ref[i] = picked[i * 8 : i * 8 + lags].astype(jnp.bfloat16)

    @pl.when(pl.program_id(0) == 0)
    def _():
        numbers = got[:, :LANES].astype(jnp.float32)
        row, lane = iota((height, LANES), 0), iota((height, LANES), 1)
        mine = lax.rem(row, EDGE_ROWS) == lags
        request = sender(row) * requests + lax.rem(lane, requests)
        digit = lax.div(lane, requests)
        counts = jnp.where(digit == 0, numbers, 0.0)
        lengths = jnp.where(digit == 1, numbers, 0.0) + jnp.where(
            digit == 2, numbers * float(1 << DIGIT), 0.0
        )
        tenants = range_ref.shape[0]
        sums, loads, members = [], [], []
        for k in range(tenants):
            start, end = range_ref[k, 0], range_ref[k, 1]
            inside = mine & (request >= start) & (request < end)
            sums.append(jnp.sum(jnp.where(inside, counts, 0.0), keepdims=True))
            loads.append(jnp.sum(jnp.where(inside, lengths, 0.0), keepdims=True))
            members.append((jnp.zeros((1, 1), jnp.int32) + (end - start)).astype(jnp.float32))
        mean = sum(loads[1:], loads[0]) / sum(members[1:], members[0])
        out = jnp.zeros((tenants, 2), jnp.float32)
        row, col = iota((tenants, 2), 0), iota((tenants, 2), 1)
        for k in range(tenants):
            rate = sums[k] / (float(steps) * members[k])
            load = loads[k] / members[k] / mean
            out = jnp.where(row == k, jnp.where(col == 0, rate, load), out)
        stats_ref[...] = out


def settle_edges(place, source, tenant_range, got, own_most, lags, steps, requests):
    smem = pl.BlockSpec(memory_space=pltpu.SMEM)
    height, channels = got[0].shape
    block = min(2048, channels)
    stats = (tenant_range.shape[0], 2)
    return pl.pallas_call(
        functools.partial(edge_kernel, steps, requests),
        grid=(channels // block,),
        in_specs=[smem] * 3 + [pl.BlockSpec((height, block), lambda j: (0, j))] * len(got),
        out_specs=[
            pl.BlockSpec((own_most, lags, block), lambda j: (0, 0, j)),
            pl.BlockSpec(stats, lambda j: (0, 0)),
        ],
        out_shape=[
            jax.ShapeDtypeStruct((own_most, lags, channels), jnp.bfloat16),
            jax.ShapeDtypeStruct(stats, jnp.float32),
        ],
        compiler_params=pltpu.CompilerParams(
            dimension_semantics=("arbitrary",), vmem_limit_bytes=VMEM_BYTES
        ),
        name="settle_edges",
    )(place, source, tenant_range, *got)


def settle_kernel(source_ref, bound_ref, got_hbm, owned_hbm, rows_ref, in_sems, sems):
    slots, own_most = got_hbm.shape[0], owned_hbm.shape[0]
    size = slots // PARTS
    parts = [slice(q * size, (q + 1) * size) for q in range(PARTS)]
    fetches = [
        pltpu.make_async_copy(got_hbm.at[part], rows_ref.at[part], in_sems.at[q])
        for q, part in enumerate(parts)
    ]
    for fetch in fetches:
        fetch.start()
    rows_ref[slots] = jnp.zeros(rows_ref.shape[1:], rows_ref.dtype)

    def put(i):
        return pltpu.make_async_copy(rows_ref.at[source_ref[i]], owned_hbm.at[i], sems.at[i])

    def start(i, carry):
        put(i).start()
        return carry

    lax.fori_loop(bound_ref[PARTS], own_most, start, 0)
    for q, fetch in enumerate(fetches):
        fetch.wait()
        lax.fori_loop(bound_ref[q], bound_ref[q + 1], start, 0)
    for i in range(own_most):
        put(i).wait()


def settle_states(source, bounds, got, own_most):
    smem = pl.BlockSpec(memory_space=pltpu.SMEM)
    anywhere = pl.BlockSpec(memory_space=pl.ANY)
    slots, *rest = got.shape
    return pl.pallas_call(
        settle_kernel,
        in_specs=[smem, smem, anywhere],
        out_specs=anywhere,
        out_shape=pltpu.HBM((own_most, *rest), got.dtype),
        scratch_shapes=[
            pltpu.VMEM((slots + 1, *rest), got.dtype),
            pltpu.SemaphoreType.DMA((PARTS,)),
            pltpu.SemaphoreType.DMA((own_most,)),
        ],
        compiler_params=pltpu.CompilerParams(vmem_limit_bytes=VMEM_BYTES),
        name="settle_states",
    )(source, bounds, in_hbm(got))


def per_device(
    x_in, z_gate, conv_edge, conv_weight, conv_bias, x_proj_weight, dt_gain, b_gain, c_gain,
    dt_proj_weight, dt_bias, a_log, skip, ssm_state, accepted, prompt_len, tenant_range, owner,
):
    requests, states, channels = ssm_state.shape
    lags = conv_edge.shape[1]
    owners = lax.axis_size("req")
    own_most = min(requests + requests // 2, owners)
    place = lax.axis_index("req").astype(jnp.int32).reshape(1)

    by_lag = jnp.transpose(conv_edge, (1, 0, 2))
    conv, partial = conv_project(
        x_in, by_lag, conv_weight, conv_bias.reshape(1, -1), x_proj_weight.T
    )
    if lax.axis_size("tp") == 2:
        partials = (partial, lax.ppermute(partial, "tp", [(0, 1), (1, 0)]))
    else:
        partials = (lax.psum(partial, "tp"),)

    def swap(rows, delta):
        return lax.ppermute(rows, "req", [(i, i ^ delta) for i in range(owners)]) if delta else rows

    groups = kept_edges((place, accepted, prompt_len, owner), x_in, by_lag, partial, owners)
    half = len(groups) // 2
    far = [swap(rows, d * PLANE) for d, rows in enumerate(groups) if d >= half]

    gains = (dt_gain.reshape(1, -1), b_gain.reshape(1, -1), c_gain.reshape(1, -1))
    bias = dt_bias.reshape(1, -1)
    state = ssm_state.reshape(requests * states, channels)
    slots = kept_states(
        (place, accepted, owner), partials, gains[:2], dt_proj_weight, bias, a_log, conv, state, owners
    )
    got = lax.all_to_all(slots, "req", split_axis=0, concat_axis=0, tiled=True)
    mixed = scan(
        partials, gains, dt_proj_weight, bias, a_log, skip.reshape(1, -1), conv, state, z_gate
    )
    mixed, owner, *near = lax.optimization_barrier((mixed, owner, *groups[:half]))
    groups = [swap(rows, d * PLANE) for d, rows in enumerate(near)] + far
    hits = jnp.any(owner.reshape(owners, requests) == place, axis=1)
    ids = np.arange(owners, dtype=np.int32)
    ranks = jnp.sum((hits[None, :] & (ids[None, :] < ids[:, None])).astype(jnp.int32), axis=1)
    starts = np.arange(PARTS + 1, dtype=np.int32) * (owners // PARTS)
    bounds = jnp.sum((hits[None, :] & (ids[None, :] < starts[:, None])).astype(jnp.int32), axis=1)
    at = hits[None, :] & (ranks[None, :] == jnp.arange(own_most, dtype=jnp.int32)[:, None])
    source = owners - jnp.sum(jnp.where(at, owners - ids[None, :], 0), axis=1)
    groups = [swap(rows, p) for p, rows in enumerate(regroup(groups, mixed))]
    owned_edge, tenant_stats = settle_edges(
        place, source, tenant_range, groups, own_most, lags, x_in.shape[0] // requests,
        requests,
    )
    owned = settle_states(source, bounds, got, own_most)
    return (mixed, owned, owned_edge, tenant_stats)


def solution(mesh):
    placed = (
        P("req", "tp"),
        P("req", "tp"),
        P("req", None, "tp"),
        P(None, "tp"),
        P("tp"),
        P("tp", None),
        P(),
        P(),
        P(),
        P(None, "tp"),
        P("tp"),
        P(None, "tp"),
        P("tp"),
        P("req", None, "tp"),
        P("req"),
        P("req"),
        P(),
        P(),
    )
    return jax.shard_map(
        per_device,
        mesh=mesh,
        in_specs=placed,
        out_specs=(P("req", "tp"), P("req", None, "tp"), P("req", None, "tp"), P()),
        check_vma=False,
    )
```

```python
import functools

import jax
import jax.numpy as jnp
import numpy as np
from jax import lax
from jax.experimental import pallas as pl
from jax.experimental.pallas import tpu as pltpu
from jax.sharding import PartitionSpec as P

EPSILON = 1e-06
SQUARE_FLOOR = 0.25
LOG2_E = 1.4426950408889634
LANES = 128
EDGE_ROWS = 4
PLANE = 4
DIGIT = 7
VMEM_BYTES = 24 * 1024 * 1024
BLOCK = 2048
PARTS = 4
ROUND = 4
VECTOR_WEIGHT = 30000


def iota(shape, axis):
    return lax.broadcasted_iota(jnp.int32, shape, axis)


def one_hot(condition):
    return jnp.where(condition, 1.0, 0.0).astype(jnp.bfloat16)


def dot(lhs, rhs):
    return jnp.dot(lhs, rhs, preferred_element_type=jnp.float32)


def in_hbm(array):
    return pltpu.with_memory_space_constraint(array, pltpu.HBM)


def silu(value):
    return value * (0.5 + 0.5 * jnp.tanh(0.5 * value))


def to_step_major(requests, steps):
    rows = requests * steps
    row, col = iota((rows, rows), 0), iota((rows, rows), 1)
    return one_hot(col == lax.rem(row, requests) * steps + lax.div(row, requests))


def to_request_major(requests, steps):
    rows = requests * steps
    row, col = iota((rows, rows), 0), iota((rows, rows), 1)
    return one_hot(row == lax.rem(col, requests) * steps + lax.div(col, requests))


def by_request(index, scalars):
    out = jnp.zeros_like(index)
    for request, scalar in enumerate(scalars):
        out = jnp.where(index == request, scalar, out)
    return out


def conv_kernel(
    x_hbm, edge_hbm, weight_hbm, bias_hbm, proj_hbm, conv_hbm, partial_ref,
    x_ref, edge_ref, weight_ref, bias_ref, proj_ref, conv_ref, sems, out_sems,
):
    lags, requests, channels = edge_ref.shape
    taps = weight_ref.shape[0]
    steps = x_ref.shape[0] // requests
    block = min(BLOCK, channels)
    pieces = [slice(c, c + block) for c in range(0, channels, block)]
    pairs = [(weight_hbm, weight_ref), (bias_hbm, bias_ref), (edge_hbm, edge_ref)]
    pairs += [(x_hbm.at[:, piece], x_ref.at[:, piece]) for piece in pieces]
    pairs.append((proj_hbm, proj_ref))
    copies = [pltpu.make_async_copy(*pair, sems.at[i]) for i, pair in enumerate(pairs)]
    for copy in copies:
        copy.start()
    results = [
        pltpu.make_async_copy(conv_ref.at[:, piece], conv_hbm.at[:, piece], out_sems.at[i])
        for i, piece in enumerate(pieces)
    ]
    order = to_step_major(requests, steps)
    for copy in copies[:3]:
        copy.wait()
    for i, piece in enumerate(pieces):
        copies[3 + i].wait()
        stream = dot(order, x_ref[:, piece])
        window = [edge_ref[k, :, piece].astype(jnp.float32) for k in range(lags)]
        window += [stream[t * requests : (t + 1) * requests] for t in range(steps)]
        weight = [weight_ref[k : k + 1, piece] for k in range(taps)]
        outs = []
        for t in range(steps):
            added = bias_ref[:, piece] + weight[0] * window[t]
            for k in range(1, taps):
                added = added + weight[k] * window[t + k]
            outs.append(silu(added))
        conv_ref[:, piece] = jnp.concatenate(outs, axis=0).astype(jnp.bfloat16)
        results[i].start()
    copies[-1].wait()
    partial_ref[...] = lax.dot_general(
        proj_ref[...], conv_ref[...], (((1,), (1,)), ((), ())), preferred_element_type=jnp.float32
    )
    for result in results:
        result.wait()


def conv_project(x_in, conv_edge, conv_weight, conv_bias, proj):
    rows, channels = x_in.shape
    operands = (x_in, conv_edge, conv_weight, conv_bias, proj)
    pieces = channels // min(BLOCK, channels)
    return pl.pallas_call(
        conv_kernel,
        in_specs=[pl.BlockSpec(memory_space=pl.ANY)] * len(operands),
        out_specs=[pl.BlockSpec(memory_space=pl.ANY), pl.BlockSpec(memory_space=pltpu.VMEM)],
        out_shape=[
            pltpu.HBM((rows, channels), jnp.bfloat16),
            pltpu.HBM((proj.shape[0], rows), jnp.float32),
        ],
        scratch_shapes=[pltpu.VMEM(a.shape, a.dtype) for a in operands]
        + [
            pltpu.VMEM((rows, channels), jnp.bfloat16),
            pltpu.SemaphoreType.DMA((4 + pieces,)),
            pltpu.SemaphoreType.DMA((pieces,)),
        ],
        compiler_params=pltpu.CompilerParams(vmem_limit_bytes=VMEM_BYTES),
        name="conv_project",
    )(*(in_hbm(a) for a in operands))


def kept_edge_kernel(
    place_ref, accepted_ref, length_ref, owner_ref, x_ref, edge_ref, _, *group_refs
):
    lags, requests, block = edge_ref.shape
    steps = x_ref.shape[0] // requests
    place = place_ref[0]
    accepted = [accepted_ref[r] for r in range(requests)]
    lengths = [length_ref[r] + accepted[r] + 1 for r in range(requests)]
    deltas = [owner_ref[place * requests + r] ^ place for r in range(requests)]
    height = len(group_refs) * PLANE * EDGE_ROWS
    slot = lax.div(iota((height, 1), 0), EDGE_ROWS)
    lag = lax.rem(iota((height, 1), 0), EDGE_ROWS)

    def pick(request, position):
        return one_hot(
            (slot == by_request(request, deltas))
            & (position - by_request(request, accepted) == lag)
            & (lag < lags)
        )

    col = iota((1, requests * steps), 1)
    picked = dot(pick(lax.div(col, steps), lax.rem(col, steps) + lags), x_ref[...])
    col = iota((1, lags * requests), 1)
    edge = jnp.concatenate([edge_ref[k].astype(jnp.float32) for k in range(lags)], axis=0)
    picked += dot(pick(lax.rem(col, requests), lax.div(col, requests)), edge.astype(jnp.bfloat16))
    low = [length & ((1 << DIGIT) - 1) for length in lengths]
    high = [length >> DIGIT for length in lengths]
    numbers = by_request(iota((1, block), 1), accepted + low + high).astype(jnp.float32)
    picked = jnp.where(lag == lags, numbers, picked).astype(jnp.bfloat16)
    group = PLANE * EDGE_ROWS
    for d, ref in enumerate(group_refs):
        ref[...] = picked[d * group : (d + 1) * group]


def kept_edges(scalars, x_in, conv_edge, after, owners):
    channels = x_in.shape[1]
    groups = owners // PLANE
    vmem = pl.BlockSpec(memory_space=pltpu.VMEM)
    return pl.pallas_call(
        kept_edge_kernel,
        in_specs=[pl.BlockSpec(memory_space=pltpu.SMEM)] * len(scalars)
        + [vmem, vmem, pl.BlockSpec(memory_space=pl.ANY)],
        out_specs=[vmem] * groups,
        out_shape=[pltpu.HBM((PLANE * EDGE_ROWS, channels), jnp.bfloat16)] * groups,
        compiler_params=pltpu.CompilerParams(vmem_limit_bytes=VMEM_BYTES),
        name="kept_edges",
    )(*scalars, x_in, conv_edge, in_hbm(after))


def hold_kernel(rows_ref, _, out_ref):
    out_ref[...] = rows_ref[...]


def hold(rows, after):
    vmem = pl.BlockSpec(memory_space=pltpu.VMEM)
    return pl.pallas_call(
        hold_kernel,
        in_specs=[vmem, pl.BlockSpec(memory_space=pl.ANY)],
        out_specs=vmem,
        out_shape=pltpu.HBM(rows.shape, rows.dtype),
        compiler_params=pltpu.CompilerParams(vmem_limit_bytes=VMEM_BYTES),
        name="hold",
    )(rows, in_hbm(after))


def regroup_kernel(*refs):
    groups = len(refs) - 1 - PLANE
    rows = jnp.concatenate([ref[...].astype(jnp.float32) for ref in refs[:groups]], axis=0)
    for p, out_ref in enumerate(refs[-PLANE:]):
        parts = [
            rows[(d * PLANE + p) * EDGE_ROWS : (d * PLANE + p + 1) * EDGE_ROWS] for d in range(groups)
        ]
        out_ref[...] = jnp.concatenate(parts, axis=0).astype(jnp.bfloat16)


def regroup(arrived, after):
    rows, channels = arrived[0].shape
    block = min(1024, channels)
    height = len(arrived) * EDGE_ROWS
    return pl.pallas_call(
        regroup_kernel,
        grid=(channels // block,),
        in_specs=[pl.BlockSpec((rows, block), lambda j: (0, j))] * len(arrived)
        + [pl.BlockSpec(memory_space=pl.ANY)],
        out_specs=[pl.BlockSpec((height, block), lambda j: (0, j))] * PLANE,
        out_shape=[pltpu.HBM((height, channels), jnp.bfloat16)] * PLANE,
        compiler_params=pltpu.CompilerParams(
            dimension_semantics=("arbitrary",), vmem_limit_bytes=VMEM_BYTES
        ),
        name="regroup",
    )(*arrived, in_hbm(after))


def column(row):
    count = row.shape[1]
    same = iota((count, count), 0) == iota((count, count), 1)
    return jnp.sum(jnp.where(same, row, 0.0), axis=1, keepdims=True)


def normal(values, floor_value, eps_value):
    square = jnp.mean(values * values, axis=0, keepdims=True)
    return values * lax.rsqrt(jnp.maximum(square, floor_value) + eps_value)


def low_rank(total, gain):
    low = jnp.transpose(normal(total[: gain.shape[1]], 0.0, EPSILON))
    return (low * gain).astype(jnp.bfloat16)


def state_map(values, gain):
    return (normal(values, SQUARE_FLOOR, 0.0) * column(gain)).astype(jnp.bfloat16)


def summed(part_refs):
    total = part_refs[0][...]
    for part in part_refs[1:]:
        total = total + part[...]
    return total


def softplus(raw):
    return jnp.maximum(raw, 0.0) + jnp.log1p(jnp.exp(-jnp.abs(raw)))


def kept_kernel(parts, *refs):
    place_ref, accepted_ref, owner_ref = refs[:3]
    (
        dt_gain_ref, b_gain_ref, dt_weight_ref, dt_bias_ref, a_log_hbm, conv_hbm, state_hbm,
        slot_ref, part_ref, a_log_ref, conv_ref, state_ref, in_ref, size_ref, drive_ref, rate_ref, new_ref,
        in_sems, sems,
    ) = refs[3 + parts :]
    pairs = ((refs[3], part_ref), (a_log_hbm, a_log_ref), (conv_hbm, conv_ref), (state_hbm, state_ref))
    copies = [pltpu.make_async_copy(*pair, in_sems.at[i]) for i, pair in enumerate(pairs)]
    for copy in copies:
        copy.start()
    rank, states = dt_gain_ref.shape[1], b_gain_ref.shape[1]
    requests = accepted_ref.shape[0]
    rows, channels = conv_ref.shape
    steps = rows // requests
    span = min(2048, channels)
    halves = states // 8

    copies[0].wait()
    total = part_ref[...]
    for part in refs[4 : 3 + parts]:
        total = total + part[...]
    turned = state_map(total[rank : rank + states], b_gain_ref[...]).astype(jnp.float32)
    for row in range(rows):
        t, r = divmod(row, requests)
        in_ref[r * states : (r + 1) * states, t * LANES : (t + 1) * LANES] = jnp.broadcast_to(
            turned[:, row : row + 1], (states, LANES)
        )

    low = low_rank(total, dt_gain_ref[...])
    row = iota((rows, 1), 0)
    live = lax.div(row, requests) < by_request(
        lax.rem(row, requests), [accepted_ref[r] for r in range(requests)]
    )
    copies[1].wait()
    copies[2].wait()
    for first in range(0, channels, span):
        piece = slice(first, first + span)
        size = softplus(dot(low, dt_weight_ref[:, piece]) + dt_bias_ref[:, piece])
        size = jnp.where(live, size, 0.0)
        drive = size * conv_ref[:, piece].astype(jnp.float32)
        for c in range(span // LANES):
            tile = slice(c * LANES, (c + 1) * LANES)
            size_ref[first // LANES + c, :rows, :] = size[:, tile]
            drive_ref[first // LANES + c, :rows, :] = drive[:, tile]
        rate_ref[:, piece] = jnp.exp(a_log_ref[:, piece]) * (-LOG2_E)

    def one_request(r, carry):
        own = pl.multiple_of(r * states, states)
        rounds = lax.div(accepted_ref[r] + (ROUND - 1), ROUND)

        def one_span(part, inner):
            tiles = [pl.multiple_of(part * span + c, LANES) for c in range(0, span, LANES)]

            rates = [
                [rate_ref[8 * h : 8 * (h + 1), pl.ds(tile, LANES)] for tile in tiles]
                for h in range(halves)
            ]

            def one_round(i, hidden):
                hidden = [list(h) for h in hidden]
                for u in range(ROUND):
                    t = i * ROUND + u
                    at = pl.ds(t * requests + r, 8, stride=0)
                    lanes = pl.ds(pl.multiple_of(t * LANES, LANES), LANES)
                    b = [in_ref[pl.ds(own + 8 * h, 8), lanes] for h in range(halves)]
                    for c, tile in enumerate(tiles):
                        place = part * (span // LANES) + c
                        now, drive = size_ref[place, at, :], drive_ref[place, at, :]
                        for h in range(halves):
                            decay = jnp.exp2(now * rates[h][c])
                            hidden[h][c] = decay * hidden[h][c] + drive * b[h]
                return tuple(tuple(h) for h in hidden)

            lanes = pl.ds(pl.multiple_of(part * span, span), span)
            old = state_ref[pl.ds(own, states), lanes].astype(jnp.float32)
            start = tuple(
                tuple(
                    old[8 * h : 8 * (h + 1), c * LANES : (c + 1) * LANES] for c in range(len(tiles))
                )
                for h in range(halves)
            )
            done = lax.fori_loop(0, rounds, one_round, start)
            new = jnp.concatenate([jnp.concatenate(h, axis=1) for h in done], axis=0)
            new_ref[r, :, lanes] = new.astype(jnp.bfloat16)
            return inner

        lax.fori_loop(0, channels // span, one_span, 0)
        slot = owner_ref[place_ref[0] * requests + r]
        pltpu.make_async_copy(new_ref.at[r], slot_ref.at[slot], sems.at[r]).start()
        return carry

    copies[3].wait()
    lax.fori_loop(0, requests, one_request, 0)
    for r in range(requests):
        slot = owner_ref[place_ref[0] * requests + r]
        pltpu.make_async_copy(new_ref.at[r], slot_ref.at[slot], sems.at[r]).wait()


def kept_states(scalars, partials, gains, dt_weight, dt_bias, a_log, conv, state, slots):
    rows, channels = conv.shape
    states, rank = a_log.shape[0], dt_weight.shape[0]
    requests = scalars[1].shape[0]
    near = [*partials[1:], *gains, dt_weight, dt_bias]
    far = [in_hbm(a_log), in_hbm(conv), in_hbm(state)]
    anywhere = pl.BlockSpec(memory_space=pl.ANY)
    return pl.pallas_call(
        functools.partial(kept_kernel, len(partials)),
        in_specs=[pl.BlockSpec(memory_space=pltpu.SMEM)] * len(scalars)
        + [anywhere]
        + [pl.BlockSpec(memory_space=pltpu.VMEM)] * len(near)
        + [anywhere] * len(far),
        out_specs=anywhere,
        out_shape=pltpu.HBM((slots, states, channels), jnp.bfloat16),
        scratch_shapes=[
            pltpu.VMEM(partials[0].shape, jnp.float32),
            pltpu.VMEM(a_log.shape, jnp.float32),
            pltpu.VMEM(conv.shape, jnp.bfloat16),
            pltpu.VMEM(state.shape, jnp.bfloat16),
            pltpu.VMEM((requests * states, rows // requests * LANES), jnp.float32),
            pltpu.VMEM((channels // LANES, rows + 8, LANES), jnp.float32),
            pltpu.VMEM((channels // LANES, rows + 8, LANES), jnp.float32),
            pltpu.VMEM((states, channels), jnp.float32),
            pltpu.VMEM((requests, states, channels), jnp.bfloat16),
            pltpu.SemaphoreType.DMA((1 + len(far),)),
            pltpu.SemaphoreType.DMA((requests,)),
        ],
        compiler_params=pltpu.CompilerParams(vmem_limit_bytes=VMEM_BYTES),
        cost_estimate=pl.CostEstimate(
            flops=VECTOR_WEIGHT * 4 * rows * states * channels,
            transcendentals=rows * states * channels,
            bytes_accessed=2 * channels * (rows + rank + states * (requests + slots)),
        ),
        name="kept_states",
    )(*scalars, in_hbm(partials[0]), *near, *far)


def scan_kernel(parts, *refs):
    (
        dt_gain_ref, b_gain_ref, c_gain_ref, dt_weight_ref, dt_bias_ref, a_log_ref, skip_ref,
        conv_ref, state_ref, z_ref, mixed_ref,
        low_ref, in_ref, out_ref, size_ref, drive_ref, rate_ref, start_ref, sum_ref,
    ) = refs[parts:]
    rank, states = dt_gain_ref.shape[1], b_gain_ref.shape[1]
    rows, block = conv_ref.shape
    requests = state_ref.shape[0] // states
    steps = rows // requests

    @pl.when(pl.program_id(0) == 0)
    def _():
        total = summed(refs[:parts])
        low_ref[...] = low_rank(total, dt_gain_ref[...])
        in_map = state_map(total[rank : rank + states], b_gain_ref[...])
        out_map = state_map(total[rank + states :], c_gain_ref[...])
        wide = states * LANES
        spread = one_hot(lax.div(iota((states, wide), 1), LANES) == iota((states, wide), 0))
        turn = (((0,), (0,)), ((), ()))
        in_ref[...] = lax.dot_general(in_map, spread, turn, preferred_element_type=jnp.float32)
        out_ref[...] = lax.dot_general(out_map, spread, turn, preferred_element_type=jnp.float32)

    conv = conv_ref[...].astype(jnp.float32)
    size = softplus(dot(low_ref[...], dt_weight_ref[...]) + dt_bias_ref[...])
    size_ref[...] = size
    drive_ref[...] = size * conv
    start_ref[...] = dot(to_step_major(requests, states), state_ref[...])
    rate = jnp.exp(a_log_ref[...]) * (-LOG2_E)
    for n in range(states):
        rate_ref[n * requests : (n + 1) * requests, :] = jnp.broadcast_to(
            rate[n : n + 1, :], (requests, block)
        )

    pair = 2 if block % (2 * LANES) == 0 else 1

    def columns(c, carry):
        spans = [pl.ds(pl.multiple_of((c * pair + i) * LANES, LANES), LANES) for i in range(pair)]
        start = tuple(
            tuple(start_ref[n * requests : (n + 1) * requests, s] for s in spans)
            for n in range(states)
        )

        def step(t, hidden):
            at = pl.ds(pl.multiple_of(t * requests, requests), requests)
            sizes = [size_ref[at, s] for s in spans]
            drives = [drive_ref[at, s] for s in spans]
            sums = [None] * pair
            new = []
            for n in range(states):
                b = in_ref[at, n * LANES : (n + 1) * LANES]
                c_map = out_ref[at, n * LANES : (n + 1) * LANES]
                own = slice(n * requests, (n + 1) * requests)
                mine = []
                for i, s in enumerate(spans):
                    h = jnp.exp2(sizes[i] * rate_ref[own, s]) * hidden[n][i] + drives[i] * b
                    term = c_map * h
                    sums[i] = term if sums[i] is None else sums[i] + term
                    mine.append(h)
                new.append(tuple(mine))
            for i, s in enumerate(spans):
                sum_ref[at, s] = sums[i]
            return tuple(new)

        lax.fori_loop(0, steps, step, start, unroll=2)
        return carry

    lax.fori_loop(0, block // (pair * LANES), columns, 0)

    gate = silu(dot(to_step_major(requests, steps), z_ref[...]))
    mixed = ((sum_ref[...] + skip_ref[...] * conv) * gate).astype(jnp.bfloat16)
    mixed_ref[...] = dot(to_request_major(requests, steps), mixed).astype(jnp.bfloat16)


def scan(partials, gains, dt_weight, dt_bias, a_log, skip, conv, state, z_gate):
    rows, channels = conv.shape
    states, rank = a_log.shape[0], dt_weight.shape[0]
    block = min(512, channels)

    def whole(array):
        return pl.BlockSpec(array.shape, lambda j: (0, 0))

    wide = [in_hbm(dt_weight), dt_bias, in_hbm(a_log), skip, in_hbm(conv), in_hbm(state), in_hbm(z_gate)]
    tall = pltpu.VMEM((rows, block), jnp.float32)
    table = pltpu.VMEM((rows, states * LANES), jnp.float32)
    return pl.pallas_call(
        functools.partial(scan_kernel, len(partials)),
        grid=(channels // block,),
        in_specs=[whole(a) for a in (*partials, *gains)]
        + [pl.BlockSpec((a.shape[0], block), lambda j: (0, j)) for a in wide],
        out_specs=pl.BlockSpec((rows, block), lambda j: (0, j)),
        out_shape=jax.ShapeDtypeStruct((rows, channels), jnp.bfloat16),
        scratch_shapes=[
            pltpu.VMEM((rows, rank), jnp.bfloat16), table, table, tall, tall,
            pltpu.VMEM((state.shape[0], block), jnp.float32),
            pltpu.VMEM((state.shape[0], block), jnp.float32),
            tall,
        ],
        compiler_params=pltpu.CompilerParams(
            dimension_semantics=("arbitrary",), vmem_limit_bytes=VMEM_BYTES
        ),
        cost_estimate=pl.CostEstimate(
            flops=VECTOR_WEIGHT * 8 * rows * states * channels,
            transcendentals=rows * states * channels,
            bytes_accessed=2 * channels * (3 * rows + rank),
        ),
        name="scan",
    )(*partials, *gains, *wide)


def edge_kernel(steps, requests, place_ref, source_ref, range_ref, *refs):
    group_refs, edge_ref, stats_ref = refs[:-2], refs[-2], refs[-1]
    own_most, lags, block = edge_ref.shape
    groups = group_refs[0].shape[0] // EDGE_ROWS
    height = len(group_refs) * groups * EDGE_ROWS
    place = place_ref[0]

    def sender(index):
        p, d = lax.div(index, groups * EDGE_ROWS), lax.rem(lax.div(index, EDGE_ROWS), groups)
        return (d * PLANE + p) ^ place

    got = jnp.concatenate([ref[...] for ref in group_refs], axis=0)
    row, col = iota((own_most * 8, 1), 0), iota((1, height), 1)
    wanted = jnp.full((own_most * 8, 1), -1, jnp.int32)
    for i in range(own_most):
        wanted = jnp.where(lax.div(row, 8) == i, source_ref[i], wanted)
    pick = (sender(col) == wanted) & (lax.rem(col, EDGE_ROWS) == lax.rem(row, 8))
    picked = dot(one_hot(pick), got)
    for i in range(own_most):
        edge_ref[i] = picked[i * 8 : i * 8 + lags].astype(jnp.bfloat16)

    @pl.when(pl.program_id(0) == 0)
    def _():
        numbers = got[:, :LANES].astype(jnp.float32)
        row, lane = iota((height, LANES), 0), iota((height, LANES), 1)
        mine = lax.rem(row, EDGE_ROWS) == lags
        request = sender(row) * requests + lax.rem(lane, requests)
        digit = lax.div(lane, requests)
        counts = jnp.where(digit == 0, numbers, 0.0)
        lengths = jnp.where(digit == 1, numbers, 0.0) + jnp.where(
            digit == 2, numbers * float(1 << DIGIT), 0.0
        )
        tenants = range_ref.shape[0]
        sums, loads, members = [], [], []
        for k in range(tenants):
            start, end = range_ref[k, 0], range_ref[k, 1]
            inside = mine & (request >= start) & (request < end)
            sums.append(jnp.sum(jnp.where(inside, counts, 0.0), keepdims=True))
            loads.append(jnp.sum(jnp.where(inside, lengths, 0.0), keepdims=True))
            members.append((jnp.zeros((1, 1), jnp.int32) + (end - start)).astype(jnp.float32))
        mean = sum(loads[1:], loads[0]) / sum(members[1:], members[0])
        out = jnp.zeros((tenants, 2), jnp.float32)
        row, col = iota((tenants, 2), 0), iota((tenants, 2), 1)
        for k in range(tenants):
            rate = sums[k] / (float(steps) * members[k])
            load = loads[k] / members[k] / mean
            out = jnp.where(row == k, jnp.where(col == 0, rate, load), out)
        stats_ref[...] = out


def settle_edges(place, source, tenant_range, got, own_most, lags, steps, requests):
    smem = pl.BlockSpec(memory_space=pltpu.SMEM)
    height, channels = got[0].shape
    block = min(2048, channels)
    stats = (tenant_range.shape[0], 2)
    return pl.pallas_call(
        functools.partial(edge_kernel, steps, requests),
        grid=(channels // block,),
        in_specs=[smem] * 3 + [pl.BlockSpec((height, block), lambda j: (0, j))] * len(got),
        out_specs=[
            pl.BlockSpec((own_most, lags, block), lambda j: (0, 0, j)),
            pl.BlockSpec(stats, lambda j: (0, 0)),
        ],
        out_shape=[
            jax.ShapeDtypeStruct((own_most, lags, channels), jnp.bfloat16),
            jax.ShapeDtypeStruct(stats, jnp.float32),
        ],
        compiler_params=pltpu.CompilerParams(
            dimension_semantics=("arbitrary",), vmem_limit_bytes=VMEM_BYTES
        ),
        name="settle_edges",
    )(place, source, tenant_range, *got)


def settle_kernel(source_ref, bound_ref, got_hbm, owned_hbm, rows_ref, in_sems, sems):
    slots, own_most = got_hbm.shape[0], owned_hbm.shape[0]
    size = slots // PARTS
    parts = [slice(q * size, (q + 1) * size) for q in range(PARTS)]
    fetches = [
        pltpu.make_async_copy(got_hbm.at[part], rows_ref.at[part], in_sems.at[q])
        for q, part in enumerate(parts)
    ]
    for fetch in fetches:
        fetch.start()
    rows_ref[slots] = jnp.zeros(rows_ref.shape[1:], rows_ref.dtype)

    def put(i):
        return pltpu.make_async_copy(rows_ref.at[source_ref[i]], owned_hbm.at[i], sems.at[i])

    def start(i, carry):
        put(i).start()
        return carry

    lax.fori_loop(bound_ref[PARTS], own_most, start, 0)
    for q, fetch in enumerate(fetches):
        fetch.wait()
        lax.fori_loop(bound_ref[q], bound_ref[q + 1], start, 0)
    for i in range(own_most):
        put(i).wait()


def settle_states(source, bounds, got, own_most):
    smem = pl.BlockSpec(memory_space=pltpu.SMEM)
    anywhere = pl.BlockSpec(memory_space=pl.ANY)
    slots, *rest = got.shape
    return pl.pallas_call(
        settle_kernel,
        in_specs=[smem, smem, anywhere],
        out_specs=anywhere,
        out_shape=pltpu.HBM((own_most, *rest), got.dtype),
        scratch_shapes=[
            pltpu.VMEM((slots + 1, *rest), got.dtype),
            pltpu.SemaphoreType.DMA((PARTS,)),
            pltpu.SemaphoreType.DMA((own_most,)),
        ],
        compiler_params=pltpu.CompilerParams(vmem_limit_bytes=VMEM_BYTES),
        name="settle_states",
    )(source, bounds, in_hbm(got))


def per_device(
    x_in, z_gate, conv_edge, conv_weight, conv_bias, x_proj_weight, dt_gain, b_gain, c_gain,
    dt_proj_weight, dt_bias, a_log, skip, ssm_state, accepted, prompt_len, tenant_range, owner,
):
    requests, states, channels = ssm_state.shape
    lags = conv_edge.shape[1]
    owners = lax.axis_size("req")
    own_most = min(requests + requests // 2, owners)
    place = lax.axis_index("req").astype(jnp.int32).reshape(1)

    by_lag = jnp.transpose(conv_edge, (1, 0, 2))
    conv, partial = conv_project(
        x_in, by_lag, conv_weight, conv_bias.reshape(1, -1), x_proj_weight.T
    )
    if lax.axis_size("tp") == 2:
        partials = (partial, lax.ppermute(partial, "tp", [(0, 1), (1, 0)]))
    else:
        partials = (lax.psum(partial, "tp"),)

    def swap(rows, delta):
        return lax.ppermute(rows, "req", [(i, i ^ delta) for i in range(owners)]) if delta else rows

    groups = kept_edges((place, accepted, prompt_len, owner), x_in, by_lag, partial, owners)
    half = len(groups) // 2
    far = [swap(rows, d * PLANE) for d, rows in enumerate(groups) if d >= half]

    gains = (dt_gain.reshape(1, -1), b_gain.reshape(1, -1), c_gain.reshape(1, -1))
    bias = dt_bias.reshape(1, -1)
    state = ssm_state.reshape(requests * states, channels)
    slots = kept_states(
        (place, accepted, owner), partials, gains[:2], dt_proj_weight, bias, a_log, conv, state, owners
    )
    near = [hold(rows, slots) if d else rows for d, rows in enumerate(groups[:half])]
    got = lax.all_to_all(slots, "req", split_axis=0, concat_axis=0, tiled=True)
    groups = [swap(rows, d * PLANE) for d, rows in enumerate(near)] + far
    mixed = scan(
        partials, gains, dt_proj_weight, bias, a_log, skip.reshape(1, -1), conv, state, z_gate
    )
    mixed, owner = lax.optimization_barrier((mixed, owner))
    hits = jnp.any(owner.reshape(owners, requests) == place, axis=1)
    ids = np.arange(owners, dtype=np.int32)
    ranks = jnp.sum((hits[None, :] & (ids[None, :] < ids[:, None])).astype(jnp.int32), axis=1)
    starts = np.arange(PARTS + 1, dtype=np.int32) * (owners // PARTS)
    bounds = jnp.sum((hits[None, :] & (ids[None, :] < starts[:, None])).astype(jnp.int32), axis=1)
    at = hits[None, :] & (ranks[None, :] == jnp.arange(own_most, dtype=jnp.int32)[:, None])
    source = owners - jnp.sum(jnp.where(at, owners - ids[None, :], 0), axis=1)
    groups = [swap(rows, p) for p, rows in enumerate(regroup(groups, mixed))]
    owned_edge, tenant_stats = settle_edges(
        place, source, tenant_range, groups, own_most, lags, x_in.shape[0] // requests,
        requests,
    )
    owned = settle_states(source, bounds, got, own_most)
    return (mixed, owned, owned_edge, tenant_stats)


def solution(mesh):
    placed = (
        P("req", "tp"),
        P("req", "tp"),
        P("req", None, "tp"),
        P(None, "tp"),
        P("tp"),
        P("tp", None),
        P(),
        P(),
        P(),
        P(None, "tp"),
        P("tp"),
        P(None, "tp"),
        P("tp"),
        P("req", None, "tp"),
        P("req"),
        P("req"),
        P(),
        P(),
    )
    return jax.shard_map(
        per_device,
        mesh=mesh,
        in_specs=placed,
        out_specs=(P("req", "tp"), P("req", None, "tp"), P("req", None, "tp"), P()),
        check_vma=False,
    )
```

```python
import functools

import jax
import jax.numpy as jnp
import numpy as np
from jax import lax
from jax.experimental import pallas as pl
from jax.experimental.pallas import tpu as pltpu
from jax.sharding import PartitionSpec as P

EPSILON = 1e-06
SQUARE_FLOOR = 0.25
LOG2_E = 1.4426950408889634
LANES = 128
EDGE_ROWS = 4
PLANE = 4
DIGIT = 7
VMEM_BYTES = 24 * 1024 * 1024
BLOCK = 2048
PARTS = 4
ROUND = 4
VECTOR_WEIGHT = 30000


def iota(shape, axis):
    return lax.broadcasted_iota(jnp.int32, shape, axis)


def one_hot(condition):
    return jnp.where(condition, 1.0, 0.0).astype(jnp.bfloat16)


def dot(lhs, rhs):
    return jnp.dot(lhs, rhs, preferred_element_type=jnp.float32)


def in_hbm(array):
    return pltpu.with_memory_space_constraint(array, pltpu.HBM)


def silu(value):
    return value * (0.5 + 0.5 * jnp.tanh(0.5 * value))


def to_step_major(requests, steps):
    rows = requests * steps
    row, col = iota((rows, rows), 0), iota((rows, rows), 1)
    return one_hot(col == lax.rem(row, requests) * steps + lax.div(row, requests))


def to_request_major(requests, steps):
    rows = requests * steps
    row, col = iota((rows, rows), 0), iota((rows, rows), 1)
    return one_hot(row == lax.rem(col, requests) * steps + lax.div(col, requests))


def by_request(index, scalars):
    out = jnp.zeros_like(index)
    for request, scalar in enumerate(scalars):
        out = jnp.where(index == request, scalar, out)
    return out


def conv_kernel(
    x_hbm, edge_hbm, weight_hbm, bias_hbm, proj_hbm, conv_hbm, partial_ref,
    x_ref, edge_ref, weight_ref, bias_ref, proj_ref, conv_ref, sems, out_sems,
):
    lags, requests, channels = edge_ref.shape
    taps = weight_ref.shape[0]
    steps = x_ref.shape[0] // requests
    block = min(BLOCK, channels)
    pieces = [slice(c, c + block) for c in range(0, channels, block)]
    pairs = [(weight_hbm, weight_ref), (bias_hbm, bias_ref), (edge_hbm, edge_ref)]
    pairs += [(x_hbm.at[:, piece], x_ref.at[:, piece]) for piece in pieces]
    pairs.append((proj_hbm, proj_ref))
    copies = [pltpu.make_async_copy(*pair, sems.at[i]) for i, pair in enumerate(pairs)]
    for copy in copies:
        copy.start()
    results = [
        pltpu.make_async_copy(conv_ref.at[:, piece], conv_hbm.at[:, piece], out_sems.at[i])
        for i, piece in enumerate(pieces)
    ]
    order = to_step_major(requests, steps)
    for copy in copies[:3]:
        copy.wait()
    for i, piece in enumerate(pieces):
        copies[3 + i].wait()
        stream = dot(order, x_ref[:, piece])
        window = [edge_ref[k, :, piece].astype(jnp.float32) for k in range(lags)]
        window += [stream[t * requests : (t + 1) * requests] for t in range(steps)]
        weight = [weight_ref[k : k + 1, piece] for k in range(taps)]
        outs = []
        for t in range(steps):
            added = bias_ref[:, piece] + weight[0] * window[t]
            for k in range(1, taps):
                added = added + weight[k] * window[t + k]
            outs.append(silu(added))
        conv_ref[:, piece] = jnp.concatenate(outs, axis=0).astype(jnp.bfloat16)
        results[i].start()
    copies[-1].wait()
    partial_ref[...] = lax.dot_general(
        proj_ref[...], conv_ref[...], (((1,), (1,)), ((), ())), preferred_element_type=jnp.float32
    )
    for result in results:
        result.wait()


def conv_project(x_in, conv_edge, conv_weight, conv_bias, proj):
    rows, channels = x_in.shape
    operands = (x_in, conv_edge, conv_weight, conv_bias, proj)
    pieces = channels // min(BLOCK, channels)
    return pl.pallas_call(
        conv_kernel,
        in_specs=[pl.BlockSpec(memory_space=pl.ANY)] * len(operands),
        out_specs=[pl.BlockSpec(memory_space=pl.ANY), pl.BlockSpec(memory_space=pltpu.VMEM)],
        out_shape=[
            pltpu.HBM((rows, channels), jnp.bfloat16),
            pltpu.HBM((proj.shape[0], rows), jnp.float32),
        ],
        scratch_shapes=[pltpu.VMEM(a.shape, a.dtype) for a in operands]
        + [
            pltpu.VMEM((rows, channels), jnp.bfloat16),
            pltpu.SemaphoreType.DMA((4 + pieces,)),
            pltpu.SemaphoreType.DMA((pieces,)),
        ],
        compiler_params=pltpu.CompilerParams(vmem_limit_bytes=VMEM_BYTES),
        name="conv_project",
    )(*(in_hbm(a) for a in operands))


def kept_edge_kernel(
    place_ref, accepted_ref, length_ref, owner_ref, x_ref, edge_ref, _, *group_refs
):
    lags, requests, block = edge_ref.shape
    steps = x_ref.shape[0] // requests
    place = place_ref[0]
    accepted = [accepted_ref[r] for r in range(requests)]
    lengths = [length_ref[r] + accepted[r] + 1 for r in range(requests)]
    deltas = [owner_ref[place * requests + r] ^ place for r in range(requests)]
    height = len(group_refs) * PLANE * EDGE_ROWS
    slot = lax.div(iota((height, 1), 0), EDGE_ROWS)
    lag = lax.rem(iota((height, 1), 0), EDGE_ROWS)

    def pick(request, position):
        return one_hot(
            (slot == by_request(request, deltas))
            & (position - by_request(request, accepted) == lag)
            & (lag < lags)
        )

    col = iota((1, requests * steps), 1)
    picked = dot(pick(lax.div(col, steps), lax.rem(col, steps) + lags), x_ref[...])
    col = iota((1, lags * requests), 1)
    edge = jnp.concatenate([edge_ref[k].astype(jnp.float32) for k in range(lags)], axis=0)
    picked += dot(pick(lax.rem(col, requests), lax.div(col, requests)), edge.astype(jnp.bfloat16))
    low = [length & ((1 << DIGIT) - 1) for length in lengths]
    high = [length >> DIGIT for length in lengths]
    numbers = by_request(iota((1, block), 1), accepted + low + high).astype(jnp.float32)
    picked = jnp.where(lag == lags, numbers, picked).astype(jnp.bfloat16)
    group = PLANE * EDGE_ROWS
    for d, ref in enumerate(group_refs):
        ref[...] = picked[d * group : (d + 1) * group]


def kept_edges(scalars, x_in, conv_edge, after, owners):
    channels = x_in.shape[1]
    groups = owners // PLANE
    vmem = pl.BlockSpec(memory_space=pltpu.VMEM)
    return pl.pallas_call(
        kept_edge_kernel,
        in_specs=[pl.BlockSpec(memory_space=pltpu.SMEM)] * len(scalars)
        + [vmem, vmem, pl.BlockSpec(memory_space=pl.ANY)],
        out_specs=[vmem] * groups,
        out_shape=[pltpu.HBM((PLANE * EDGE_ROWS, channels), jnp.bfloat16)] * groups,
        compiler_params=pltpu.CompilerParams(vmem_limit_bytes=VMEM_BYTES),
        name="kept_edges",
    )(*scalars, x_in, conv_edge, in_hbm(after))


def regroup_kernel(*refs):
    groups = len(refs) - 1 - PLANE
    rows = jnp.concatenate([ref[...].astype(jnp.float32) for ref in refs[:groups]], axis=0)
    for p, out_ref in enumerate(refs[-PLANE:]):
        parts = [
            rows[(d * PLANE + p) * EDGE_ROWS : (d * PLANE + p + 1) * EDGE_ROWS] for d in range(groups)
        ]
        out_ref[...] = jnp.concatenate(parts, axis=0).astype(jnp.bfloat16)


def regroup(arrived, after):
    rows, channels = arrived[0].shape
    block = min(1024, channels)
    height = len(arrived) * EDGE_ROWS
    return pl.pallas_call(
        regroup_kernel,
        grid=(channels // block,),
        in_specs=[pl.BlockSpec((rows, block), lambda j: (0, j))] * len(arrived)
        + [pl.BlockSpec(memory_space=pl.ANY)],
        out_specs=[pl.BlockSpec((height, block), lambda j: (0, j))] * PLANE,
        out_shape=[pltpu.HBM((height, channels), jnp.bfloat16)] * PLANE,
        compiler_params=pltpu.CompilerParams(
            dimension_semantics=("arbitrary",), vmem_limit_bytes=VMEM_BYTES
        ),
        name="regroup",
    )(*arrived, in_hbm(after))


def column(row):
    count = row.shape[1]
    same = iota((count, count), 0) == iota((count, count), 1)
    return jnp.sum(jnp.where(same, row, 0.0), axis=1, keepdims=True)


def normal(values, floor_value, eps_value):
    square = jnp.mean(values * values, axis=0, keepdims=True)
    return values * lax.rsqrt(jnp.maximum(square, floor_value) + eps_value)


def low_rank(total, gain):
    low = jnp.transpose(normal(total[: gain.shape[1]], 0.0, EPSILON))
    return (low * gain).astype(jnp.bfloat16)


def state_map(values, gain):
    return (normal(values, SQUARE_FLOOR, 0.0) * column(gain)).astype(jnp.bfloat16)


def summed(part_refs):
    total = part_refs[0][...]
    for part in part_refs[1:]:
        total = total + part[...]
    return total


def softplus(raw):
    return jnp.maximum(raw, 0.0) + jnp.log1p(jnp.exp(-jnp.abs(raw)))


def kept_kernel(parts, *refs):
    place_ref, accepted_ref, owner_ref = refs[:3]
    (
        dt_gain_ref, b_gain_ref, dt_weight_ref, dt_bias_ref, a_log_hbm, conv_hbm, state_hbm,
        slot_ref, part_ref, a_log_ref, conv_ref, state_ref, in_ref, size_ref, drive_ref, rate_ref, new_ref,
        in_sems, sems,
    ) = refs[3 + parts :]
    pairs = ((refs[3], part_ref), (a_log_hbm, a_log_ref), (conv_hbm, conv_ref), (state_hbm, state_ref))
    copies = [pltpu.make_async_copy(*pair, in_sems.at[i]) for i, pair in enumerate(pairs)]
    for copy in copies:
        copy.start()
    rank, states = dt_gain_ref.shape[1], b_gain_ref.shape[1]
    requests = accepted_ref.shape[0]
    rows, channels = conv_ref.shape
    steps = rows // requests
    span = min(2048, channels)
    halves = states // 8

    copies[0].wait()
    total = part_ref[...]
    for part in refs[4 : 3 + parts]:
        total = total + part[...]
    turned = state_map(total[rank : rank + states], b_gain_ref[...]).astype(jnp.float32)
    for row in range(rows):
        t, r = divmod(row, requests)
        in_ref[r * states : (r + 1) * states, t * LANES : (t + 1) * LANES] = jnp.broadcast_to(
            turned[:, row : row + 1], (states, LANES)
        )

    low = low_rank(total, dt_gain_ref[...])
    row = iota((rows, 1), 0)
    live = lax.div(row, requests) < by_request(
        lax.rem(row, requests), [accepted_ref[r] for r in range(requests)]
    )
    copies[1].wait()
    copies[2].wait()
    for first in range(0, channels, span):
        piece = slice(first, first + span)
        size = softplus(dot(low, dt_weight_ref[:, piece]) + dt_bias_ref[:, piece])
        size = jnp.where(live, size, 0.0)
        drive = size * conv_ref[:, piece].astype(jnp.float32)
        for c in range(span // LANES):
            tile = slice(c * LANES, (c + 1) * LANES)
            size_ref[first // LANES + c, :rows, :] = size[:, tile]
            drive_ref[first // LANES + c, :rows, :] = drive[:, tile]
        rate_ref[:, piece] = jnp.exp(a_log_ref[:, piece]) * (-LOG2_E)

    def one_request(r, carry):
        own = pl.multiple_of(r * states, states)
        rounds = lax.div(accepted_ref[r] + (ROUND - 1), ROUND)

        def one_span(part, inner):
            tiles = [pl.multiple_of(part * span + c, LANES) for c in range(0, span, LANES)]

            rates = [
                [rate_ref[8 * h : 8 * (h + 1), pl.ds(tile, LANES)] for tile in tiles]
                for h in range(halves)
            ]

            def one_round(i, hidden):
                hidden = [list(h) for h in hidden]
                for u in range(ROUND):
                    t = i * ROUND + u
                    at = pl.ds(t * requests + r, 8, stride=0)
                    lanes = pl.ds(pl.multiple_of(t * LANES, LANES), LANES)
                    b = [in_ref[pl.ds(own + 8 * h, 8), lanes] for h in range(halves)]
                    for c, tile in enumerate(tiles):
                        place = part * (span // LANES) + c
                        now, drive = size_ref[place, at, :], drive_ref[place, at, :]
                        for h in range(halves):
                            decay = jnp.exp2(now * rates[h][c])
                            hidden[h][c] = decay * hidden[h][c] + drive * b[h]
                return tuple(tuple(h) for h in hidden)

            lanes = pl.ds(pl.multiple_of(part * span, span), span)
            old = state_ref[pl.ds(own, states), lanes].astype(jnp.float32)
            start = tuple(
                tuple(
                    old[8 * h : 8 * (h + 1), c * LANES : (c + 1) * LANES] for c in range(len(tiles))
                )
                for h in range(halves)
            )
            done = lax.fori_loop(0, rounds, one_round, start)
            new = jnp.concatenate([jnp.concatenate(h, axis=1) for h in done], axis=0)
            new_ref[r, :, lanes] = new.astype(jnp.bfloat16)
            return inner

        lax.fori_loop(0, channels // span, one_span, 0)
        slot = owner_ref[place_ref[0] * requests + r]
        pltpu.make_async_copy(new_ref.at[r], slot_ref.at[slot], sems.at[r]).start()
        return carry

    copies[3].wait()
    lax.fori_loop(0, requests, one_request, 0)
    for r in range(requests):
        slot = owner_ref[place_ref[0] * requests + r]
        pltpu.make_async_copy(new_ref.at[r], slot_ref.at[slot], sems.at[r]).wait()


def kept_states(scalars, partials, gains, dt_weight, dt_bias, a_log, conv, state, slots):
    rows, channels = conv.shape
    states, rank = a_log.shape[0], dt_weight.shape[0]
    requests = scalars[1].shape[0]
    near = [*partials[1:], *gains, dt_weight, dt_bias]
    far = [in_hbm(a_log), in_hbm(conv), in_hbm(state)]
    anywhere = pl.BlockSpec(memory_space=pl.ANY)
    return pl.pallas_call(
        functools.partial(kept_kernel, len(partials)),
        in_specs=[pl.BlockSpec(memory_space=pltpu.SMEM)] * len(scalars)
        + [anywhere]
        + [pl.BlockSpec(memory_space=pltpu.VMEM)] * len(near)
        + [anywhere] * len(far),
        out_specs=anywhere,
        out_shape=pltpu.HBM((slots, states, channels), jnp.bfloat16),
        scratch_shapes=[
            pltpu.VMEM(partials[0].shape, jnp.float32),
            pltpu.VMEM(a_log.shape, jnp.float32),
            pltpu.VMEM(conv.shape, jnp.bfloat16),
            pltpu.VMEM(state.shape, jnp.bfloat16),
            pltpu.VMEM((requests * states, rows // requests * LANES), jnp.float32),
            pltpu.VMEM((channels // LANES, rows + 8, LANES), jnp.float32),
            pltpu.VMEM((channels // LANES, rows + 8, LANES), jnp.float32),
            pltpu.VMEM((states, channels), jnp.float32),
            pltpu.VMEM((requests, states, channels), jnp.bfloat16),
            pltpu.SemaphoreType.DMA((1 + len(far),)),
            pltpu.SemaphoreType.DMA((requests,)),
        ],
        compiler_params=pltpu.CompilerParams(vmem_limit_bytes=VMEM_BYTES),
        cost_estimate=pl.CostEstimate(
            flops=VECTOR_WEIGHT * 4 * rows * states * channels,
            transcendentals=rows * states * channels,
            bytes_accessed=2 * channels * (rows + rank + states * (requests + slots)),
        ),
        name="kept_states",
    )(*scalars, in_hbm(partials[0]), *near, *far)


def scan_kernel(parts, *refs):
    (
        dt_gain_ref, b_gain_ref, c_gain_ref, dt_weight_ref, dt_bias_ref, a_log_ref, skip_ref,
        conv_ref, state_ref, z_ref, mixed_ref,
        low_ref, in_ref, out_ref, size_ref, drive_ref, rate_ref, start_ref, sum_ref,
    ) = refs[parts:]
    rank, states = dt_gain_ref.shape[1], b_gain_ref.shape[1]
    rows, block = conv_ref.shape
    requests = state_ref.shape[0] // states
    steps = rows // requests

    @pl.when(pl.program_id(0) == 0)
    def _():
        total = summed(refs[:parts])
        low_ref[...] = low_rank(total, dt_gain_ref[...])
        in_map = state_map(total[rank : rank + states], b_gain_ref[...])
        out_map = state_map(total[rank + states :], c_gain_ref[...])
        wide = states * LANES
        spread = one_hot(lax.div(iota((states, wide), 1), LANES) == iota((states, wide), 0))
        turn = (((0,), (0,)), ((), ()))
        in_ref[...] = lax.dot_general(in_map, spread, turn, preferred_element_type=jnp.float32)
        out_ref[...] = lax.dot_general(out_map, spread, turn, preferred_element_type=jnp.float32)

    conv = conv_ref[...].astype(jnp.float32)
    size = softplus(dot(low_ref[...], dt_weight_ref[...]) + dt_bias_ref[...])
    size_ref[...] = size
    drive_ref[...] = size * conv
    start_ref[...] = dot(to_step_major(requests, states), state_ref[...])
    rate = jnp.exp(a_log_ref[...]) * (-LOG2_E)
    for n in range(states):
        rate_ref[n * requests : (n + 1) * requests, :] = jnp.broadcast_to(
            rate[n : n + 1, :], (requests, block)
        )

    pair = 2 if block % (2 * LANES) == 0 else 1

    def columns(c, carry):
        spans = [pl.ds(pl.multiple_of((c * pair + i) * LANES, LANES), LANES) for i in range(pair)]
        start = tuple(
            tuple(start_ref[n * requests : (n + 1) * requests, s] for s in spans)
            for n in range(states)
        )

        def step(t, hidden):
            at = pl.ds(pl.multiple_of(t * requests, requests), requests)
            sizes = [size_ref[at, s] for s in spans]
            drives = [drive_ref[at, s] for s in spans]
            sums = [None] * pair
            new = []
            for n in range(states):
                b = in_ref[at, n * LANES : (n + 1) * LANES]
                c_map = out_ref[at, n * LANES : (n + 1) * LANES]
                own = slice(n * requests, (n + 1) * requests)
                mine = []
                for i, s in enumerate(spans):
                    h = jnp.exp2(sizes[i] * rate_ref[own, s]) * hidden[n][i] + drives[i] * b
                    term = c_map * h
                    sums[i] = term if sums[i] is None else sums[i] + term
                    mine.append(h)
                new.append(tuple(mine))
            for i, s in enumerate(spans):
                sum_ref[at, s] = sums[i]
            return tuple(new)

        lax.fori_loop(0, steps, step, start, unroll=2)
        return carry

    lax.fori_loop(0, block // (pair * LANES), columns, 0)

    gate = silu(dot(to_step_major(requests, steps), z_ref[...]))
    mixed = ((sum_ref[...] + skip_ref[...] * conv) * gate).astype(jnp.bfloat16)
    mixed_ref[...] = dot(to_request_major(requests, steps), mixed).astype(jnp.bfloat16)


def scan(partials, gains, dt_weight, dt_bias, a_log, skip, conv, state, z_gate):
    rows, channels = conv.shape
    states, rank = a_log.shape[0], dt_weight.shape[0]
    block = min(512, channels)

    def whole(array):
        return pl.BlockSpec(array.shape, lambda j: (0, 0))

    wide = [in_hbm(dt_weight), dt_bias, in_hbm(a_log), skip, in_hbm(conv), in_hbm(state), in_hbm(z_gate)]
    tall = pltpu.VMEM((rows, block), jnp.float32)
    table = pltpu.VMEM((rows, states * LANES), jnp.float32)
    return pl.pallas_call(
        functools.partial(scan_kernel, len(partials)),
        grid=(channels // block,),
        in_specs=[whole(a) for a in (*partials, *gains)]
        + [pl.BlockSpec((a.shape[0], block), lambda j: (0, j)) for a in wide],
        out_specs=pl.BlockSpec((rows, block), lambda j: (0, j)),
        out_shape=jax.ShapeDtypeStruct((rows, channels), jnp.bfloat16),
        scratch_shapes=[
            pltpu.VMEM((rows, rank), jnp.bfloat16), table, table, tall, tall,
            pltpu.VMEM((state.shape[0], block), jnp.float32),
            pltpu.VMEM((state.shape[0], block), jnp.float32),
            tall,
        ],
        compiler_params=pltpu.CompilerParams(
            dimension_semantics=("arbitrary",), vmem_limit_bytes=VMEM_BYTES
        ),
        cost_estimate=pl.CostEstimate(
            flops=VECTOR_WEIGHT * 8 * rows * states * channels,
            transcendentals=rows * states * channels,
            bytes_accessed=2 * channels * (3 * rows + rank),
        ),
        name="scan",
    )(*partials, *gains, *wide)


def edge_kernel(steps, requests, place_ref, source_ref, range_ref, *refs):
    group_refs, edge_ref, stats_ref = refs[:-2], refs[-2], refs[-1]
    own_most, lags, block = edge_ref.shape
    groups = group_refs[0].shape[0] // EDGE_ROWS
    height = len(group_refs) * groups * EDGE_ROWS
    place = place_ref[0]

    def sender(index):
        p, d = lax.div(index, groups * EDGE_ROWS), lax.rem(lax.div(index, EDGE_ROWS), groups)
        return (d * PLANE + p) ^ place

    got = jnp.concatenate([ref[...] for ref in group_refs], axis=0)
    row, col = iota((own_most * 8, 1), 0), iota((1, height), 1)
    wanted = jnp.full((own_most * 8, 1), -1, jnp.int32)
    for i in range(own_most):
        wanted = jnp.where(lax.div(row, 8) == i, source_ref[i], wanted)
    pick = (sender(col) == wanted) & (lax.rem(col, EDGE_ROWS) == lax.rem(row, 8))
    picked = dot(one_hot(pick), got)
    for i in range(own_most):
        edge_ref[i] = picked[i * 8 : i * 8 + lags].astype(jnp.bfloat16)

    @pl.when(pl.program_id(0) == 0)
    def _():
        numbers = got[:, :LANES].astype(jnp.float32)
        row, lane = iota((height, LANES), 0), iota((height, LANES), 1)
        mine = lax.rem(row, EDGE_ROWS) == lags
        request = sender(row) * requests + lax.rem(lane, requests)
        digit = lax.div(lane, requests)
        counts = jnp.where(digit == 0, numbers, 0.0)
        lengths = jnp.where(digit == 1, numbers, 0.0) + jnp.where(
            digit == 2, numbers * float(1 << DIGIT), 0.0
        )
        tenants = range_ref.shape[0]
        sums, loads, members = [], [], []
        for k in range(tenants):
            start, end = range_ref[k, 0], range_ref[k, 1]
            inside = mine & (request >= start) & (request < end)
            sums.append(jnp.sum(jnp.where(inside, counts, 0.0), keepdims=True))
            loads.append(jnp.sum(jnp.where(inside, lengths, 0.0), keepdims=True))
            members.append((jnp.zeros((1, 1), jnp.int32) + (end - start)).astype(jnp.float32))
        mean = sum(loads[1:], loads[0]) / sum(members[1:], members[0])
        out = jnp.zeros((tenants, 2), jnp.float32)
        row, col = iota((tenants, 2), 0), iota((tenants, 2), 1)
        for k in range(tenants):
            rate = sums[k] / (float(steps) * members[k])
            load = loads[k] / members[k] / mean
            out = jnp.where(row == k, jnp.where(col == 0, rate, load), out)
        stats_ref[...] = out


def settle_edges(place, source, tenant_range, got, own_most, lags, steps, requests):
    smem = pl.BlockSpec(memory_space=pltpu.SMEM)
    height, channels = got[0].shape
    block = min(2048, channels)
    stats = (tenant_range.shape[0], 2)
    return pl.pallas_call(
        functools.partial(edge_kernel, steps, requests),
        grid=(channels // block,),
        in_specs=[smem] * 3 + [pl.BlockSpec((height, block), lambda j: (0, j))] * len(got),
        out_specs=[
            pl.BlockSpec((own_most, lags, block), lambda j: (0, 0, j)),
            pl.BlockSpec(stats, lambda j: (0, 0)),
        ],
        out_shape=[
            jax.ShapeDtypeStruct((own_most, lags, channels), jnp.bfloat16),
            jax.ShapeDtypeStruct(stats, jnp.float32),
        ],
        compiler_params=pltpu.CompilerParams(
            dimension_semantics=("arbitrary",), vmem_limit_bytes=VMEM_BYTES
        ),
        name="settle_edges",
    )(place, source, tenant_range, *got)


def settle_kernel(source_ref, bound_ref, got_hbm, owned_hbm, rows_ref, in_sems, sems):
    slots, own_most = got_hbm.shape[0], owned_hbm.shape[0]
    size = slots // PARTS
    parts = [slice(q * size, (q + 1) * size) for q in range(PARTS)]
    fetches = [
        pltpu.make_async_copy(got_hbm.at[part], rows_ref.at[part], in_sems.at[q])
        for q, part in enumerate(parts)
    ]
    for fetch in fetches:
        fetch.start()
    rows_ref[slots] = jnp.zeros(rows_ref.shape[1:], rows_ref.dtype)

    def put(i):
        return pltpu.make_async_copy(rows_ref.at[source_ref[i]], owned_hbm.at[i], sems.at[i])

    def start(i, carry):
        put(i).start()
        return carry

    lax.fori_loop(bound_ref[PARTS], own_most, start, 0)
    for q, fetch in enumerate(fetches):
        fetch.wait()
        lax.fori_loop(bound_ref[q], bound_ref[q + 1], start, 0)
    for i in range(own_most):
        put(i).wait()


def settle_states(source, bounds, got, own_most):
    smem = pl.BlockSpec(memory_space=pltpu.SMEM)
    anywhere = pl.BlockSpec(memory_space=pl.ANY)
    slots, *rest = got.shape
    return pl.pallas_call(
        settle_kernel,
        in_specs=[smem, smem, anywhere],
        out_specs=anywhere,
        out_shape=pltpu.HBM((own_most, *rest), got.dtype),
        scratch_shapes=[
            pltpu.VMEM((slots + 1, *rest), got.dtype),
            pltpu.SemaphoreType.DMA((PARTS,)),
            pltpu.SemaphoreType.DMA((own_most,)),
        ],
        compiler_params=pltpu.CompilerParams(vmem_limit_bytes=VMEM_BYTES),
        name="settle_states",
    )(source, bounds, in_hbm(got))


def per_device(
    x_in, z_gate, conv_edge, conv_weight, conv_bias, x_proj_weight, dt_gain, b_gain, c_gain,
    dt_proj_weight, dt_bias, a_log, skip, ssm_state, accepted, prompt_len, tenant_range, owner,
):
    requests, states, channels = ssm_state.shape
    lags = conv_edge.shape[1]
    owners = lax.axis_size("req")
    own_most = min(requests + requests // 2, owners)
    place = lax.axis_index("req").astype(jnp.int32).reshape(1)

    by_lag = jnp.transpose(conv_edge, (1, 0, 2))
    conv, partial = conv_project(
        x_in, by_lag, conv_weight, conv_bias.reshape(1, -1), x_proj_weight.T
    )
    if lax.axis_size("tp") == 2:
        partials = (partial, lax.ppermute(partial, "tp", [(0, 1), (1, 0)]))
    else:
        partials = (lax.psum(partial, "tp"),)

    def swap(rows, delta):
        return lax.ppermute(rows, "req", [(i, i ^ delta) for i in range(owners)]) if delta else rows

    groups = kept_edges((place, accepted, prompt_len, owner), x_in, by_lag, partial, owners)
    half = len(groups) // 2
    far = [swap(rows, d * PLANE) for d, rows in enumerate(groups) if d >= half]

    gains = (dt_gain.reshape(1, -1), b_gain.reshape(1, -1), c_gain.reshape(1, -1))
    bias = dt_bias.reshape(1, -1)
    state = ssm_state.reshape(requests * states, channels)
    slots = kept_states(
        (place, accepted, owner), partials, gains[:2], dt_proj_weight, bias, a_log, conv, state, owners
    )
    slots, *near = lax.optimization_barrier((slots, *groups[:half]))
    got = lax.all_to_all(slots, "req", split_axis=0, concat_axis=0, tiled=True)
    groups = [swap(rows, d * PLANE) for d, rows in enumerate(near)] + far
    mixed = scan(
        partials, gains, dt_proj_weight, bias, a_log, skip.reshape(1, -1), conv, state, z_gate
    )
    mixed, owner = lax.optimization_barrier((mixed, owner))
    hits = jnp.any(owner.reshape(owners, requests) == place, axis=1)
    ids = np.arange(owners, dtype=np.int32)
    ranks = jnp.sum((hits[None, :] & (ids[None, :] < ids[:, None])).astype(jnp.int32), axis=1)
    starts = np.arange(PARTS + 1, dtype=np.int32) * (owners // PARTS)
    bounds = jnp.sum((hits[None, :] & (ids[None, :] < starts[:, None])).astype(jnp.int32), axis=1)
    at = hits[None, :] & (ranks[None, :] == jnp.arange(own_most, dtype=jnp.int32)[:, None])
    source = owners - jnp.sum(jnp.where(at, owners - ids[None, :], 0), axis=1)
    groups = [swap(rows, p) for p, rows in enumerate(regroup(groups, mixed))]
    owned_edge, tenant_stats = settle_edges(
        place, source, tenant_range, groups, own_most, lags, x_in.shape[0] // requests,
        requests,
    )
    owned = settle_states(source, bounds, got, own_most)
    return (mixed, owned, owned_edge, tenant_stats)


def solution(mesh):
    placed = (
        P("req", "tp"),
        P("req", "tp"),
        P("req", None, "tp"),
        P(None, "tp"),
        P("tp"),
        P("tp", None),
        P(),
        P(),
        P(),
        P(None, "tp"),
        P("tp"),
        P(None, "tp"),
        P("tp"),
        P("req", None, "tp"),
        P("req"),
        P("req"),
        P(),
        P(),
    )
    return jax.shard_map(
        per_device,
        mesh=mesh,
        in_specs=placed,
        out_specs=(P("req", "tp"), P("req", None, "tp"), P("req", None, "tp"), P()),
        check_vma=False,
    )
```

```python
import functools

import jax
import jax.numpy as jnp
import numpy as np
from jax import lax
from jax.experimental import pallas as pl
from jax.experimental.pallas import tpu as pltpu
from jax.sharding import PartitionSpec as P

EPSILON = 1e-06
SQUARE_FLOOR = 0.25
LOG2_E = 1.4426950408889634
LANES = 128
EDGE_ROWS = 4
PLANE = 4
DIGIT = 7
VMEM_BYTES = 24 * 1024 * 1024
BLOCK = 2048
PARTS = 4
ROUND = 4
VECTOR_WEIGHT = 30000


def iota(shape, axis):
    return lax.broadcasted_iota(jnp.int32, shape, axis)


def one_hot(condition):
    return jnp.where(condition, 1.0, 0.0).astype(jnp.bfloat16)


def dot(lhs, rhs):
    return jnp.dot(lhs, rhs, preferred_element_type=jnp.float32)


def in_hbm(array):
    return pltpu.with_memory_space_constraint(array, pltpu.HBM)


def silu(value):
    return value * (0.5 + 0.5 * jnp.tanh(0.5 * value))


def to_step_major(requests, steps):
    rows = requests * steps
    row, col = iota((rows, rows), 0), iota((rows, rows), 1)
    return one_hot(col == lax.rem(row, requests) * steps + lax.div(row, requests))


def to_request_major(requests, steps):
    rows = requests * steps
    row, col = iota((rows, rows), 0), iota((rows, rows), 1)
    return one_hot(row == lax.rem(col, requests) * steps + lax.div(col, requests))


def by_request(index, scalars):
    out = jnp.zeros_like(index)
    for request, scalar in enumerate(scalars):
        out = jnp.where(index == request, scalar, out)
    return out


def conv_kernel(
    x_hbm, edge_hbm, weight_hbm, bias_hbm, proj_hbm, conv_hbm, partial_ref,
    x_ref, edge_ref, weight_ref, bias_ref, proj_ref, conv_ref, sems, out_sems,
):
    lags, requests, channels = edge_ref.shape
    taps = weight_ref.shape[0]
    steps = x_ref.shape[0] // requests
    block = min(BLOCK, channels)
    pieces = [slice(c, c + block) for c in range(0, channels, block)]
    pairs = [(weight_hbm, weight_ref), (bias_hbm, bias_ref), (edge_hbm, edge_ref)]
    pairs += [(x_hbm.at[:, piece], x_ref.at[:, piece]) for piece in pieces]
    pairs.append((proj_hbm, proj_ref))
    copies = [pltpu.make_async_copy(*pair, sems.at[i]) for i, pair in enumerate(pairs)]
    for copy in copies:
        copy.start()
    results = [
        pltpu.make_async_copy(conv_ref.at[:, piece], conv_hbm.at[:, piece], out_sems.at[i])
        for i, piece in enumerate(pieces)
    ]
    order = to_step_major(requests, steps)
    for copy in copies[:3]:
        copy.wait()
    for i, piece in enumerate(pieces):
        copies[3 + i].wait()
        stream = dot(order, x_ref[:, piece])
        window = [edge_ref[k, :, piece].astype(jnp.float32) for k in range(lags)]
        window += [stream[t * requests : (t + 1) * requests] for t in range(steps)]
        weight = [weight_ref[k : k + 1, piece] for k in range(taps)]
        outs = []
        for t in range(steps):
            added = bias_ref[:, piece] + weight[0] * window[t]
            for k in range(1, taps):
                added = added + weight[k] * window[t + k]
            outs.append(silu(added))
        conv_ref[:, piece] = jnp.concatenate(outs, axis=0).astype(jnp.bfloat16)
        results[i].start()
    copies[-1].wait()
    partial_ref[...] = lax.dot_general(
        proj_ref[...], conv_ref[...], (((1,), (1,)), ((), ())), preferred_element_type=jnp.float32
    )
    for result in results:
        result.wait()


def conv_project(x_in, conv_edge, conv_weight, conv_bias, proj):
    rows, channels = x_in.shape
    operands = (x_in, conv_edge, conv_weight, conv_bias, proj)
    pieces = channels // min(BLOCK, channels)
    return pl.pallas_call(
        conv_kernel,
        in_specs=[pl.BlockSpec(memory_space=pl.ANY)] * len(operands),
        out_specs=[pl.BlockSpec(memory_space=pl.ANY), pl.BlockSpec(memory_space=pltpu.VMEM)],
        out_shape=[
            pltpu.HBM((rows, channels), jnp.bfloat16),
            pltpu.HBM((proj.shape[0], rows), jnp.float32),
        ],
        scratch_shapes=[pltpu.VMEM(a.shape, a.dtype) for a in operands]
        + [
            pltpu.VMEM((rows, channels), jnp.bfloat16),
            pltpu.SemaphoreType.DMA((4 + pieces,)),
            pltpu.SemaphoreType.DMA((pieces,)),
        ],
        compiler_params=pltpu.CompilerParams(vmem_limit_bytes=VMEM_BYTES),
        name="conv_project",
    )(*(in_hbm(a) for a in operands))


def kept_edge_kernel(
    place_ref, accepted_ref, length_ref, owner_ref, x_ref, edge_ref, _, *group_refs
):
    lags, requests, block = edge_ref.shape
    steps = x_ref.shape[0] // requests
    place = place_ref[0]
    accepted = [accepted_ref[r] for r in range(requests)]
    lengths = [length_ref[r] + accepted[r] + 1 for r in range(requests)]
    deltas = [owner_ref[place * requests + r] ^ place for r in range(requests)]
    height = len(group_refs) * PLANE * EDGE_ROWS
    slot = lax.div(iota((height, 1), 0), EDGE_ROWS)
    lag = lax.rem(iota((height, 1), 0), EDGE_ROWS)

    def pick(request, position):
        return one_hot(
            (slot == by_request(request, deltas))
            & (position - by_request(request, accepted) == lag)
            & (lag < lags)
        )

    col = iota((1, requests * steps), 1)
    picked = dot(pick(lax.div(col, steps), lax.rem(col, steps) + lags), x_ref[...])
    col = iota((1, lags * requests), 1)
    edge = jnp.concatenate([edge_ref[k].astype(jnp.float32) for k in range(lags)], axis=0)
    picked += dot(pick(lax.rem(col, requests), lax.div(col, requests)), edge.astype(jnp.bfloat16))
    low = [length & ((1 << DIGIT) - 1) for length in lengths]
    high = [length >> DIGIT for length in lengths]
    numbers = by_request(iota((1, block), 1), accepted + low + high).astype(jnp.float32)
    picked = jnp.where(lag == lags, numbers, picked).astype(jnp.bfloat16)
    group = PLANE * EDGE_ROWS
    for d, ref in enumerate(group_refs):
        ref[...] = picked[d * group : (d + 1) * group]


def kept_edges(scalars, x_in, conv_edge, after, owners):
    channels = x_in.shape[1]
    groups = owners // PLANE
    vmem = pl.BlockSpec(memory_space=pltpu.VMEM)
    return pl.pallas_call(
        kept_edge_kernel,
        in_specs=[pl.BlockSpec(memory_space=pltpu.SMEM)] * len(scalars)
        + [vmem, vmem, pl.BlockSpec(memory_space=pl.ANY)],
        out_specs=[vmem] * groups,
        out_shape=[pltpu.HBM((PLANE * EDGE_ROWS, channels), jnp.bfloat16)] * groups,
        compiler_params=pltpu.CompilerParams(vmem_limit_bytes=VMEM_BYTES),
        name="kept_edges",
    )(*scalars, x_in, conv_edge, in_hbm(after))


def regroup_kernel(*refs):
    groups = len(refs) - 1 - PLANE
    rows = jnp.concatenate([ref[...].astype(jnp.float32) for ref in refs[:groups]], axis=0)
    for p, out_ref in enumerate(refs[-PLANE:]):
        parts = [
            rows[(d * PLANE + p) * EDGE_ROWS : (d * PLANE + p + 1) * EDGE_ROWS] for d in range(groups)
        ]
        out_ref[...] = jnp.concatenate(parts, axis=0).astype(jnp.bfloat16)


def regroup(arrived, after):
    rows, channels = arrived[0].shape
    block = min(1024, channels)
    height = len(arrived) * EDGE_ROWS
    return pl.pallas_call(
        regroup_kernel,
        grid=(channels // block,),
        in_specs=[pl.BlockSpec((rows, block), lambda j: (0, j))] * len(arrived)
        + [pl.BlockSpec(memory_space=pl.ANY)],
        out_specs=[pl.BlockSpec((height, block), lambda j: (0, j))] * PLANE,
        out_shape=[pltpu.HBM((height, channels), jnp.bfloat16)] * PLANE,
        compiler_params=pltpu.CompilerParams(
            dimension_semantics=("arbitrary",), vmem_limit_bytes=VMEM_BYTES
        ),
        name="regroup",
    )(*arrived, in_hbm(after))


def column(row):
    count = row.shape[1]
    same = iota((count, count), 0) == iota((count, count), 1)
    return jnp.sum(jnp.where(same, row, 0.0), axis=1, keepdims=True)


def normal(values, floor_value, eps_value):
    square = jnp.mean(values * values, axis=0, keepdims=True)
    return values * lax.rsqrt(jnp.maximum(square, floor_value) + eps_value)


def low_rank(total, gain):
    low = jnp.transpose(normal(total[: gain.shape[1]], 0.0, EPSILON))
    return (low * gain).astype(jnp.bfloat16)


def state_map(values, gain):
    return (normal(values, SQUARE_FLOOR, 0.0) * column(gain)).astype(jnp.bfloat16)


def summed(part_refs):
    total = part_refs[0][...]
    for part in part_refs[1:]:
        total = total + part[...]
    return total


def softplus(raw):
    return jnp.maximum(raw, 0.0) + jnp.log1p(jnp.exp(-jnp.abs(raw)))


def kept_kernel(parts, *refs):
    place_ref, accepted_ref, owner_ref = refs[:3]
    (
        dt_gain_ref, b_gain_ref, dt_weight_ref, dt_bias_ref, a_log_hbm, conv_hbm, state_hbm,
        slot_ref, part_ref, a_log_ref, conv_ref, state_ref, in_ref, size_ref, drive_ref, rate_ref, new_ref,
        in_sems, sems,
    ) = refs[3 + parts :]
    pairs = ((refs[3], part_ref), (a_log_hbm, a_log_ref), (conv_hbm, conv_ref), (state_hbm, state_ref))
    copies = [pltpu.make_async_copy(*pair, in_sems.at[i]) for i, pair in enumerate(pairs)]
    for copy in copies:
        copy.start()
    rank, states = dt_gain_ref.shape[1], b_gain_ref.shape[1]
    requests = accepted_ref.shape[0]
    rows, channels = conv_ref.shape
    steps = rows // requests
    span = min(2048, channels)
    halves = states // 8

    copies[1].wait()
    rate_ref[...] = jnp.exp(a_log_ref[...]) * (-LOG2_E)
    copies[0].wait()
    total = part_ref[...]
    for part in refs[4 : 3 + parts]:
        total = total + part[...]
    turned = state_map(total[rank : rank + states], b_gain_ref[...]).astype(jnp.float32)
    for row in range(rows):
        t, r = divmod(row, requests)
        in_ref[r * states : (r + 1) * states, t * LANES : (t + 1) * LANES] = jnp.broadcast_to(
            turned[:, row : row + 1], (states, LANES)
        )

    low = low_rank(total, dt_gain_ref[...])
    row = iota((rows, 1), 0)
    live = lax.div(row, requests) < by_request(
        lax.rem(row, requests), [accepted_ref[r] for r in range(requests)]
    )
    copies[2].wait()
    for first in range(0, channels, span):
        piece = slice(first, first + span)
        size = softplus(dot(low, dt_weight_ref[:, piece]) + dt_bias_ref[:, piece])
        size = jnp.where(live, size, 0.0)
        drive = size * conv_ref[:, piece].astype(jnp.float32)
        for c in range(span // LANES):
            tile = slice(c * LANES, (c + 1) * LANES)
            size_ref[first // LANES + c, :rows, :] = size[:, tile]
            drive_ref[first // LANES + c, :rows, :] = drive[:, tile]

    def one_request(r, carry):
        own = pl.multiple_of(r * states, states)
        rounds = lax.div(accepted_ref[r] + (ROUND - 1), ROUND)

        def one_span(part, inner):
            tiles = [pl.multiple_of(part * span + c, LANES) for c in range(0, span, LANES)]

            rates = [
                [rate_ref[8 * h : 8 * (h + 1), pl.ds(tile, LANES)] for tile in tiles]
                for h in range(halves)
            ]

            def one_round(i, hidden):
                hidden = [list(h) for h in hidden]
                for u in range(ROUND):
                    t = i * ROUND + u
                    at = pl.ds(t * requests + r, 8, stride=0)
                    lanes = pl.ds(pl.multiple_of(t * LANES, LANES), LANES)
                    b = [in_ref[pl.ds(own + 8 * h, 8), lanes] for h in range(halves)]
                    for c, tile in enumerate(tiles):
                        place = part * (span // LANES) + c
                        now, drive = size_ref[place, at, :], drive_ref[place, at, :]
                        for h in range(halves):
                            decay = jnp.exp2(now * rates[h][c])
                            hidden[h][c] = decay * hidden[h][c] + drive * b[h]
                return tuple(tuple(h) for h in hidden)

            lanes = pl.ds(pl.multiple_of(part * span, span), span)
            old = state_ref[pl.ds(own, states), lanes].astype(jnp.float32)
            start = tuple(
                tuple(
                    old[8 * h : 8 * (h + 1), c * LANES : (c + 1) * LANES] for c in range(len(tiles))
                )
                for h in range(halves)
            )
            done = lax.fori_loop(0, rounds, one_round, start)
            new = jnp.concatenate([jnp.concatenate(h, axis=1) for h in done], axis=0)
            new_ref[r, :, lanes] = new.astype(jnp.bfloat16)
            return inner

        lax.fori_loop(0, channels // span, one_span, 0)
        slot = owner_ref[place_ref[0] * requests + r]
        pltpu.make_async_copy(new_ref.at[r], slot_ref.at[slot], sems.at[r]).start()
        return carry

    copies[3].wait()
    lax.fori_loop(0, requests, one_request, 0)
    for r in range(requests):
        slot = owner_ref[place_ref[0] * requests + r]
        pltpu.make_async_copy(new_ref.at[r], slot_ref.at[slot], sems.at[r]).wait()


def kept_states(scalars, partials, gains, dt_weight, dt_bias, a_log, conv, state, slots):
    rows, channels = conv.shape
    states, rank = a_log.shape[0], dt_weight.shape[0]
    requests = scalars[1].shape[0]
    near = [*partials[1:], *gains, dt_weight, dt_bias]
    far = [in_hbm(a_log), in_hbm(conv), in_hbm(state)]
    anywhere = pl.BlockSpec(memory_space=pl.ANY)
    return pl.pallas_call(
        functools.partial(kept_kernel, len(partials)),
        in_specs=[pl.BlockSpec(memory_space=pltpu.SMEM)] * len(scalars)
        + [anywhere]
        + [pl.BlockSpec(memory_space=pltpu.VMEM)] * len(near)
        + [anywhere] * len(far),
        out_specs=anywhere,
        out_shape=pltpu.HBM((slots, states, channels), jnp.bfloat16),
        scratch_shapes=[
            pltpu.VMEM(partials[0].shape, jnp.float32),
            pltpu.VMEM(a_log.shape, jnp.float32),
            pltpu.VMEM(conv.shape, jnp.bfloat16),
            pltpu.VMEM(state.shape, jnp.bfloat16),
            pltpu.VMEM((requests * states, rows // requests * LANES), jnp.float32),
            pltpu.VMEM((channels // LANES, rows + 8, LANES), jnp.float32),
            pltpu.VMEM((channels // LANES, rows + 8, LANES), jnp.float32),
            pltpu.VMEM((states, channels), jnp.float32),
            pltpu.VMEM((requests, states, channels), jnp.bfloat16),
            pltpu.SemaphoreType.DMA((1 + len(far),)),
            pltpu.SemaphoreType.DMA((requests,)),
        ],
        compiler_params=pltpu.CompilerParams(vmem_limit_bytes=VMEM_BYTES),
        cost_estimate=pl.CostEstimate(
            flops=VECTOR_WEIGHT * 4 * rows * states * channels,
            transcendentals=rows * states * channels,
            bytes_accessed=2 * channels * (rows + rank + states * (requests + slots)),
        ),
        name="kept_states",
    )(*scalars, in_hbm(partials[0]), *near, *far)


def scan_kernel(parts, *refs):
    (
        dt_gain_ref, b_gain_ref, c_gain_ref, dt_weight_ref, dt_bias_ref, a_log_ref, skip_ref,
        conv_ref, state_ref, z_ref, mixed_ref,
        low_ref, in_ref, out_ref, size_ref, drive_ref, rate_ref, start_ref, sum_ref,
    ) = refs[parts:]
    rank, states = dt_gain_ref.shape[1], b_gain_ref.shape[1]
    rows, block = conv_ref.shape
    requests = state_ref.shape[0] // states
    steps = rows // requests

    @pl.when(pl.program_id(0) == 0)
    def _():
        total = summed(refs[:parts])
        low_ref[...] = low_rank(total, dt_gain_ref[...])
        in_map = state_map(total[rank : rank + states], b_gain_ref[...])
        out_map = state_map(total[rank + states :], c_gain_ref[...])
        wide = states * LANES
        spread = one_hot(lax.div(iota((states, wide), 1), LANES) == iota((states, wide), 0))
        turn = (((0,), (0,)), ((), ()))
        in_ref[...] = lax.dot_general(in_map, spread, turn, preferred_element_type=jnp.float32)
        out_ref[...] = lax.dot_general(out_map, spread, turn, preferred_element_type=jnp.float32)

    conv = conv_ref[...].astype(jnp.float32)
    size = softplus(dot(low_ref[...], dt_weight_ref[...]) + dt_bias_ref[...])
    size_ref[...] = size
    drive_ref[...] = size * conv
    start_ref[...] = dot(to_step_major(requests, states), state_ref[...])
    rate = jnp.exp(a_log_ref[...]) * (-LOG2_E)
    for n in range(states):
        rate_ref[n * requests : (n + 1) * requests, :] = jnp.broadcast_to(
            rate[n : n + 1, :], (requests, block)
        )

    pair = 2 if block % (2 * LANES) == 0 else 1

    def columns(c, carry):
        spans = [pl.ds(pl.multiple_of((c * pair + i) * LANES, LANES), LANES) for i in range(pair)]
        start = tuple(
            tuple(start_ref[n * requests : (n + 1) * requests, s] for s in spans)
            for n in range(states)
        )

        def step(t, hidden):
            at = pl.ds(pl.multiple_of(t * requests, requests), requests)
            sizes = [size_ref[at, s] for s in spans]
            drives = [drive_ref[at, s] for s in spans]
            sums = [None] * pair
            new = []
            for n in range(states):
                b = in_ref[at, n * LANES : (n + 1) * LANES]
                c_map = out_ref[at, n * LANES : (n + 1) * LANES]
                own = slice(n * requests, (n + 1) * requests)
                mine = []
                for i, s in enumerate(spans):
                    h = jnp.exp2(sizes[i] * rate_ref[own, s]) * hidden[n][i] + drives[i] * b
                    term = c_map * h
                    sums[i] = term if sums[i] is None else sums[i] + term
                    mine.append(h)
                new.append(tuple(mine))
            for i, s in enumerate(spans):
                sum_ref[at, s] = sums[i]
            return tuple(new)

        lax.fori_loop(0, steps, step, start, unroll=2)
        return carry

    lax.fori_loop(0, block // (pair * LANES), columns, 0)

    gate = silu(dot(to_step_major(requests, steps), z_ref[...]))
    mixed = ((sum_ref[...] + skip_ref[...] * conv) * gate).astype(jnp.bfloat16)
    mixed_ref[...] = dot(to_request_major(requests, steps), mixed).astype(jnp.bfloat16)


def scan(partials, gains, dt_weight, dt_bias, a_log, skip, conv, state, z_gate):
    rows, channels = conv.shape
    states, rank = a_log.shape[0], dt_weight.shape[0]
    block = min(512, channels)

    def whole(array):
        return pl.BlockSpec(array.shape, lambda j: (0, 0))

    wide = [in_hbm(dt_weight), dt_bias, in_hbm(a_log), skip, in_hbm(conv), in_hbm(state), in_hbm(z_gate)]
    tall = pltpu.VMEM((rows, block), jnp.float32)
    table = pltpu.VMEM((rows, states * LANES), jnp.float32)
    return pl.pallas_call(
        functools.partial(scan_kernel, len(partials)),
        grid=(channels // block,),
        in_specs=[whole(a) for a in (*partials, *gains)]
        + [pl.BlockSpec((a.shape[0], block), lambda j: (0, j)) for a in wide],
        out_specs=pl.BlockSpec((rows, block), lambda j: (0, j)),
        out_shape=jax.ShapeDtypeStruct((rows, channels), jnp.bfloat16),
        scratch_shapes=[
            pltpu.VMEM((rows, rank), jnp.bfloat16), table, table, tall, tall,
            pltpu.VMEM((state.shape[0], block), jnp.float32),
            pltpu.VMEM((state.shape[0], block), jnp.float32),
            tall,
        ],
        compiler_params=pltpu.CompilerParams(
            dimension_semantics=("arbitrary",), vmem_limit_bytes=VMEM_BYTES
        ),
        cost_estimate=pl.CostEstimate(
            flops=VECTOR_WEIGHT * 8 * rows * states * channels,
            transcendentals=rows * states * channels,
            bytes_accessed=2 * channels * (3 * rows + rank),
        ),
        name="scan",
    )(*partials, *gains, *wide)


def edge_kernel(steps, requests, place_ref, source_ref, range_ref, *refs):
    group_refs, edge_ref, stats_ref = refs[:-2], refs[-2], refs[-1]
    own_most, lags, block = edge_ref.shape
    groups = group_refs[0].shape[0] // EDGE_ROWS
    height = len(group_refs) * groups * EDGE_ROWS
    place = place_ref[0]

    def sender(index):
        p, d = lax.div(index, groups * EDGE_ROWS), lax.rem(lax.div(index, EDGE_ROWS), groups)
        return (d * PLANE + p) ^ place

    got = jnp.concatenate([ref[...] for ref in group_refs], axis=0)
    row, col = iota((own_most * 8, 1), 0), iota((1, height), 1)
    wanted = jnp.full((own_most * 8, 1), -1, jnp.int32)
    for i in range(own_most):
        wanted = jnp.where(lax.div(row, 8) == i, source_ref[i], wanted)
    pick = (sender(col) == wanted) & (lax.rem(col, EDGE_ROWS) == lax.rem(row, 8))
    picked = dot(one_hot(pick), got)
    for i in range(own_most):
        edge_ref[i] = picked[i * 8 : i * 8 + lags].astype(jnp.bfloat16)

    @pl.when(pl.program_id(0) == 0)
    def _():
        numbers = got[:, :LANES].astype(jnp.float32)
        row, lane = iota((height, LANES), 0), iota((height, LANES), 1)
        mine = lax.rem(row, EDGE_ROWS) == lags
        request = sender(row) * requests + lax.rem(lane, requests)
        digit = lax.div(lane, requests)
        counts = jnp.where(digit == 0, numbers, 0.0)
        lengths = jnp.where(digit == 1, numbers, 0.0) + jnp.where(
            digit == 2, numbers * float(1 << DIGIT), 0.0
        )
        tenants = range_ref.shape[0]
        sums, loads, members = [], [], []
        for k in range(tenants):
            start, end = range_ref[k, 0], range_ref[k, 1]
            inside = mine & (request >= start) & (request < end)
            sums.append(jnp.sum(jnp.where(inside, counts, 0.0), keepdims=True))
            loads.append(jnp.sum(jnp.where(inside, lengths, 0.0), keepdims=True))
            members.append((jnp.zeros((1, 1), jnp.int32) + (end - start)).astype(jnp.float32))
        mean = sum(loads[1:], loads[0]) / sum(members[1:], members[0])
        out = jnp.zeros((tenants, 2), jnp.float32)
        row, col = iota((tenants, 2), 0), iota((tenants, 2), 1)
        for k in range(tenants):
            rate = sums[k] / (float(steps) * members[k])
            load = loads[k] / members[k] / mean
            out = jnp.where(row == k, jnp.where(col == 0, rate, load), out)
        stats_ref[...] = out


def settle_edges(place, source, tenant_range, got, own_most, lags, steps, requests):
    smem = pl.BlockSpec(memory_space=pltpu.SMEM)
    height, channels = got[0].shape
    block = min(2048, channels)
    stats = (tenant_range.shape[0], 2)
    return pl.pallas_call(
        functools.partial(edge_kernel, steps, requests),
        grid=(channels // block,),
        in_specs=[smem] * 3 + [pl.BlockSpec((height, block), lambda j: (0, j))] * len(got),
        out_specs=[
            pl.BlockSpec((own_most, lags, block), lambda j: (0, 0, j)),
            pl.BlockSpec(stats, lambda j: (0, 0)),
        ],
        out_shape=[
            jax.ShapeDtypeStruct((own_most, lags, channels), jnp.bfloat16),
            jax.ShapeDtypeStruct(stats, jnp.float32),
        ],
        compiler_params=pltpu.CompilerParams(
            dimension_semantics=("arbitrary",), vmem_limit_bytes=VMEM_BYTES
        ),
        name="settle_edges",
    )(place, source, tenant_range, *got)


def settle_kernel(source_ref, bound_ref, got_hbm, owned_hbm, rows_ref, in_sems, sems):
    slots, own_most = got_hbm.shape[0], owned_hbm.shape[0]
    size = slots // PARTS
    parts = [slice(q * size, (q + 1) * size) for q in range(PARTS)]
    fetches = [
        pltpu.make_async_copy(got_hbm.at[part], rows_ref.at[part], in_sems.at[q])
        for q, part in enumerate(parts)
    ]
    for fetch in fetches:
        fetch.start()
    rows_ref[slots] = jnp.zeros(rows_ref.shape[1:], rows_ref.dtype)

    def put(i):
        return pltpu.make_async_copy(rows_ref.at[source_ref[i]], owned_hbm.at[i], sems.at[i])

    def start(i, carry):
        put(i).start()
        return carry

    lax.fori_loop(bound_ref[PARTS], own_most, start, 0)
    for q, fetch in enumerate(fetches):
        fetch.wait()
        lax.fori_loop(bound_ref[q], bound_ref[q + 1], start, 0)
    for i in range(own_most):
        put(i).wait()


def settle_states(source, bounds, got, own_most):
    smem = pl.BlockSpec(memory_space=pltpu.SMEM)
    anywhere = pl.BlockSpec(memory_space=pl.ANY)
    slots, *rest = got.shape
    return pl.pallas_call(
        settle_kernel,
        in_specs=[smem, smem, anywhere],
        out_specs=anywhere,
        out_shape=pltpu.HBM((own_most, *rest), got.dtype),
        scratch_shapes=[
            pltpu.VMEM((slots + 1, *rest), got.dtype),
            pltpu.SemaphoreType.DMA((PARTS,)),
            pltpu.SemaphoreType.DMA((own_most,)),
        ],
        compiler_params=pltpu.CompilerParams(vmem_limit_bytes=VMEM_BYTES),
        name="settle_states",
    )(source, bounds, in_hbm(got))


def per_device(
    x_in, z_gate, conv_edge, conv_weight, conv_bias, x_proj_weight, dt_gain, b_gain, c_gain,
    dt_proj_weight, dt_bias, a_log, skip, ssm_state, accepted, prompt_len, tenant_range, owner,
):
    requests, states, channels = ssm_state.shape
    lags = conv_edge.shape[1]
    owners = lax.axis_size("req")
    own_most = min(requests + requests // 2, owners)
    place = lax.axis_index("req").astype(jnp.int32).reshape(1)

    by_lag = jnp.transpose(conv_edge, (1, 0, 2))
    conv, partial = conv_project(
        x_in, by_lag, conv_weight, conv_bias.reshape(1, -1), x_proj_weight.T
    )
    if lax.axis_size("tp") == 2:
        partials = (partial, lax.ppermute(partial, "tp", [(0, 1), (1, 0)]))
    else:
        partials = (lax.psum(partial, "tp"),)

    def swap(rows, delta):
        return lax.ppermute(rows, "req", [(i, i ^ delta) for i in range(owners)]) if delta else rows

    groups = kept_edges((place, accepted, prompt_len, owner), x_in, by_lag, partial, owners)
    half = len(groups) // 2
    far = [swap(rows, d * PLANE) for d, rows in enumerate(groups) if d >= half]

    gains = (dt_gain.reshape(1, -1), b_gain.reshape(1, -1), c_gain.reshape(1, -1))
    bias = dt_bias.reshape(1, -1)
    state = ssm_state.reshape(requests * states, channels)
    slots = kept_states(
        (place, accepted, owner), partials, gains[:2], dt_proj_weight, bias, a_log, conv, state, owners
    )
    slots, *near = lax.optimization_barrier((slots, *groups[:half]))
    got = lax.all_to_all(slots, "req", split_axis=0, concat_axis=0, tiled=True)
    groups = [swap(rows, d * PLANE) for d, rows in enumerate(near)] + far
    mixed = scan(
        partials, gains, dt_proj_weight, bias, a_log, skip.reshape(1, -1), conv, state, z_gate
    )
    mixed, owner = lax.optimization_barrier((mixed, owner))
    hits = jnp.any(owner.reshape(owners, requests) == place, axis=1)
    ids = np.arange(owners, dtype=np.int32)
    ranks = jnp.sum((hits[None, :] & (ids[None, :] < ids[:, None])).astype(jnp.int32), axis=1)
    starts = np.arange(PARTS + 1, dtype=np.int32) * (owners // PARTS)
    bounds = jnp.sum((hits[None, :] & (ids[None, :] < starts[:, None])).astype(jnp.int32), axis=1)
    at = hits[None, :] & (ranks[None, :] == jnp.arange(own_most, dtype=jnp.int32)[:, None])
    source = owners - jnp.sum(jnp.where(at, owners - ids[None, :], 0), axis=1)
    groups = [swap(rows, p) for p, rows in enumerate(regroup(groups, mixed))]
    owned_edge, tenant_stats = settle_edges(
        place, source, tenant_range, groups, own_most, lags, x_in.shape[0] // requests,
        requests,
    )
    owned = settle_states(source, bounds, got, own_most)
    return (mixed, owned, owned_edge, tenant_stats)


def solution(mesh):
    placed = (
        P("req", "tp"),
        P("req", "tp"),
        P("req", None, "tp"),
        P(None, "tp"),
        P("tp"),
        P("tp", None),
        P(),
        P(),
        P(),
        P(None, "tp"),
        P("tp"),
        P(None, "tp"),
        P("tp"),
        P("req", None, "tp"),
        P("req"),
        P("req"),
        P(),
        P(),
    )
    return jax.shard_map(
        per_device,
        mesh=mesh,
        in_specs=placed,
        out_specs=(P("req", "tp"), P("req", None, "tp"), P("req", None, "tp"), P()),
        check_vma=False,
    )
```

```python
import functools

import jax
import jax.numpy as jnp
import numpy as np
from jax import lax
from jax.experimental import pallas as pl
from jax.experimental.pallas import tpu as pltpu
from jax.sharding import PartitionSpec as P

EPSILON = 1e-06
SQUARE_FLOOR = 0.25
LOG2_E = 1.4426950408889634
LANES = 128
EDGE_ROWS = 4
PLANE = 4
DIGIT = 7
VMEM_BYTES = 24 * 1024 * 1024
BLOCK = 2048
PARTS = 8
ROUND = 4
VECTOR_WEIGHT = 30000


def iota(shape, axis):
    return lax.broadcasted_iota(jnp.int32, shape, axis)


def one_hot(condition):
    return jnp.where(condition, 1.0, 0.0).astype(jnp.bfloat16)


def dot(lhs, rhs):
    return jnp.dot(lhs, rhs, preferred_element_type=jnp.float32)


def in_hbm(array):
    return pltpu.with_memory_space_constraint(array, pltpu.HBM)


def silu(value):
    return value * (0.5 + 0.5 * jnp.tanh(0.5 * value))


def to_step_major(requests, steps):
    rows = requests * steps
    row, col = iota((rows, rows), 0), iota((rows, rows), 1)
    return one_hot(col == lax.rem(row, requests) * steps + lax.div(row, requests))


def to_request_major(requests, steps):
    rows = requests * steps
    row, col = iota((rows, rows), 0), iota((rows, rows), 1)
    return one_hot(row == lax.rem(col, requests) * steps + lax.div(col, requests))


def by_request(index, scalars):
    out = jnp.zeros_like(index)
    for request, scalar in enumerate(scalars):
        out = jnp.where(index == request, scalar, out)
    return out


def conv_kernel(
    x_hbm, edge_hbm, weight_hbm, bias_hbm, proj_hbm, conv_hbm, partial_ref,
    x_ref, edge_ref, weight_ref, bias_ref, proj_ref, conv_ref, sems, out_sems,
):
    lags, requests, channels = edge_ref.shape
    taps = weight_ref.shape[0]
    steps = x_ref.shape[0] // requests
    block = min(BLOCK, channels)
    pieces = [slice(c, c + block) for c in range(0, channels, block)]
    pairs = [(weight_hbm, weight_ref), (bias_hbm, bias_ref), (edge_hbm, edge_ref)]
    pairs += [(x_hbm.at[:, piece], x_ref.at[:, piece]) for piece in pieces]
    pairs.append((proj_hbm, proj_ref))
    copies = [pltpu.make_async_copy(*pair, sems.at[i]) for i, pair in enumerate(pairs)]
    for copy in copies:
        copy.start()
    results = [
        pltpu.make_async_copy(conv_ref.at[:, piece], conv_hbm.at[:, piece], out_sems.at[i])
        for i, piece in enumerate(pieces)
    ]
    order = to_step_major(requests, steps)
    for copy in copies[:3]:
        copy.wait()
    for i, piece in enumerate(pieces):
        copies[3 + i].wait()
        stream = dot(order, x_ref[:, piece])
        window = [edge_ref[k, :, piece].astype(jnp.float32) for k in range(lags)]
        window += [stream[t * requests : (t + 1) * requests] for t in range(steps)]
        weight = [weight_ref[k : k + 1, piece] for k in range(taps)]
        outs = []
        for t in range(steps):
            added = bias_ref[:, piece] + weight[0] * window[t]
            for k in range(1, taps):
                added = added + weight[k] * window[t + k]
            outs.append(silu(added))
        conv_ref[:, piece] = jnp.concatenate(outs, axis=0).astype(jnp.bfloat16)
        results[i].start()
    copies[-1].wait()
    partial_ref[...] = lax.dot_general(
        proj_ref[...], conv_ref[...], (((1,), (1,)), ((), ())), preferred_element_type=jnp.float32
    )
    for result in results:
        result.wait()


def conv_project(x_in, conv_edge, conv_weight, conv_bias, proj):
    rows, channels = x_in.shape
    operands = (x_in, conv_edge, conv_weight, conv_bias, proj)
    pieces = channels // min(BLOCK, channels)
    return pl.pallas_call(
        conv_kernel,
        in_specs=[pl.BlockSpec(memory_space=pl.ANY)] * len(operands),
        out_specs=[pl.BlockSpec(memory_space=pl.ANY), pl.BlockSpec(memory_space=pltpu.VMEM)],
        out_shape=[
            pltpu.HBM((rows, channels), jnp.bfloat16),
            pltpu.HBM((proj.shape[0], rows), jnp.float32),
        ],
        scratch_shapes=[pltpu.VMEM(a.shape, a.dtype) for a in operands]
        + [
            pltpu.VMEM((rows, channels), jnp.bfloat16),
            pltpu.SemaphoreType.DMA((4 + pieces,)),
            pltpu.SemaphoreType.DMA((pieces,)),
        ],
        compiler_params=pltpu.CompilerParams(vmem_limit_bytes=VMEM_BYTES),
        name="conv_project",
    )(*(in_hbm(a) for a in operands))


def kept_edge_kernel(
    place_ref, accepted_ref, length_ref, owner_ref, x_ref, edge_ref, _, *group_refs
):
    lags, requests, block = edge_ref.shape
    steps = x_ref.shape[0] // requests
    place = place_ref[0]
    accepted = [accepted_ref[r] for r in range(requests)]
    lengths = [length_ref[r] + accepted[r] + 1 for r in range(requests)]
    deltas = [owner_ref[place * requests + r] ^ place for r in range(requests)]
    height = len(group_refs) * PLANE * EDGE_ROWS
    slot = lax.div(iota((height, 1), 0), EDGE_ROWS)
    lag = lax.rem(iota((height, 1), 0), EDGE_ROWS)

    def pick(request, position):
        return one_hot(
            (slot == by_request(request, deltas))
            & (position - by_request(request, accepted) == lag)
            & (lag < lags)
        )

    col = iota((1, requests * steps), 1)
    picked = dot(pick(lax.div(col, steps), lax.rem(col, steps) + lags), x_ref[...])
    col = iota((1, lags * requests), 1)
    edge = jnp.concatenate([edge_ref[k].astype(jnp.float32) for k in range(lags)], axis=0)
    picked += dot(pick(lax.rem(col, requests), lax.div(col, requests)), edge.astype(jnp.bfloat16))
    low = [length & ((1 << DIGIT) - 1) for length in lengths]
    high = [length >> DIGIT for length in lengths]
    numbers = by_request(iota((1, block), 1), accepted + low + high).astype(jnp.float32)
    picked = jnp.where(lag == lags, numbers, picked).astype(jnp.bfloat16)
    group = PLANE * EDGE_ROWS
    for d, ref in enumerate(group_refs):
        ref[...] = picked[d * group : (d + 1) * group]


def kept_edges(scalars, x_in, conv_edge, after, owners):
    channels = x_in.shape[1]
    groups = owners // PLANE
    vmem = pl.BlockSpec(memory_space=pltpu.VMEM)
    return pl.pallas_call(
        kept_edge_kernel,
        in_specs=[pl.BlockSpec(memory_space=pltpu.SMEM)] * len(scalars)
        + [vmem, vmem, pl.BlockSpec(memory_space=pl.ANY)],
        out_specs=[vmem] * groups,
        out_shape=[pltpu.HBM((PLANE * EDGE_ROWS, channels), jnp.bfloat16)] * groups,
        compiler_params=pltpu.CompilerParams(vmem_limit_bytes=VMEM_BYTES),
        name="kept_edges",
    )(*scalars, x_in, conv_edge, in_hbm(after))


def regroup_kernel(*refs):
    groups = len(refs) - 1 - PLANE
    rows = jnp.concatenate([ref[...].astype(jnp.float32) for ref in refs[:groups]], axis=0)
    for p, out_ref in enumerate(refs[-PLANE:]):
        parts = [
            rows[(d * PLANE + p) * EDGE_ROWS : (d * PLANE + p + 1) * EDGE_ROWS] for d in range(groups)
        ]
        out_ref[...] = jnp.concatenate(parts, axis=0).astype(jnp.bfloat16)


def regroup(arrived, after):
    rows, channels = arrived[0].shape
    block = min(1024, channels)
    height = len(arrived) * EDGE_ROWS
    return pl.pallas_call(
        regroup_kernel,
        grid=(channels // block,),
        in_specs=[pl.BlockSpec((rows, block), lambda j: (0, j))] * len(arrived)
        + [pl.BlockSpec(memory_space=pl.ANY)],
        out_specs=[pl.BlockSpec((height, block), lambda j: (0, j))] * PLANE,
        out_shape=[pltpu.HBM((height, channels), jnp.bfloat16)] * PLANE,
        compiler_params=pltpu.CompilerParams(
            dimension_semantics=("arbitrary",), vmem_limit_bytes=VMEM_BYTES
        ),
        name="regroup",
    )(*arrived, in_hbm(after))


def column(row):
    count = row.shape[1]
    same = iota((count, count), 0) == iota((count, count), 1)
    return jnp.sum(jnp.where(same, row, 0.0), axis=1, keepdims=True)


def normal(values, floor_value, eps_value):
    square = jnp.mean(values * values, axis=0, keepdims=True)
    return values * lax.rsqrt(jnp.maximum(square, floor_value) + eps_value)


def low_rank(total, gain):
    low = jnp.transpose(normal(total[: gain.shape[1]], 0.0, EPSILON))
    return (low * gain).astype(jnp.bfloat16)


def state_map(values, gain):
    return (normal(values, SQUARE_FLOOR, 0.0) * column(gain)).astype(jnp.bfloat16)


def summed(part_refs):
    total = part_refs[0][...]
    for part in part_refs[1:]:
        total = total + part[...]
    return total


def softplus(raw):
    return jnp.maximum(raw, 0.0) + jnp.log1p(jnp.exp(-jnp.abs(raw)))


def kept_kernel(parts, *refs):
    place_ref, accepted_ref, owner_ref = refs[:3]
    (
        dt_gain_ref, b_gain_ref, dt_weight_ref, dt_bias_ref, a_log_hbm, conv_hbm, state_hbm,
        slot_ref, part_ref, a_log_ref, conv_ref, state_ref, in_ref, size_ref, drive_ref, rate_ref, new_ref,
        in_sems, sems,
    ) = refs[3 + parts :]
    pairs = ((refs[3], part_ref), (a_log_hbm, a_log_ref), (conv_hbm, conv_ref), (state_hbm, state_ref))
    copies = [pltpu.make_async_copy(*pair, in_sems.at[i]) for i, pair in enumerate(pairs)]
    for copy in copies:
        copy.start()
    rank, states = dt_gain_ref.shape[1], b_gain_ref.shape[1]
    requests = accepted_ref.shape[0]
    rows, channels = conv_ref.shape
    steps = rows // requests
    span = min(2048, channels)
    halves = states // 8

    copies[1].wait()
    rate_ref[...] = jnp.exp(a_log_ref[...]) * (-LOG2_E)
    copies[0].wait()
    total = part_ref[...]
    for part in refs[4 : 3 + parts]:
        total = total + part[...]
    turned = state_map(total[rank : rank + states], b_gain_ref[...]).astype(jnp.float32)
    for row in range(rows):
        t, r = divmod(row, requests)
        in_ref[r * states : (r + 1) * states, t * LANES : (t + 1) * LANES] = jnp.broadcast_to(
            turned[:, row : row + 1], (states, LANES)
        )

    low = low_rank(total, dt_gain_ref[...])
    row = iota((rows, 1), 0)
    live = lax.div(row, requests) < by_request(
        lax.rem(row, requests), [accepted_ref[r] for r in range(requests)]
    )
    copies[2].wait()
    for first in range(0, channels, span):
        piece = slice(first, first + span)
        size = softplus(dot(low, dt_weight_ref[:, piece]) + dt_bias_ref[:, piece])
        size = jnp.where(live, size, 0.0)
        drive = size * conv_ref[:, piece].astype(jnp.float32)
        for c in range(span // LANES):
            tile = slice(c * LANES, (c + 1) * LANES)
            size_ref[first // LANES + c, :rows, :] = size[:, tile]
            drive_ref[first // LANES + c, :rows, :] = drive[:, tile]

    def one_request(r, carry):
        own = pl.multiple_of(r * states, states)
        rounds = lax.div(accepted_ref[r] + (ROUND - 1), ROUND)

        def one_span(part, inner):
            tiles = [pl.multiple_of(part * span + c, LANES) for c in range(0, span, LANES)]

            rates = [
                [rate_ref[8 * h : 8 * (h + 1), pl.ds(tile, LANES)] for tile in tiles]
                for h in range(halves)
            ]

            def one_round(i, hidden):
                hidden = [list(h) for h in hidden]
                for u in range(ROUND):
                    t = i * ROUND + u
                    at = pl.ds(t * requests + r, 8, stride=0)
                    lanes = pl.ds(pl.multiple_of(t * LANES, LANES), LANES)
                    b = [in_ref[pl.ds(own + 8 * h, 8), lanes] for h in range(halves)]
                    for c, tile in enumerate(tiles):
                        place = part * (span // LANES) + c
                        now, drive = size_ref[place, at, :], drive_ref[place, at, :]
                        for h in range(halves):
                            decay = jnp.exp2(now * rates[h][c])
                            hidden[h][c] = decay * hidden[h][c] + drive * b[h]
                return tuple(tuple(h) for h in hidden)

            lanes = pl.ds(pl.multiple_of(part * span, span), span)
            old = state_ref[pl.ds(own, states), lanes].astype(jnp.float32)
            start = tuple(
                tuple(
                    old[8 * h : 8 * (h + 1), c * LANES : (c + 1) * LANES] for c in range(len(tiles))
                )
                for h in range(halves)
            )
            done = lax.fori_loop(0, rounds, one_round, start)
            new = jnp.concatenate([jnp.concatenate(h, axis=1) for h in done], axis=0)
            new_ref[r, :, lanes] = new.astype(jnp.bfloat16)
            return inner

        lax.fori_loop(0, channels // span, one_span, 0)
        slot = owner_ref[place_ref[0] * requests + r]
        pltpu.make_async_copy(new_ref.at[r], slot_ref.at[slot], sems.at[r]).start()
        return carry

    copies[3].wait()
    lax.fori_loop(0, requests, one_request, 0)
    for r in range(requests):
        slot = owner_ref[place_ref[0] * requests + r]
        pltpu.make_async_copy(new_ref.at[r], slot_ref.at[slot], sems.at[r]).wait()


def kept_states(scalars, partials, gains, dt_weight, dt_bias, a_log, conv, state, slots):
    rows, channels = conv.shape
    states, rank = a_log.shape[0], dt_weight.shape[0]
    requests = scalars[1].shape[0]
    near = [*partials[1:], *gains, dt_weight, dt_bias]
    far = [in_hbm(a_log), in_hbm(conv), in_hbm(state)]
    anywhere = pl.BlockSpec(memory_space=pl.ANY)
    return pl.pallas_call(
        functools.partial(kept_kernel, len(partials)),
        in_specs=[pl.BlockSpec(memory_space=pltpu.SMEM)] * len(scalars)
        + [anywhere]
        + [pl.BlockSpec(memory_space=pltpu.VMEM)] * len(near)
        + [anywhere] * len(far),
        out_specs=anywhere,
        out_shape=pltpu.HBM((slots, states, channels), jnp.bfloat16),
        scratch_shapes=[
            pltpu.VMEM(partials[0].shape, jnp.float32),
            pltpu.VMEM(a_log.shape, jnp.float32),
            pltpu.VMEM(conv.shape, jnp.bfloat16),
            pltpu.VMEM(state.shape, jnp.bfloat16),
            pltpu.VMEM((requests * states, rows // requests * LANES), jnp.float32),
            pltpu.VMEM((channels // LANES, rows + 8, LANES), jnp.float32),
            pltpu.VMEM((channels // LANES, rows + 8, LANES), jnp.float32),
            pltpu.VMEM((states, channels), jnp.float32),
            pltpu.VMEM((requests, states, channels), jnp.bfloat16),
            pltpu.SemaphoreType.DMA((1 + len(far),)),
            pltpu.SemaphoreType.DMA((requests,)),
        ],
        compiler_params=pltpu.CompilerParams(vmem_limit_bytes=VMEM_BYTES),
        cost_estimate=pl.CostEstimate(
            flops=VECTOR_WEIGHT * 4 * rows * states * channels,
            transcendentals=rows * states * channels,
            bytes_accessed=2 * channels * (rows + rank + states * (requests + slots)),
        ),
        name="kept_states",
    )(*scalars, in_hbm(partials[0]), *near, *far)


def scan_kernel(parts, *refs):
    (
        dt_gain_ref, b_gain_ref, c_gain_ref, dt_weight_ref, dt_bias_ref, a_log_ref, skip_ref,
        conv_ref, state_ref, z_ref, mixed_ref,
        low_ref, in_ref, out_ref, size_ref, drive_ref, rate_ref, start_ref, sum_ref,
    ) = refs[parts:]
    rank, states = dt_gain_ref.shape[1], b_gain_ref.shape[1]
    rows, block = conv_ref.shape
    requests = state_ref.shape[0] // states
    steps = rows // requests

    @pl.when(pl.program_id(0) == 0)
    def _():
        total = summed(refs[:parts])
        low_ref[...] = low_rank(total, dt_gain_ref[...])
        in_map = state_map(total[rank : rank + states], b_gain_ref[...])
        out_map = state_map(total[rank + states :], c_gain_ref[...])
        wide = states * LANES
        spread = one_hot(lax.div(iota((states, wide), 1), LANES) == iota((states, wide), 0))
        turn = (((0,), (0,)), ((), ()))
        in_ref[...] = lax.dot_general(in_map, spread, turn, preferred_element_type=jnp.float32)
        out_ref[...] = lax.dot_general(out_map, spread, turn, preferred_element_type=jnp.float32)

    conv = conv_ref[...].astype(jnp.float32)
    size = softplus(dot(low_ref[...], dt_weight_ref[...]) + dt_bias_ref[...])
    size_ref[...] = size
    drive_ref[...] = size * conv
    start_ref[...] = dot(to_step_major(requests, states), state_ref[...])
    rate = jnp.exp(a_log_ref[...]) * (-LOG2_E)
    for n in range(states):
        rate_ref[n * requests : (n + 1) * requests, :] = jnp.broadcast_to(
            rate[n : n + 1, :], (requests, block)
        )

    pair = 2 if block % (2 * LANES) == 0 else 1

    def columns(c, carry):
        spans = [pl.ds(pl.multiple_of((c * pair + i) * LANES, LANES), LANES) for i in range(pair)]
        start = tuple(
            tuple(start_ref[n * requests : (n + 1) * requests, s] for s in spans)
            for n in range(states)
        )

        def step(t, hidden):
            at = pl.ds(pl.multiple_of(t * requests, requests), requests)
            sizes = [size_ref[at, s] for s in spans]
            drives = [drive_ref[at, s] for s in spans]
            sums = [None] * pair
            new = []
            for n in range(states):
                b = in_ref[at, n * LANES : (n + 1) * LANES]
                c_map = out_ref[at, n * LANES : (n + 1) * LANES]
                own = slice(n * requests, (n + 1) * requests)
                mine = []
                for i, s in enumerate(spans):
                    h = jnp.exp2(sizes[i] * rate_ref[own, s]) * hidden[n][i] + drives[i] * b
                    term = c_map * h
                    sums[i] = term if sums[i] is None else sums[i] + term
                    mine.append(h)
                new.append(tuple(mine))
            for i, s in enumerate(spans):
                sum_ref[at, s] = sums[i]
            return tuple(new)

        lax.fori_loop(0, steps, step, start, unroll=2)
        return carry

    lax.fori_loop(0, block // (pair * LANES), columns, 0)

    gate = silu(dot(to_step_major(requests, steps), z_ref[...]))
    mixed = ((sum_ref[...] + skip_ref[...] * conv) * gate).astype(jnp.bfloat16)
    mixed_ref[...] = dot(to_request_major(requests, steps), mixed).astype(jnp.bfloat16)


def scan(partials, gains, dt_weight, dt_bias, a_log, skip, conv, state, z_gate):
    rows, channels = conv.shape
    states, rank = a_log.shape[0], dt_weight.shape[0]
    block = min(512, channels)

    def whole(array):
        return pl.BlockSpec(array.shape, lambda j: (0, 0))

    wide = [in_hbm(dt_weight), dt_bias, in_hbm(a_log), skip, in_hbm(conv), in_hbm(state), in_hbm(z_gate)]
    tall = pltpu.VMEM((rows, block), jnp.float32)
    table = pltpu.VMEM((rows, states * LANES), jnp.float32)
    return pl.pallas_call(
        functools.partial(scan_kernel, len(partials)),
        grid=(channels // block,),
        in_specs=[whole(a) for a in (*partials, *gains)]
        + [pl.BlockSpec((a.shape[0], block), lambda j: (0, j)) for a in wide],
        out_specs=pl.BlockSpec((rows, block), lambda j: (0, j)),
        out_shape=jax.ShapeDtypeStruct((rows, channels), jnp.bfloat16),
        scratch_shapes=[
            pltpu.VMEM((rows, rank), jnp.bfloat16), table, table, tall, tall,
            pltpu.VMEM((state.shape[0], block), jnp.float32),
            pltpu.VMEM((state.shape[0], block), jnp.float32),
            tall,
        ],
        compiler_params=pltpu.CompilerParams(
            dimension_semantics=("arbitrary",), vmem_limit_bytes=VMEM_BYTES
        ),
        cost_estimate=pl.CostEstimate(
            flops=VECTOR_WEIGHT * 8 * rows * states * channels,
            transcendentals=rows * states * channels,
            bytes_accessed=2 * channels * (3 * rows + rank),
        ),
        name="scan",
    )(*partials, *gains, *wide)


def edge_kernel(steps, requests, place_ref, source_ref, range_ref, *refs):
    group_refs, edge_ref, stats_ref = refs[:-2], refs[-2], refs[-1]
    own_most, lags, block = edge_ref.shape
    groups = group_refs[0].shape[0] // EDGE_ROWS
    height = len(group_refs) * groups * EDGE_ROWS
    place = place_ref[0]

    def sender(index):
        p, d = lax.div(index, groups * EDGE_ROWS), lax.rem(lax.div(index, EDGE_ROWS), groups)
        return (d * PLANE + p) ^ place

    got = jnp.concatenate([ref[...] for ref in group_refs], axis=0)
    row, col = iota((own_most * 8, 1), 0), iota((1, height), 1)
    wanted = jnp.full((own_most * 8, 1), -1, jnp.int32)
    for i in range(own_most):
        wanted = jnp.where(lax.div(row, 8) == i, source_ref[i], wanted)
    pick = (sender(col) == wanted) & (lax.rem(col, EDGE_ROWS) == lax.rem(row, 8))
    picked = dot(one_hot(pick), got)
    for i in range(own_most):
        edge_ref[i] = picked[i * 8 : i * 8 + lags].astype(jnp.bfloat16)

    @pl.when(pl.program_id(0) == 0)
    def _():
        numbers = got[:, :LANES].astype(jnp.float32)
        row, lane = iota((height, LANES), 0), iota((height, LANES), 1)
        mine = lax.rem(row, EDGE_ROWS) == lags
        request = sender(row) * requests + lax.rem(lane, requests)
        digit = lax.div(lane, requests)
        counts = jnp.where(digit == 0, numbers, 0.0)
        lengths = jnp.where(digit == 1, numbers, 0.0) + jnp.where(
            digit == 2, numbers * float(1 << DIGIT), 0.0
        )
        tenants = range_ref.shape[0]
        sums, loads, members = [], [], []
        for k in range(tenants):
            start, end = range_ref[k, 0], range_ref[k, 1]
            inside = mine & (request >= start) & (request < end)
            sums.append(jnp.sum(jnp.where(inside, counts, 0.0), keepdims=True))
            loads.append(jnp.sum(jnp.where(inside, lengths, 0.0), keepdims=True))
            members.append((jnp.zeros((1, 1), jnp.int32) + (end - start)).astype(jnp.float32))
        mean = sum(loads[1:], loads[0]) / sum(members[1:], members[0])
        out = jnp.zeros((tenants, 2), jnp.float32)
        row, col = iota((tenants, 2), 0), iota((tenants, 2), 1)
        for k in range(tenants):
            rate = sums[k] / (float(steps) * members[k])
            load = loads[k] / members[k] / mean
            out = jnp.where(row == k, jnp.where(col == 0, rate, load), out)
        stats_ref[...] = out


def settle_edges(place, source, tenant_range, got, own_most, lags, steps, requests):
    smem = pl.BlockSpec(memory_space=pltpu.SMEM)
    height, channels = got[0].shape
    block = min(2048, channels)
    stats = (tenant_range.shape[0], 2)
    return pl.pallas_call(
        functools.partial(edge_kernel, steps, requests),
        grid=(channels // block,),
        in_specs=[smem] * 3 + [pl.BlockSpec((height, block), lambda j: (0, j))] * len(got),
        out_specs=[
            pl.BlockSpec((own_most, lags, block), lambda j: (0, 0, j)),
            pl.BlockSpec(stats, lambda j: (0, 0)),
        ],
        out_shape=[
            jax.ShapeDtypeStruct((own_most, lags, channels), jnp.bfloat16),
            jax.ShapeDtypeStruct(stats, jnp.float32),
        ],
        compiler_params=pltpu.CompilerParams(
            dimension_semantics=("arbitrary",), vmem_limit_bytes=VMEM_BYTES
        ),
        name="settle_edges",
    )(place, source, tenant_range, *got)


def settle_kernel(source_ref, bound_ref, got_hbm, owned_hbm, rows_ref, in_sems, sems):
    slots, own_most = got_hbm.shape[0], owned_hbm.shape[0]
    size = slots // PARTS
    parts = [slice(q * size, (q + 1) * size) for q in range(PARTS)]
    fetches = [
        pltpu.make_async_copy(got_hbm.at[part], rows_ref.at[part], in_sems.at[q])
        for q, part in enumerate(parts)
    ]
    for fetch in fetches:
        fetch.start()
    rows_ref[slots] = jnp.zeros(rows_ref.shape[1:], rows_ref.dtype)

    def put(i):
        return pltpu.make_async_copy(rows_ref.at[source_ref[i]], owned_hbm.at[i], sems.at[i])

    def start(i, carry):
        put(i).start()
        return carry

    lax.fori_loop(bound_ref[PARTS], own_most, start, 0)
    for q, fetch in enumerate(fetches):
        fetch.wait()
        lax.fori_loop(bound_ref[q], bound_ref[q + 1], start, 0)
    for i in range(own_most):
        put(i).wait()


def settle_states(source, bounds, got, own_most):
    smem = pl.BlockSpec(memory_space=pltpu.SMEM)
    anywhere = pl.BlockSpec(memory_space=pl.ANY)
    slots, *rest = got.shape
    return pl.pallas_call(
        settle_kernel,
        in_specs=[smem, smem, anywhere],
        out_specs=anywhere,
        out_shape=pltpu.HBM((own_most, *rest), got.dtype),
        scratch_shapes=[
            pltpu.VMEM((slots + 1, *rest), got.dtype),
            pltpu.SemaphoreType.DMA((PARTS,)),
            pltpu.SemaphoreType.DMA((own_most,)),
        ],
        compiler_params=pltpu.CompilerParams(vmem_limit_bytes=VMEM_BYTES),
        name="settle_states",
    )(source, bounds, in_hbm(got))


def per_device(
    x_in, z_gate, conv_edge, conv_weight, conv_bias, x_proj_weight, dt_gain, b_gain, c_gain,
    dt_proj_weight, dt_bias, a_log, skip, ssm_state, accepted, prompt_len, tenant_range, owner,
):
    requests, states, channels = ssm_state.shape
    lags = conv_edge.shape[1]
    owners = lax.axis_size("req")
    own_most = min(requests + requests // 2, owners)
    place = lax.axis_index("req").astype(jnp.int32).reshape(1)

    by_lag = jnp.transpose(conv_edge, (1, 0, 2))
    conv, partial = conv_project(
        x_in, by_lag, conv_weight, conv_bias.reshape(1, -1), x_proj_weight.T
    )
    if lax.axis_size("tp") == 2:
        partials = (partial, lax.ppermute(partial, "tp", [(0, 1), (1, 0)]))
    else:
        partials = (lax.psum(partial, "tp"),)

    def swap(rows, delta):
        return lax.ppermute(rows, "req", [(i, i ^ delta) for i in range(owners)]) if delta else rows

    groups = kept_edges((place, accepted, prompt_len, owner), x_in, by_lag, partial, owners)
    half = len(groups) // 2
    far = [swap(rows, d * PLANE) for d, rows in enumerate(groups) if d >= half]

    gains = (dt_gain.reshape(1, -1), b_gain.reshape(1, -1), c_gain.reshape(1, -1))
    bias = dt_bias.reshape(1, -1)
    state = ssm_state.reshape(requests * states, channels)
    slots = kept_states(
        (place, accepted, owner), partials, gains[:2], dt_proj_weight, bias, a_log, conv, state, owners
    )
    slots, *near = lax.optimization_barrier((slots, *groups[:half]))
    got = lax.all_to_all(slots, "req", split_axis=0, concat_axis=0, tiled=True)
    groups = [swap(rows, d * PLANE) for d, rows in enumerate(near)] + far
    mixed = scan(
        partials, gains, dt_proj_weight, bias, a_log, skip.reshape(1, -1), conv, state, z_gate
    )
    mixed, owner = lax.optimization_barrier((mixed, owner))
    hits = jnp.any(owner.reshape(owners, requests) == place, axis=1)
    ids = np.arange(owners, dtype=np.int32)
    ranks = jnp.sum((hits[None, :] & (ids[None, :] < ids[:, None])).astype(jnp.int32), axis=1)
    starts = np.arange(PARTS + 1, dtype=np.int32) * (owners // PARTS)
    bounds = jnp.sum((hits[None, :] & (ids[None, :] < starts[:, None])).astype(jnp.int32), axis=1)
    at = hits[None, :] & (ranks[None, :] == jnp.arange(own_most, dtype=jnp.int32)[:, None])
    source = owners - jnp.sum(jnp.where(at, owners - ids[None, :], 0), axis=1)
    groups = [swap(rows, p) for p, rows in enumerate(regroup(groups, mixed))]
    owned_edge, tenant_stats = settle_edges(
        place, source, tenant_range, groups, own_most, lags, x_in.shape[0] // requests,
        requests,
    )
    owned = settle_states(source, bounds, got, own_most)
    return (mixed, owned, owned_edge, tenant_stats)


def solution(mesh):
    placed = (
        P("req", "tp"),
        P("req", "tp"),
        P("req", None, "tp"),
        P(None, "tp"),
        P("tp"),
        P("tp", None),
        P(),
        P(),
        P(),
        P(None, "tp"),
        P("tp"),
        P(None, "tp"),
        P("tp"),
        P("req", None, "tp"),
        P("req"),
        P("req"),
        P(),
        P(),
    )
    return jax.shard_map(
        per_device,
        mesh=mesh,
        in_specs=placed,
        out_specs=(P("req", "tp"), P("req", None, "tp"), P("req", None, "tp"), P()),
        check_vma=False,
    )
```
